32 devices in a mesh: batch: 8 (over z, y), seq: 4 (over x, core).
Axes of the slice: x: 2, y: 2, z: 4, core: 2. Of those that a mesh axis runs over, the one named last changes fastest.
Arguments:
- inputs: bfloat16 [16, 1024, 768], P('batch', 'seq'), may hold values from -6 to 6
- segments: int32 [16, 1024], P('batch'), may hold values from 0 to 7, never falling along the last dimension, each value on 1 to 512 neighbouring positions
- qkv_weight: bfloat16 [768, 2304], replicated, may hold values from -0.21875 to 0.21875
- query_bias: bfloat16 [768], replicated, may hold values from -3 to 3
- value_bias: bfloat16 [768], replicated, may hold values from -3 to 3
- out_weight: bfloat16 [768, 768], replicated, may hold values from -1.75 to 1.75
- out_bias: bfloat16 [768], replicated, may hold values from -3 to 3
- norm1_gain: bfloat16 [768], replicated, may hold values from 0.099609375 to 1.8984375
- norm1_shift: bfloat16 [768], replicated, may hold values from -3 to 3
- up_weight: bfloat16 [768, 3072], replicated, may hold values from -0.21875 to 0.21875
- up_bias: bfloat16 [3072], replicated, may hold values from -3 to 3
- down_weight: bfloat16 [3072, 768], replicated, may hold values from -0.109375 to 0.109375
- down_bias: bfloat16 [768], replicated, may hold values from -3 to 3
- norm2_gain: bfloat16 [768], replicated, may hold values from 0.099609375 to 1.8984375
- norm2_shift: bfloat16 [768], replicated, may hold values from -3 to 3
- cotangent: bfloat16 [16, 1024, 768], P('batch', 'seq'), may hold values from -6 to 6
Outputs:
- outputs: bfloat16 [16, 1024, 768], P('batch', 'seq')
- input_grad: float32 [16, 1024, 768], P('batch', 'seq')
- qkv_weight_grad: float32 [768, 2304], P('batch', 'seq')
- query_bias_grad: float32 [768], replicated
- value_bias_grad: float32 [768], replicated
- out_weight_grad: float32 [768, 768], P('batch', 'seq')
- out_bias_grad: float32 [768], replicated
- norm1_gain_grad: float32 [768], replicated
- norm1_shift_grad: float32 [768], replicated
- up_weight_grad: float32 [768, 3072], P('batch', 'seq')
- up_bias_grad: float32 [3072], replicated
- down_weight_grad: float32 [3072, 768], P('batch', 'seq')
- down_bias_grad: float32 [768], replicated
- norm2_gain_grad: float32 [768], replicated
- norm2_shift_grad: float32 [768], replicated
The draws below stay inside these ranges and needn't reach their ends.
Inputs may be any that keep to these rules, and one draw needn't show every extreme that they name: `segments`: in each packed row the passage numbers never fall, every number below 8 occurs, each passage holds 1 to 512 positions, and one passage in each row holds exactly 512.
All inputs are finite; a program needn't handle non-finite values.
Results may differ from the reference program's by a relative error of at most 0.013.
The reference program's roundings to bfloat16 on the way count: a program that leaves them out, or rounds other values in their place, can miss the bound.
Values may be sent and summed in bfloat16 or wider, within the bound.
No kernel may reach another device: no remote copies, remote signals or barrier semaphores. Data moves between devices by JAX's collectives and lax.ppermute only.
A program may use at most 192 MiB of HBM per device.

```python
import math
import jax
import jax.numpy as jnp
import numpy as np
from jax import lax

D = 768
H = 12
DH = 64
FF = 3072
ROW_LEN = 1024
PASSAGES = 8
MOST_LEN = 512
ROWS = 2
ROWS_ALL = 16


def strengthened(values, rng, source, target, shards_of, factor):
    owner, partner = [(jnp.arange(values.shape[axis_at]) // (values.shape[axis_at] // shards_of)).reshape([-1 if axis == axis_at else 1 for axis in range(values.ndim)]) for axis_at in (source, target)]
    chosen = jax.random.permutation(rng, shards_of)[partner]
    strong = (owner == chosen) | (owner == (partner + shards_of // 2) % shards_of)
    return jnp.where(strong, factor * values, values)


def level_of(stream_key, shape, cuts, smallest, largest):
    level, own = 1.0, jax.random.fold_in(stream_key, 6)
    for dim, shards_of in cuts:
        heights = jnp.exp(jax.random.uniform(jax.random.fold_in(own, dim), (shards_of,), jnp.float32, smallest / len(cuts), largest / len(cuts)))
        level = level * jnp.repeat(heights, shape[dim] // shards_of).reshape([-1 if axis == dim else 1 for axis in range(len(shape))])
    return level


def profile(count, total, reach, slope):
    loads = [(1 << 20) // math.isqrt(standing ** slope) + 1 for standing in range(2, count + 1)]
    rest, given = total - reach - (count - 1), [1] * (count - 1)
    while rest > 0:
        movable = [i for i in range(count - 1) if given[i] < reach]
        pool, left = sum([loads[i] for i in movable]), rest
        for i in movable:
            extra = min(reach - given[i], max(1, left * loads[i] // pool), rest)
            given[i] = given[i] + extra
            rest = rest - extra
    return np.array([reach] + given)


def uneven(own_key, amount, total, most, skew):
    if amount == 2:
        one = jax.random.randint(own_key, (), max(1, total - most), min(most, total - 1) + 1)
        return jnp.stack([one, total - one])
    tallies = jnp.asarray(profile(amount, total, most, skew), jnp.int32)
    twos = (amount - 1) // 2
    giver, sink = tallies[1:1 + 2 * twos:2], tallies[2:2 + 2 * twos:2]
    room = jnp.minimum(giver - 1, most - sink)
    shifted = jax.random.randint(jax.random.fold_in(own_key, 1), (twos,), 0, 1 << 20) % (room + 1)
    tallies = tallies.at[1:1 + 2 * twos:2].set(giver - shifted).at[2:2 + 2 * twos:2].set(sink + shifted)
    return tallies[jax.random.permutation(jax.random.fold_in(own_key, 2), amount)]


def bell_draw(stream_key, extent, scale, most, cuts=(), dtype=jnp.bfloat16):
    values = scale * jax.random.normal(stream_key, extent, jnp.float32)
    if cuts:
        values = values * level_of(stream_key, extent, cuts, -0.22, 0.18)
    return jnp.clip(values, -most, most).astype(dtype)


def bell_draw_with(rng, extent, deviation, most, cuts, heavy, held_as=jnp.bfloat16):
    values = deviation * jax.random.normal(rng, extent, jnp.float32)
    if cuts:
        values = values * level_of(rng, extent, cuts, -0.22, 0.18)
    return jnp.clip(strengthened(values, jax.random.fold_in(rng, 3), *heavy), -most, most).astype(held_as)


def setup_inputs(seed: int = 0) -> dict:
    key_list = jax.random.split(jax.random.key(seed), 17)
    inputs = bell_draw_with(key_list[0], (ROWS_ALL, ROW_LEN, D), 1.0, 6.0, ((0, 8), (1, 4)), (0, 2, 8, 2.0))
    segments = jax.vmap(lambda own: jnp.searchsorted(jnp.cumsum(uneven(own, PASSAGES, ROW_LEN, MOST_LEN, 2)), jnp.arange(ROW_LEN), side="right"))(jax.random.split(key_list[1], ROWS_ALL)).reshape((ROWS_ALL, ROW_LEN)).astype(jnp.int32)
    qkv_weight = bell_draw(key_list[2], (D, 3 * D), D ** -0.5, 0.21875)
    query_bias = bell_draw(key_list[3], (D,), 0.5, 3.0)
    value_bias = bell_draw(key_list[4], (D,), 0.5, 3.0)
    out_weight = bell_draw(key_list[5], (D, D), (D * 16 // ROW_LEN) ** -0.5, 1.75)
    out_bias = bell_draw(key_list[6], (D,), 0.5, 3.0)
    norm1_gain = jnp.clip(1.0 + 0.18 * jax.random.normal(key_list[7], (D,), jnp.float32), 0.099609375, 1.8984375).astype(jnp.bfloat16)
    norm1_shift = bell_draw(key_list[8], (D,), 0.5, 3.0)
    up_weight = bell_draw(key_list[9], (D, FF), D ** -0.5, 0.21875)
    up_bias = bell_draw(key_list[10], (FF,), 0.5, 3.0)
    down_weight = bell_draw(key_list[11], (FF, D), FF ** -0.5, 0.109375)
    down_bias = bell_draw(key_list[12], (D,), 0.5, 3.0)
    norm2_gain = jnp.clip(1.0 + 0.18 * jax.random.normal(key_list[13], (D,), jnp.float32), 0.099609375, 1.8984375).astype(jnp.bfloat16)
    norm2_shift = bell_draw(key_list[14], (D,), 0.5, 3.0)
    cotangent = bell_draw_with(key_list[15], (ROWS_ALL, ROW_LEN, D), 1.0, 6.0, ((0, 8), (1, 4)), (0, 2, 8, 2.0))
    return {"inputs": inputs, "segments": segments, "qkv_weight": qkv_weight, "query_bias": query_bias, "value_bias": value_bias, "out_weight": out_weight, "out_bias": out_bias, "norm1_gain": norm1_gain, "norm1_shift": norm1_shift, "up_weight": up_weight, "up_bias": up_bias, "down_weight": down_weight, "down_bias": down_bias, "norm2_gain": norm2_gain, "norm2_shift": norm2_shift, "cotangent": cotangent}


@jax.custom_vjp
def low(v):
    return lax.optimization_barrier(v.astype(jnp.bfloat16)).astype(jnp.float32)

@jax.custom_vjp
def low_back(v):
    return v

def low_keep(v):
    return (low(v), None)

def low_pass(kept, grad):
    return (grad,)

def back_keep(v):
    return (v, None)

def back_low(kept, grad):
    return (low(grad),)
low.defvjp(low_keep, low_pass)
low_back.defvjp(back_keep, back_low)
EPS = 1e-05
NEG = -1000000000.0
HIGH = lax.Precision.HIGHEST

def layer_norm(values, gain, shift):
    mean = lax.optimization_barrier(jnp.mean(values, axis=-1, keepdims=True))
    centred = values - mean
    spread = lax.optimization_barrier(jnp.mean(centred * centred, axis=-1, keepdims=True))
    return centred * lax.rsqrt(spread + EPS) * gain + shift

def attend(parts):
    query, keys, values, segment = parts
    scores = jnp.einsum('qhd,khd->hqk', query, keys, precision=HIGH) * DH ** (-0.5)
    scores = low_back(scores)
    same = segment[:, None] == segment[None, :]
    probs = jax.nn.softmax(jnp.where(same[None], scores, NEG), axis=-1)
    context = jnp.einsum('hqk,khd->qhd', low(probs), values, precision=HIGH)
    return context.reshape(context.shape[0], H * DH)

def forward(inputs, segment, params):
    qkv_w, q_b, v_b, out_w, out_b, g_one, s_one, up_w, up_b, down_w, down_b, g_two, s_two = params
    rows = inputs.shape[0]
    flat = inputs.reshape(rows * ROW_LEN, D)
    shift = jnp.concatenate([q_b, jnp.zeros((D,), jnp.float32), v_b])
    projected = low_back(low(jnp.dot(flat, qkv_w, precision=HIGH) + shift))
    split = projected.reshape(rows, ROW_LEN, 3, H, DH)
    context = lax.map(jax.checkpoint(attend), (split[:, :, 0], split[:, :, 1], split[:, :, 2], segment))
    context = low_back(low(context.reshape(rows * ROW_LEN, D)))
    summed = flat + low_back(jnp.dot(context, out_w, precision=HIGH)) + out_b
    hidden = layer_norm(summed, g_one, s_one)
    pre = low_back(jnp.dot(low(hidden), up_w, precision=HIGH) + up_b)
    act = low(jax.nn.gelu(pre, approximate=False))
    branch = low_back(jnp.dot(act, down_w, precision=HIGH)) + down_b
    return layer_norm(hidden + branch, g_two, s_two).reshape(rows, ROW_LEN, D)

def reference(inputs, segments, qkv_weight, query_bias, value_bias, out_weight, out_bias, norm1_gain, norm1_shift, up_weight, up_bias, down_weight, down_bias, norm2_gain, norm2_shift, cotangent):
    params = (qkv_weight, query_bias, value_bias, out_weight, out_bias, norm1_gain, norm1_shift, up_weight, up_bias, down_weight, down_bias, norm2_gain, norm2_shift)
    params = tuple((p.astype(jnp.float32) for p in params))
    groups = inputs.shape[0] // ROWS
    blocks_in = inputs.astype(jnp.float32).reshape(groups, ROWS, ROW_LEN, D)
    blocks_seg = segments.reshape(groups, ROWS, ROW_LEN)
    blocks_cot = cotangent.astype(jnp.float32).reshape(groups, ROWS, ROW_LEN, D)

    def step(total, block):
        block_in, block_seg, block_cot = block
        result, back = jax.vjp(lambda xv, pv: forward(xv, block_seg, pv), block_in, params)
        grad_in, grad_params = back(block_cot)
        total = jax.tree.map(lambda a, b: a + b, total, grad_params)
        return (total, (result.astype(jnp.bfloat16), grad_in))
    start = jax.tree.map(jnp.zeros_like, params)
    total, (results, grads_in) = lax.scan(step, start, (blocks_in, blocks_seg, blocks_cot))
    outputs = results.reshape(groups * ROWS, ROW_LEN, D)
    input_grad = grads_in.reshape(groups * ROWS, ROW_LEN, D)
    return (outputs, input_grad, total[0], total[1], total[2], total[3], total[4], total[5], total[6], total[7], total[8], total[9], total[10], total[11], total[12])
```

```python
import jax
import jax.numpy as jnp
from jax import lax
from jax.sharding import PartitionSpec as P

DH = 64
EPS = 1e-05
NEG = -1000000000.0
F32 = jnp.float32
LOW = jnp.bfloat16


def layer_norm(values, gain, shift):
    mean = jnp.mean(values, axis=-1, keepdims=True)
    centred = values - mean
    spread = jnp.mean(centred * centred, axis=-1, keepdims=True)
    return centred * lax.rsqrt(spread + EPS) * gain + shift


def gelu_exact(values):
    return jax.nn.gelu(values, approximate=False)


def row_scores(query, keys, segment):
    scores = jnp.einsum("qhd,khd->hqk", query, keys, preferred_element_type=F32) * DH ** (-0.5)
    same = segment[:, None] == segment[None, :]
    return jnp.where(same[None], scores, NEG)


def attend_row(query, keys, values, segment):
    scores = row_scores(query, keys, segment)
    top = jnp.max(scores, axis=-1, keepdims=True)
    expo = jnp.exp(scores - top)
    total = jnp.sum(expo, axis=-1, keepdims=True)
    probs = (expo / total).astype(LOW)
    context = jnp.einsum("hqk,khd->qhd", probs, values, preferred_element_type=F32)
    return context.astype(LOW), (top + jnp.log(total))[..., 0]


def attend_back(query, keys, values, segment, logsum, d_context):
    scores = row_scores(query, keys, segment)
    probs = jnp.exp(scores - logsum[..., None])
    d_values = jnp.einsum("hqk,qhd->khd", probs.astype(LOW), d_context, preferred_element_type=F32)
    d_probs = jnp.einsum("qhd,khd->hqk", d_context, values, preferred_element_type=F32)
    delta = jnp.sum(probs * d_probs, axis=-1, keepdims=True)
    d_scores = (probs * (d_probs - delta)).astype(LOW)
    d_query = jnp.einsum("hqk,khd->qhd", d_scores, keys, preferred_element_type=F32) * DH**-0.5
    d_keys = jnp.einsum("hqk,qhd->khd", d_scores, query, preferred_element_type=F32) * DH**-0.5
    return d_query.astype(LOW), d_keys.astype(LOW), d_values.astype(LOW)


def body(
    inputs,
    segments,
    qkv_weight,
    query_bias,
    value_bias,
    out_weight,
    out_bias,
    norm1_gain,
    norm1_shift,
    up_weight,
    up_bias,
    down_weight,
    down_bias,
    norm2_gain,
    norm2_shift,
    cotangent,
):
    rows, quarter, width = inputs.shape
    count = rows * quarter
    half = width // 2
    seq_size = lax.axis_size("seq")
    batch_size = lax.axis_size("batch")
    fine = batch_size // 8
    place = lax.axis_index("seq")
    chip, core = place // 2, place % 2
    block = lax.axis_index("batch") // fine

    def over_seq(array, flip):
        return lax.ppermute(array, "seq", [(i, i ^ flip) for i in range(seq_size)])

    def over_batch(array, flip):
        return lax.ppermute(array, "batch", [(i, i ^ flip) for i in range(batch_size)])

    def swap(array, axis):
        if axis == "x":
            return over_seq(array, 2)
        return over_batch(array, fine << "yzw".index(axis))

    def pick(array, index, axis=0):
        return lax.dynamic_index_in_dim(array, index, axis, keepdims=False)

    own = pick(inputs, chip)
    far = over_seq(pick(inputs, 1 - chip), 2)
    near = over_seq(own, 1)
    across = over_seq(far, 1)
    row_in = jnp.concatenate([own, near, far, across], axis=0)
    row_segment = pick(segments, chip).reshape(4, quarter)
    segment = jnp.concatenate([pick(row_segment, place ^ j) for j in range(4)])

    weight_half = pick(qkv_weight.reshape(width, 3, 2, half), core, 2)
    shift_half = jnp.stack(
        [
            pick(query_bias.reshape(2, half), core),
            jnp.zeros((half,), LOW),
            pick(value_bias.reshape(2, half), core),
        ]
    ).astype(F32)
    projected = (
        jnp.einsum("ti,ico->tco", row_in, weight_half, preferred_element_type=F32) + shift_half
    ).astype(LOW)
    heads = half // DH
    split = projected.reshape(4 * quarter, 3, heads, DH)
    query, keys, values = split[:, 0], split[:, 1], split[:, 2]
    context, logsum = attend_row(query, keys, values, segment)
    parts = context.reshape(4, quarter, half)
    parts = [parts[0]] + [over_seq(parts[j], j) for j in (1, 2, 3)]

    def sides(mine, other):
        low = jnp.where(core == 0, mine, other)
        high = jnp.where(core == 0, other, mine)
        return jnp.concatenate([low, high], axis=1)

    flat_ctx = jnp.concatenate([sides(parts[0], parts[1]), sides(parts[2], parts[3])], axis=0)
    flat_in = jnp.concatenate([own, pick(inputs, 1 - chip)], axis=0)
    flat_cot = jnp.concatenate([pick(cotangent, chip), pick(cotangent, 1 - chip)], axis=0)
    ctx_pair = over_seq(flat_ctx, 1)

    attn = jnp.dot(flat_ctx, out_weight, preferred_element_type=F32) + out_bias.astype(F32)
    summed = flat_in.astype(F32) + attn
    hidden, norm1_back = jax.vjp(
        layer_norm, summed, norm1_gain.astype(F32), norm1_shift.astype(F32)
    )
    hidden_low = hidden.astype(LOW)
    hidden_pair = over_seq(hidden_low, 1)
    pre_act = jnp.dot(hidden_low, up_weight, preferred_element_type=F32) + up_bias.astype(F32)
    act, gelu_back = jax.vjp(gelu_exact, pre_act)
    act_low = act.astype(LOW)
    act_pair = over_seq(act_low, 1)
    branch = jnp.dot(act_low, down_weight, preferred_element_type=F32) + down_bias.astype(F32)
    final, norm2_back = jax.vjp(
        layer_norm, hidden + branch, norm2_gain.astype(F32), norm2_shift.astype(F32)
    )
    d_res_two, d_gain_two, d_shift_two = norm2_back(flat_cot.astype(F32))
    d_down_bias = jnp.sum(d_res_two, axis=0)
    d_branch = d_res_two.astype(LOW)

    def columns(array, flip):
        split = array.reshape(count, 4, array.shape[1] // 4)
        return jnp.concatenate(
            [pick(split, place ^ flip, 1), pick(split, place ^ flip ^ 2, 1)], axis=1
        )

    def weight_grad(left, left_pair, right):
        mine, theirs = columns(right, 0), over_seq(columns(right, 1), 1)
        grad = jnp.einsum("ti,to->io", left, mine, preferred_element_type=F32) + jnp.einsum(
            "ti,to->io", left_pair, theirs, preferred_element_type=F32
        )
        depth, wide = grad.shape
        return grad.reshape(8, depth // 8, 2, wide // 2)

    def relative(grad, order):
        split = jnp.stack([pick(grad, block ^ j) for j in range(8)])
        split = split.reshape((2, 2, 2) + grad.shape[1:])
        dims = {"w": 0, "z": 1, "y": 2, "x": 4}
        return split.transpose([dims[axis] for axis in order] + [3, 5])

    def settle(grad, order):
        for axis in order:
            grad = grad[0] + swap(grad[1].astype(LOW), axis).astype(F32)
        if fine > 1:
            groups = [[i * fine + j for j in range(fine)] for i in range(8)]
            grad = lax.psum_scatter(
                grad, "batch", scatter_dimension=0, axis_index_groups=groups, tiled=True
            )
        return grad

    down_total = settle(relative(weight_grad(act_low, act_pair, d_branch), "yzxw"), "yzxw")
    d_act = jnp.einsum("to,io->ti", d_branch, down_weight, preferred_element_type=F32)
    (d_pre,) = gelu_back(d_act)
    d_pre_low = d_pre.astype(LOW)
    d_up_bias = jnp.sum(d_pre_low.astype(F32), axis=0)
    up_total = settle(relative(weight_grad(hidden_low, hidden_pair, d_pre_low), "zyxw"), "zyxw")
    d_hidden = d_res_two + jnp.einsum(
        "to,io->ti", d_pre_low, up_weight, preferred_element_type=F32
    )
    d_summed, d_gain_one, d_shift_one = norm1_back(d_hidden)
    d_out_bias = jnp.sum(d_summed, axis=0)
    d_attn = d_summed.astype(LOW)
    d_context = jnp.einsum("to,io->ti", d_attn, out_weight, preferred_element_type=F32).astype(LOW)
    d_split = d_context.reshape(2, quarter, 2, half)
    d_sides = [[pick(d_split[i], core, 1), pick(d_split[i], 1 - core, 1)] for i in range(2)]
    d_heads = jnp.concatenate(
        [
            d_sides[0][0],
            over_seq(d_sides[0][1], 1),
            over_seq(d_sides[1][0], 2),
            over_seq(d_sides[1][1], 3),
        ],
        axis=0,
    ).reshape(4 * quarter, heads, DH)
    out_total = settle(relative(weight_grad(flat_ctx, ctx_pair, d_attn), "yzxw"), "yzxw")

    def spread(vector):
        for flip in (1, 2):
            vector = vector + over_seq(vector, flip)
        flip = 1
        while flip < batch_size:
            vector = vector + over_batch(vector, flip)
            flip *= 2
        return vector

    early = spread(
        jnp.concatenate(
            [d_out_bias, d_gain_one, d_shift_one, d_down_bias, d_gain_two, d_shift_two, d_up_bias]
        )
    )

    d_parts = attend_back(query, keys, values, segment, logsum, d_heads)
    d_proj = jnp.stack([part.reshape(4 * quarter, half) for part in d_parts], axis=1)
    bias_part = jnp.sum(d_proj[:, ::2].astype(F32), axis=0)
    late = spread(
        jnp.concatenate(
            [
                jnp.where(core == 0, bias_part, 0.0)[:, None],
                jnp.where(core == 1, bias_part, 0.0)[:, None],
            ],
            axis=1,
        ).reshape(2 * width)
    )

    d_qkv = jnp.einsum("ti,tco->ico", row_in, d_proj, preferred_element_type=F32)
    unit = half // 2
    d_qkv = d_qkv.reshape(8, width // 8, 6, unit)
    d_qkv = jnp.stack([pick(d_qkv, block ^ j) for j in range(8)])
    d_qkv = d_qkv.reshape(2, 2, 2, width // 8, 6 * unit).transpose(2, 1, 0, 3, 4)
    for axis in "yz":
        d_qkv = d_qkv[0] + swap(d_qkv[1].astype(LOW), axis).astype(F32)
    d_unit = d_qkv.reshape(2, width // 8, 6, unit)

    def units(*which):
        return d_unit[:, :, jnp.array(which)]

    sent = over_seq(jnp.where(core == 0, units(2, 3, 5), units(0, 2, 3)), 1)
    kept = jnp.where(core == 0, units(0, 1, 4), units(1, 4, 5))
    first = jnp.where(
        core == 0,
        jnp.stack([kept[:, :, 0], kept[:, :, 1], sent[:, :, 0]], axis=2),
        jnp.stack([kept[:, :, 0], sent[:, :, 0], sent[:, :, 1]], axis=2),
    )
    second = jnp.where(
        core == 0,
        jnp.stack([sent[:, :, 1], sent[:, :, 2], kept[:, :, 2]], axis=2),
        jnp.stack([sent[:, :, 2], kept[:, :, 1], kept[:, :, 2]], axis=2),
    )
    d_unit = jnp.stack(
        [jnp.where(chip == 0, first, second), jnp.where(chip == 0, second, first)]
    ).reshape(2, 2, width // 8, 3 * unit)
    d_unit = d_unit[:, :, :, :]
    d_pick = jnp.stack([d_unit[0], d_unit[1]])
    qkv_total = settle(d_pick, "xw")

    d_row = jnp.einsum("tco,ico->ti", d_proj, weight_half, preferred_element_type=F32)
    d_row = d_row.reshape(4, quarter, width)
    d_row = jnp.stack([d_row[0], d_row[2]]) + over_seq(jnp.stack([d_row[1], d_row[3]]), 1)
    d_near = d_summed[:quarter] + d_row[0]
    d_far = d_summed[quarter:] + over_seq(d_row[1].astype(LOW), 2).astype(F32)
    d_inputs = jnp.stack([jnp.where(chip == 0, d_near, d_far), jnp.where(chip == 0, d_far, d_near)])
    final = final.astype(LOW).reshape(rows, quarter, width)
    outputs = jnp.where(chip == 0, final, final[::-1])
    at = [0]

    def take(size):
        at[0] += size
        return early[at[0] - size : at[0]]

    d_out_bias, d_gain_one, d_shift_one, d_down_bias, d_gain_two, d_shift_two = [
        take(width) for _ in range(6)
    ]
    d_up_bias = early[at[0] :]
    return (
        outputs,
        d_inputs,
        qkv_total,
        late[:width],
        late[width:],
        out_total,
        d_out_bias,
        d_gain_one,
        d_shift_one,
        up_total,
        d_up_bias,
        down_total,
        d_down_bias,
        d_gain_two,
        d_shift_two,
    )


def solution(mesh):
    whole, split = P(), P("batch", "seq")
    tokens = P("batch", "seq", None)
    return jax.shard_map(
        body,
        mesh=mesh,
        in_specs=(tokens, P("batch", None)) + (whole,) * 13 + (tokens,),
        out_specs=(tokens, tokens, split, whole, whole, split)
        + (whole,) * 3
        + (split, whole, split)
        + (whole,) * 3,
        check_vma=False,
    )
```

```python
import functools

import jax
import jax.numpy as jnp
from jax import lax
from jax.experimental import pallas as pl
from jax.experimental.pallas import tpu as pltpu
from jax.sharding import PartitionSpec as P

DH = 64
EPS = 1e-05
NEG = -1000000000.0
F32 = jnp.float32
LOW = jnp.bfloat16
PAIR = 2 * DH
SCALE = DH**-0.5
BLOCK = 256
ROOT_HALF = 0.5**0.5
ROOT_TWO_PI = 0.3989422804014327


def shaped(shape, dtype):
    return jax.ShapeDtypeStruct(shape, dtype)


def dot_nn(left, right):
    return jnp.dot(left, right, preferred_element_type=F32)


def dot_nt(left, right):
    return lax.dot_general(left, right, (((1,), (1,)), ((), ())), preferred_element_type=F32)


def params(mib):
    return pltpu.CompilerParams(vmem_limit_bytes=mib << 20, dimension_semantics=("arbitrary",))


def full(shape):
    return pl.BlockSpec(shape, lambda *_: (0,) * len(shape))


def one_head(array, head):
    lane = lax.broadcasted_iota(jnp.int32, array.shape, 1)
    return jnp.where((lane < DH) if head == 0 else (lane >= DH), array, jnp.zeros_like(array))


def mask_columns(seg_col, seg_row):
    return jnp.where(seg_col == seg_row, 0.0, NEG)


def forward_kernel(
    info, x0, x1, x2, x3, wq, wk, wv, bq, bv, seg_col, seg_row,
    q_out, k_out, v_out, c0, c1, c2, c3, lse_out,
    xs, bias, qs, vt, ctx,
):
    place = info[0]
    tokens = xs.shape[0]
    quarter = tokens // 4
    blocks = tokens // BLOCK

    @pl.when(pl.program_id(0) == 0)
    def _():
        for j, ref in enumerate((x0, x1, x2, x3)):
            xs[pl.ds(pl.multiple_of((place ^ j) * quarter, quarter), quarter), :] = ref[...]
        for b in range(blocks):
            row = seg_row[:, b * BLOCK : (b + 1) * BLOCK]
            bias[b] = mask_columns(seg_col[...], row)

    weights = jnp.concatenate([wq[...], wk[...], wv[...]], axis=1)
    projected = dot_nn(xs[...], weights)
    query = (projected[:, :PAIR] + bq[...].astype(F32)).astype(LOW)
    key = projected[:, PAIR : 2 * PAIR].astype(LOW)
    value = (projected[:, 2 * PAIR :] + bv[...].astype(F32)).astype(LOW)
    q_out[...] = query
    k_out[...] = key
    v_out[...] = value
    qs[...] = query * jnp.asarray(SCALE, LOW)
    vt[...] = value.T

    def step(b, _):
        start = pl.multiple_of(b * BLOCK, BLOCK)
        q_block = qs[pl.ds(start, BLOCK), :]
        sides = []
        for head in range(2):
            scores = dot_nt(k_out[...], one_head(q_block, head)) + bias[b]
            top = jnp.max(scores, axis=0, keepdims=True)
            expo = jnp.exp(scores - top)
            total = jnp.sum(expo, axis=0, keepdims=True)
            probs = (expo * (1.0 / total)).astype(LOW)
            sides.append(dot_nn(vt[head * DH : (head + 1) * DH, :], probs))
            lse_out[0, head, pl.ds(b, 1), :] = top + jnp.log(total)
        ctx[pl.ds(start, BLOCK), :] = jnp.concatenate(sides, axis=0).T.astype(LOW)
        return 0

    lax.fori_loop(0, blocks, step, 0)
    for j, ref in enumerate((c0, c1, c2, c3)):
        ref[...] = ctx[pl.ds(pl.multiple_of((place ^ j) * quarter, quarter), quarter), :]


def attend_forward(info, quarters, qkv_weight, query_bias, value_bias, seg):
    quarter, width = quarters[0].shape
    tokens, half = 4 * quarter, width // 2
    pairs = half // PAIR

    def weight_spec(t):
        return pl.BlockSpec((width, PAIR), lambda p, i: (0, (2 * t + i[1]) * pairs + p))

    def bias_spec():
        return pl.BlockSpec((1, PAIR), lambda p, i: (0, i[1] * pairs + p))

    col = pl.BlockSpec((tokens, PAIR), lambda p, i: (0, p))
    part = pl.BlockSpec((quarter, PAIR), lambda p, i: (0, p))
    blocks = tokens // BLOCK
    return pl.pallas_call(
        forward_kernel,
        grid_spec=pltpu.PrefetchScalarGridSpec(
            num_scalar_prefetch=1,
            grid=(pairs,),
            in_specs=[full((quarter, width))] * 4
            + [weight_spec(0), weight_spec(1), weight_spec(2), bias_spec(), bias_spec()]
            + [full((tokens, 1)), full((1, tokens))],
            out_specs=[col] * 3
            + [part] * 4
            + [pl.BlockSpec((1, 2, blocks, BLOCK), lambda p, i: (p, 0, 0, 0))],
            scratch_shapes=[
                pltpu.VMEM((tokens, width), LOW),
                pltpu.VMEM((blocks, tokens, BLOCK), F32),
                pltpu.VMEM((tokens, PAIR), LOW),
                pltpu.VMEM((PAIR, tokens), LOW),
                pltpu.VMEM((tokens, PAIR), LOW),
            ],
        ),
        out_shape=[shaped((tokens, half), LOW)] * 3
        + [shaped((quarter, half), LOW)] * 4
        + [shaped((pairs, 2, blocks, BLOCK), F32)],
        compiler_params=params(56),
        name="attend_forward",
    )(
        info,
        *quarters,
        qkv_weight,
        qkv_weight,
        qkv_weight,
        query_bias[None],
        value_bias[None],
        seg[:, None],
        seg[None],
    )


def backward_kernel(
    info, q_in, k_in, v_in, o0, o1, o2, o3, lse, seg_col, seg_row,
    dq_out, dk_out, dv_out, bias_out,
    bias, qs, do, kt, dk, dv,
):
    place = info[0]
    tokens = q_in.shape[0]
    quarter = tokens // 4
    blocks = tokens // BLOCK

    @pl.when(pl.program_id(0) == 0)
    def _():
        for b in range(blocks):
            row = seg_row[:, b * BLOCK : (b + 1) * BLOCK]
            bias[b] = mask_columns(seg_col[...], row)

    for j, ref in enumerate((o0, o1, o2, o3)):
        do[pl.ds(pl.multiple_of((place ^ j) * quarter, quarter), quarter), :] = ref[...]
    qs[...] = q_in[...] * jnp.asarray(SCALE, LOW)
    kt[...] = k_in[...].T
    dk[...] = jnp.zeros_like(dk)
    dv[...] = jnp.zeros_like(dv)

    def step(b, dq_sum):
        start = pl.multiple_of(b * BLOCK, BLOCK)
        q_block = qs[pl.ds(start, BLOCK), :]
        o_block = do[pl.ds(start, BLOCK), :]
        sides, probs_low, d_scores_low, q_heads, o_heads = [], [], [], [], []
        for head in range(2):
            q_head, o_head = one_head(q_block, head), one_head(o_block, head)
            scores = dot_nt(k_in[...], q_head) + bias[b]
            probs = jnp.exp(scores - lse[0, head, pl.ds(b, 1), :])
            d_probs = dot_nt(v_in[...], o_head)
            delta = jnp.sum(probs * d_probs, axis=0, keepdims=True)
            d_scores = (probs * (d_probs - delta)).astype(LOW)
            sides.append(dot_nn(kt[head * DH : (head + 1) * DH, :], d_scores))
            probs_low.append(probs.astype(LOW))
            d_scores_low.append(d_scores)
            q_heads.append(q_head)
            o_heads.append(o_head)
        dk[...] += dot_nn(jnp.concatenate(d_scores_low, axis=1), jnp.concatenate(q_heads, axis=0))
        dv[...] += dot_nn(jnp.concatenate(probs_low, axis=1), jnp.concatenate(o_heads, axis=0))
        d_query = (jnp.concatenate(sides, axis=0).T * SCALE).astype(LOW)
        dq_out[pl.ds(start, BLOCK), :] = d_query
        return dq_sum + jnp.sum(d_query.astype(F32), axis=0, keepdims=True)

    dq_sum = lax.fori_loop(0, blocks, step, jnp.zeros((1, PAIR), F32))
    dk_out[...] = dk[...].astype(LOW)
    d_value = dv[...].astype(LOW)
    dv_out[...] = d_value
    bias_out[0, 0:1, :] = dq_sum
    bias_out[0, 1:2, :] = jnp.sum(d_value.astype(F32), axis=0, keepdims=True)


def attend_backward(info, query, key, value, parts, lse, seg):
    tokens, half = query.shape
    quarter, pairs, blocks = tokens // 4, half // PAIR, tokens // BLOCK
    col = pl.BlockSpec((tokens, PAIR), lambda p, i: (0, p))
    part = pl.BlockSpec((quarter, PAIR), lambda p, i: (0, p))
    return pl.pallas_call(
        backward_kernel,
        grid_spec=pltpu.PrefetchScalarGridSpec(
            num_scalar_prefetch=1,
            grid=(pairs,),
            in_specs=[col] * 3
            + [part] * 4
            + [pl.BlockSpec((1, 2, blocks, BLOCK), lambda p, i: (p, 0, 0, 0))]
            + [full((tokens, 1)), full((1, tokens))],
            out_specs=[col] * 3 + [pl.BlockSpec((1, 2, PAIR), lambda p, i: (p, 0, 0))],
            scratch_shapes=[
                pltpu.VMEM((blocks, tokens, BLOCK), F32),
                pltpu.VMEM((tokens, PAIR), LOW),
                pltpu.VMEM((tokens, PAIR), LOW),
                pltpu.VMEM((PAIR, tokens), LOW),
                pltpu.VMEM((tokens, PAIR), F32),
                pltpu.VMEM((tokens, PAIR), F32),
            ],
        ),
        out_shape=[shaped((tokens, half), LOW)] * 3 + [shaped((pairs, 2, PAIR), F32)],
        compiler_params=params(56),
        name="attend_backward",
    )(info, query, key, value, *parts, lse, seg[:, None], seg[None])


def normalise(values):
    centred = values - jnp.mean(values, axis=1, keepdims=True)
    root = lax.rsqrt(jnp.mean(centred * centred, axis=1, keepdims=True) + EPS)
    return centred * root, root


def norm_back(grad, gain, normal, root):
    e = grad * gain
    along = jnp.mean(e * normal, axis=1, keepdims=True)
    return root * (e - jnp.mean(e, axis=1, keepdims=True) - normal * along)


def column_sum(values):
    return jnp.sum(values, axis=0, keepdims=True)


def store_columns(place, flipped, mine, send):
    size = flipped.shape[0] // 4
    for b in range(4):
        rel = place ^ b

        @pl.when(rel % 2 == 0)
        def _():
            mine[pl.ds(rel // 2, 1)] = flipped[b * size : (b + 1) * size][None]

        @pl.when(rel % 2 == 1)
        def _():
            send[pl.ds(rel // 2, 1)] = flipped[b * size : (b + 1) * size][None]


def middle_forward_kernel(
    info, p0, p1, p2, p3, x_in, cot, wo, bo, g1, s1, up, bup, down, bdown, g2, s2,
    out, d_res, n1, r1, hid_t, ctx_t, act, slope, mine, send, vec,
    hid, hid_low, branch,
):
    place, core, chip = info[0], info[1], info[2]
    step = pl.program_id(0)
    quarter = p0.shape[0]

    @pl.when(step == 0)
    def _():
        first = core == 0

        def sides(a, b):
            a, b = a[...], b[...]
            return jnp.concatenate([jnp.where(first, a, b), jnp.where(first, b, a)], axis=1)

        ctx = jnp.concatenate([sides(p0, p1), sides(p2, p3)], axis=0)
        ctx_t[...] = ctx.T
        x = jnp.concatenate([x_in[chip], x_in[1 - chip]], axis=0).astype(F32)
        summed = x + dot_nn(ctx, wo[...]) + bo[...].astype(F32)
        normal, root = normalise(summed)
        n1[...] = normal
        r1[...] = root
        hidden = normal * g1[...].astype(F32) + s1[...].astype(F32)
        hid[...] = hidden
        low = hidden.astype(LOW)
        hid_low[...] = low
        hid_t[...] = low.T
        branch[...] = jnp.zeros_like(branch)

    pre = dot_nn(hid_low[...], up[...]) + bup[...].astype(F32)
    phi = 0.5 + 0.5 * lax.erf(pre * ROOT_HALF)
    low = (pre * phi).astype(LOW)
    act[...] = low
    slope[...] = phi + pre * (jnp.exp(-0.5 * pre * pre) * ROOT_TWO_PI)
    branch[...] += dot_nn(low, down[...])

    @pl.when(step == pl.num_programs(0) - 1)
    def _():
        normal, root = normalise(hid[...] + branch[...] + bdown[...].astype(F32))
        final = (normal * g2[...].astype(F32) + s2[...].astype(F32)).astype(LOW)
        out[pl.ds(chip, 1)] = final[:quarter][None]
        out[pl.ds(1 - chip, 1)] = final[quarter:][None]
        grad = jnp.concatenate([cot[chip], cot[1 - chip]], axis=0).astype(F32)
        back = norm_back(grad, g2[...].astype(F32), normal, root)
        d_res[...] = back
        vec[0:1, :] = column_sum(back)
        vec[1:2, :] = column_sum(grad * normal)
        vec[2:3, :] = column_sum(grad)
        store_columns(place, back.astype(LOW).T, mine, send)


def middle_forward(info, parts, inputs, cotangent, wo, bo, g1, s1, up, bup, down, bdown, g2, s2):
    quarter, half = parts[0].shape
    width, inner = 2 * half, up.shape[1]
    count, steps = 2 * quarter, 4
    chunk = inner // steps
    vector = full((1, width))
    tokens = full((count, width))
    turned = full((2, width // 4, count))
    return pl.pallas_call(
        middle_forward_kernel,
        grid_spec=pltpu.PrefetchScalarGridSpec(
            num_scalar_prefetch=1,
            grid=(steps,),
            in_specs=[full((quarter, half))] * 4
            + [full((2, quarter, width))] * 2
            + [full((width, width)), vector, vector, vector]
            + [
                pl.BlockSpec((width, chunk), lambda c, i: (0, c)),
                pl.BlockSpec((1, chunk), lambda c, i: (0, c)),
                pl.BlockSpec((chunk, width), lambda c, i: (c, 0)),
            ]
            + [vector] * 3,
            out_specs=[full((2, quarter, width)), tokens, tokens, full((count, 1))]
            + [full((width, count))] * 2
            + [pl.BlockSpec((count, chunk), lambda c, i: (0, c))] * 2
            + [turned, turned, full((8, width))],
            scratch_shapes=[
                pltpu.VMEM((count, width), F32),
                pltpu.VMEM((count, width), LOW),
                pltpu.VMEM((count, width), F32),
            ],
        ),
        out_shape=[
            shaped((2, quarter, width), LOW),
            shaped((count, width), F32),
            shaped((count, width), F32),
            shaped((count, 1), F32),
            shaped((width, count), LOW),
            shaped((width, count), LOW),
            shaped((count, inner), LOW),
            shaped((count, inner), F32),
            shaped((2, width // 4, count), LOW),
            shaped((2, width // 4, count), LOW),
            shaped((8, width), F32),
        ],
        compiler_params=params(60),
        name="middle_forward",
    )(
        info, *parts, inputs, cotangent, wo, bo[None], g1[None], s1[None],
        up, bup[None], down, bdown[None], g2[None], s2[None],
    )


def middle_backward_kernel(
    info, d_res, slope, down, up, wo, n1, r1, g1,
    send_pre, mine_pre, d_up_bias, d_summed, q0, q1, q2, q3, mine, send, vec,
    d_branch, d_hidden,
):
    place, core = info[0], info[1]
    step = pl.program_id(0)
    quarter = q0.shape[0]
    half = q0.shape[1]

    @pl.when(step == 0)
    def _():
        d_branch[...] = d_res[...].astype(LOW)
        d_hidden[...] = d_res[...]

    d_pre = (dot_nt(d_branch[...], down[...]) * slope[...]).astype(LOW)
    d_up_bias[...] = column_sum(d_pre.astype(F32))
    d_hidden[...] += dot_nt(d_pre, up[...])

    @pl.when(step < 2)
    def _():
        send_pre[0] = d_pre

    @pl.when(step >= 2)
    def _():
        mine_pre[0] = d_pre

    @pl.when(step == pl.num_programs(0) - 1)
    def _():
        grad = d_hidden[...]
        normal = n1[...]
        back = norm_back(grad, g1[...].astype(F32), normal, r1[...])
        d_summed[...] = back
        vec[0:1, :] = column_sum(back)
        vec[1:2, :] = column_sum(grad * normal)
        vec[2:3, :] = column_sum(grad)
        low = back.astype(LOW)
        store_columns(place, low.T, mine, send)
        d_ctx = dot_nt(low, wo[...]).astype(LOW)
        first = core == 0
        left, right = d_ctx[:, :half], d_ctx[:, half:]
        same = jnp.where(first, left, right)
        other = jnp.where(first, right, left)
        q0[...] = same[:quarter]
        q1[...] = other[:quarter]
        q2[...] = same[quarter:]
        q3[...] = other[quarter:]


def middle_backward(info, d_res, slope, down, up, wo, n1, r1, g1):
    count, width = d_res.shape
    inner, quarter, half = up.shape[1], count // 2, width // 2
    steps = 4
    chunk = inner // steps

    def block(c, i):
        return i[0] ^ (1 - c // 2 + 2 * (c % 2))

    tokens = full((count, width))
    turned = full((2, width // 4, count))
    return pl.pallas_call(
        middle_backward_kernel,
        grid_spec=pltpu.PrefetchScalarGridSpec(
            num_scalar_prefetch=1,
            grid=(steps,),
            in_specs=[
                tokens,
                pl.BlockSpec((count, chunk), lambda c, i: (0, block(c, i))),
                pl.BlockSpec((chunk, width), lambda c, i: (block(c, i), 0)),
                pl.BlockSpec((width, chunk), lambda c, i: (0, block(c, i))),
                full((width, width)),
                tokens,
                full((count, 1)),
                full((1, width)),
            ],
            out_specs=[
                pl.BlockSpec((1, count, chunk), lambda c, i: (jnp.minimum(c, 1), 0, 0)),
                pl.BlockSpec((1, count, chunk), lambda c, i: (jnp.maximum(c - 2, 0), 0, 0)),
                pl.BlockSpec((1, chunk), lambda c, i: (0, block(c, i))),
                tokens,
            ]
            + [full((quarter, half))] * 4
            + [turned, turned, full((8, width))],
            scratch_shapes=[pltpu.VMEM((count, width), LOW), pltpu.VMEM((count, width), F32)],
        ),
        out_shape=[
            shaped((2, count, chunk), LOW),
            shaped((2, count, chunk), LOW),
            shaped((1, inner), F32),
            shaped((count, width), F32),
        ]
        + [shaped((quarter, half), LOW)] * 4
        + [
            shaped((2, width // 4, count), LOW),
            shaped((2, width // 4, count), LOW),
            shaped((8, width), F32),
        ],
        compiler_params=params(60),
        name="middle_backward",
    )(info, d_res, slope, down, up, wo, n1, r1, g1[None])


def spot(rel, flip_x, order):
    bits = {"y": rel % 2, "z": (rel // 2) % 2, "w": rel // 4, "x": flip_x}
    index = 0
    for axis in order[1:]:
        index = index * 2 + bits[axis]
    return bits[order[0]], index


def put(value, rel, flip_x, order, send, keep):
    sent, index = spot(rel, flip_x, order)
    if isinstance(sent, int):
        if sent:
            send[pl.ds(index, 1)] = value.astype(LOW)[None]
        else:
            keep[pl.ds(index, 1)] = value[None]
        return

    @pl.when(sent == 1)
    def _():
        send[pl.ds(index, 1)] = value.astype(LOW)[None]

    @pl.when(sent == 0)
    def _():
        keep[pl.ds(index, 1)] = value[None]


DOWN_ORDERS = ("yzxw", "zyxw", "xyzw")


def down_kernel(info, mine, theirs, act, act_pair, *outs):
    rel = pl.program_id(0)
    size = mine.shape[1]
    left = jnp.concatenate([mine[0], mine[1]], axis=0)
    left_pair = jnp.concatenate([theirs[0], theirs[1]], axis=0)
    grad = dot_nn(left, act[...]) + dot_nn(left_pair, act_pair[...])
    wide = grad.shape[1] // len(DOWN_ORDERS)
    for n, order in enumerate(DOWN_ORDERS):
        for flip in range(2):
            value = grad[flip * size : (flip + 1) * size, n * wide : (n + 1) * wide]
            put(value, rel, flip, order, outs[2 * n], outs[2 * n + 1])


def down_grad(info, mine, theirs, act, act_pair):
    _, size, count = mine.shape
    block = act.shape[1] // 8
    wide = block // len(DOWN_ORDERS)
    part = full((8, size, wide))
    shapes = [shaped((8, size, wide), LOW), shaped((8, size, wide), F32)]
    spec = pl.BlockSpec((count, block), lambda r, i: (0, r ^ i[3]))
    return pl.pallas_call(
        down_kernel,
        grid_spec=pltpu.PrefetchScalarGridSpec(
            num_scalar_prefetch=1,
            grid=(8,),
            in_specs=[full((2, size, count))] * 2 + [spec, spec],
            out_specs=[part] * 2 * len(DOWN_ORDERS),
        ),
        out_shape=shapes * len(DOWN_ORDERS),
        compiler_params=params(48),
        name="down_grad",
    )(info, mine, theirs, act, act_pair)


UP_ORDERS = ("zyxw", "xyzw", "yzxw")


def up_kernel(info, left, left_pair, mine, theirs, *outs):
    me = info[3]
    step = pl.program_id(0)
    n_parts = len(UP_ORDERS)
    grad = dot_nn(left[...], mine[0]) + dot_nn(left_pair[...], theirs[0])
    deep = grad.shape[0] // 8
    flip = step // n_parts
    for n, order in enumerate(UP_ORDERS):

        @pl.when(step % n_parts == n)
        def _():
            for b in range(8):
                value = grad[b * deep : (b + 1) * deep]
                put(value, me ^ b, flip, order, outs[2 * n], outs[2 * n + 1])


def up_grad(info, left, left_pair, mine, theirs):
    width, count = left.shape
    n_parts = len(UP_ORDERS)
    wide = mine.shape[2] // n_parts
    part = full((8, width // 8, wide))
    shapes = [shaped((8, width // 8, wide), LOW), shaped((8, width // 8, wide), F32)]
    spec = pl.BlockSpec((1, count, wide), lambda s, i: (s // n_parts, 0, s % n_parts))
    return pl.pallas_call(
        up_kernel,
        grid_spec=pltpu.PrefetchScalarGridSpec(
            num_scalar_prefetch=1,
            grid=(2 * n_parts,),
            in_specs=[full((width, count))] * 2 + [spec, spec],
            out_specs=[part] * 2 * n_parts,
        ),
        out_shape=shapes * n_parts,
        compiler_params=params(48),
        name="up_grad",
    )(info, left, left_pair, mine, theirs)


def out_kernel(info, left, left_pair, mine, theirs, send, keep):
    me = info[3]
    right = jnp.concatenate([mine[0], mine[1]], axis=0)
    right_pair = jnp.concatenate([theirs[0], theirs[1]], axis=0)
    grad = dot_nt(left[...], right) + dot_nt(left_pair[...], right_pair)
    deep = grad.shape[0] // 8
    for b in range(8):
        put(grad[b * deep : (b + 1) * deep], me ^ b, 0, "yzw", send, keep)


def out_grad(info, left, left_pair, mine, theirs):
    width, count = left.shape
    wide = 2 * mine.shape[1]
    part = full((4, width // 8, wide))
    return pl.pallas_call(
        out_kernel,
        grid_spec=pltpu.PrefetchScalarGridSpec(
            num_scalar_prefetch=1,
            grid=(1,),
            in_specs=[full((width, count))] * 2 + [full(mine.shape)] * 2,
            out_specs=[part, part],
        ),
        out_shape=[shaped((4, width // 8, wide), LOW), shaped((4, width // 8, wide), F32)],
        compiler_params=params(48),
        name="out_grad",
    )(info, left, left_pair, mine, theirs)


QKV_ORDERS = ("yzw", "zyw", "ywz")


def qkv_kernel(info, x_t, dq, dk, dv, *outs):
    me = info[3]
    step = pl.program_id(0)
    for n, (ref, order) in enumerate(zip((dq, dk, dv), QKV_ORDERS)):

        @pl.when(step == n)
        def _():
            grad = dot_nn(x_t[...], ref[...])
            deep = grad.shape[0] // 8
            for b in range(8):
                value = grad[b * deep : (b + 1) * deep]
                put(value, me ^ b, 0, order, outs[2 * n], outs[2 * n + 1])


def qkv_grad(info, x_t, dq, dk, dv):
    width, tokens = x_t.shape
    half = dq.shape[1]
    part = full((4, width // 8, half))
    shapes = [shaped((4, width // 8, half), LOW), shaped((4, width // 8, half), F32)]
    return pl.pallas_call(
        qkv_kernel,
        grid_spec=pltpu.PrefetchScalarGridSpec(
            num_scalar_prefetch=1,
            grid=(3,),
            in_specs=[full((width, tokens))] + [full((tokens, half))] * 3,
            out_specs=[part] * 6,
        ),
        out_shape=shapes * 3,
        compiler_params=params(48),
        name="qkv_grad",
    )(info, x_t, dq, dk, dv)


def input_kernel(info, dq, dk, dv, wq, wk, wv, keep, send):
    rel = pl.program_id(0)
    grad = dot_nt(dq[...], wq[...]) + dot_nt(dk[...], wk[...]) + dot_nt(dv[...], wv[...])

    @pl.when(rel < 2)
    def _():
        send[0] = grad

    @pl.when(rel >= 2)
    def _():
        keep[0] = grad


def input_part(info, dq, dk, dv, qkv_weight):
    tokens, half = dq.shape
    quarter, width = tokens // 4, 2 * half

    rows = pl.BlockSpec((quarter, half), lambda c, i: (i[0] ^ (1 - c // 2 + 2 * (c % 2)), 0))

    def weight(t):
        return pl.BlockSpec((width, half), lambda c, i: (0, 2 * t + i[1]))

    return pl.pallas_call(
        input_kernel,
        grid_spec=pltpu.PrefetchScalarGridSpec(
            num_scalar_prefetch=1,
            grid=(4,),
            in_specs=[rows] * 3 + [weight(0), weight(1), weight(2)],
            out_specs=[
                pl.BlockSpec((1, quarter, width), lambda c, i: (jnp.maximum(c - 2, 0), 0, 0)),
                pl.BlockSpec((1, quarter, width), lambda c, i: (jnp.minimum(c, 1), 0, 0)),
            ],
        ),
        out_shape=[shaped((2, quarter, width), F32)] * 2,
        compiler_params=params(48),
        name="input_part",
    )(info, dq, dk, dv, qkv_weight, qkv_weight, qkv_weight)


def turn_kernel(info, x0, x1, x2, x3, x_t):
    quarter = x0.shape[0]
    for j, ref in enumerate((x0, x1, x2, x3)):
        at = pl.multiple_of((info[0] ^ j) * quarter, quarter)
        x_t[:, pl.ds(at, quarter)] = ref[...].T


def turn(info, quarters):
    quarter, width = quarters[0].shape
    return pl.pallas_call(
        turn_kernel,
        grid_spec=pltpu.PrefetchScalarGridSpec(
            num_scalar_prefetch=1,
            grid=(1,),
            in_specs=[full((quarter, width))] * 4,
            out_specs=full((width, 4 * quarter)),
        ),
        out_shape=shaped((width, 4 * quarter), LOW),
        compiler_params=params(48),
        name="turn",
    )(info, *quarters)


def body(
    inputs,
    segments,
    qkv_weight,
    query_bias,
    value_bias,
    out_weight,
    out_bias,
    norm1_gain,
    norm1_shift,
    up_weight,
    up_bias,
    down_weight,
    down_bias,
    norm2_gain,
    norm2_shift,
    cotangent,
):
    rows, quarter, width = inputs.shape
    half = width // 2
    seq_size = lax.axis_size("seq")
    batch_size = lax.axis_size("batch")
    fine = batch_size // 8
    place = lax.axis_index("seq")
    chip, core = place // 2, place % 2
    info = jnp.stack([place, core, chip, lax.axis_index("batch") // fine]).astype(jnp.int32)

    def over_seq(array, flip):
        return lax.ppermute(array, "seq", [(i, i ^ flip) for i in range(seq_size)])

    def over_batch(array, flip):
        return lax.ppermute(array, "batch", [(i, i ^ flip) for i in range(batch_size)])

    def swap(array, axis):
        if axis == "x":
            return over_seq(array, 2)
        return over_batch(array, fine << "yzw".index(axis))

    def pick(array, index, axis=0):
        return lax.dynamic_index_in_dim(array, index, axis, keepdims=False)

    def settle(sent, kept, order):
        for axis in order:
            total = kept + swap(sent, axis).astype(F32)
            middle = total.shape[0] // 2
            if middle:
                kept, sent = total[:middle], total[middle:].astype(LOW)
        return total[0]

    def finish(grad):
        if fine > 1:
            groups = [[i * fine + j for j in range(fine)] for i in range(8)]
            grad = lax.psum_scatter(
                grad, "batch", scatter_dimension=0, axis_index_groups=groups, tiled=True
            )
        return grad

    own = pick(inputs, chip)
    far = over_seq(pick(inputs, 1 - chip), 2)
    near = over_seq(own, 1)
    across = over_seq(far, 1)
    quarters = (own, near, far, across)
    segment = pick(segments, chip)

    query, key, value, *parts, lse = attend_forward(
        info, quarters, qkv_weight, query_bias, value_bias, segment
    )
    parts = [parts[0]] + [over_seq(parts[j], j) for j in (1, 2, 3)]
    x_t = turn(info, quarters)

    outputs, d_res, n1, r1, hid_t, ctx_t, act, slope, mine, send, vec_two = middle_forward(
        info, parts, inputs, cotangent, out_weight, out_bias, norm1_gain, norm1_shift,
        up_weight, up_bias, down_weight, down_bias, norm2_gain, norm2_shift,
    )
    hid_pair, ctx_pair, act_pair = over_seq(hid_t, 1), over_seq(ctx_t, 1), over_seq(act, 1)
    downs = down_grad(info, mine, over_seq(send, 1), act, act_pair)
    down_total = [
        settle(downs[2 * n], downs[2 * n + 1], order) for n, order in enumerate(DOWN_ORDERS)
    ]
    down_total = finish(jnp.concatenate(down_total, axis=1).T)

    send_pre, mine_pre, d_up_bias, d_summed, q0, q1, q2, q3, mine, send, vec_one = middle_backward(
        info, d_res, slope, down_weight, up_weight, out_weight, n1, r1, norm1_gain
    )
    d_parts = [q0, over_seq(q1, 1), over_seq(q2, 2), over_seq(q3, 3)]
    ups = up_grad(info, hid_t, hid_pair, mine_pre, over_seq(send_pre, 1))
    up_total = [settle(ups[2 * n], ups[2 * n + 1], order) for n, order in enumerate(UP_ORDERS)]
    up_total = finish(jnp.concatenate(up_total, axis=1))
    outs = out_grad(info, ctx_t, ctx_pair, mine, over_seq(send, 1))
    out_total = settle(outs[0], outs[1], "yzw")
    wide = out_total.shape[1] // 2
    out_total = out_total[:, :wide] + over_seq(out_total[:, wide:].astype(LOW), 2).astype(F32)
    out_total = finish(out_total)

    def spread(vector):
        for flip in (1, 2):
            vector = vector + over_seq(vector, flip)
        flip = 1
        while flip < batch_size:
            vector = vector + over_batch(vector, flip)
            flip *= 2
        return vector

    early = spread(jnp.concatenate([vec_one[:3], vec_two[:3], d_up_bias.reshape(-1, width)]))

    dq, dk, dv, bias_part = attend_backward(info, query, key, value, d_parts, lse, segment)
    bias_part = bias_part.transpose(1, 0, 2).reshape(2, 1, half)
    late = spread(
        jnp.concatenate(
            [jnp.where(core == 0, bias_part, 0.0), jnp.where(core == 1, bias_part, 0.0)], axis=1
        ).reshape(2, width)
    )

    qkvs = qkv_grad(info, x_t, dq, dk, dv)
    d_qkv = [settle(qkvs[2 * n], qkvs[2 * n + 1], order) for n, order in enumerate(QKV_ORDERS)]
    unit = half // 2
    units = [part[:, side * unit : (side + 1) * unit] for part in d_qkv for side in range(2)]
    first = core == 0
    sent = [jnp.where(first, units[a], units[b]) for a, b in ((2, 0), (3, 2), (5, 3))]
    kept = [jnp.where(first, units[a], units[b]) for a, b in ((0, 1), (1, 4), (4, 5))]
    swapped = over_seq(jnp.stack(sent), 1)
    chip_zero = jnp.stack(
        [kept[0], jnp.where(first, kept[1], swapped[0]), jnp.where(first, swapped[0], swapped[1])]
    )
    chip_one = jnp.stack(
        [jnp.where(first, swapped[1], swapped[2]), jnp.where(first, swapped[2], kept[1]), kept[2]]
    )
    stay = jnp.where(chip == 0, chip_zero, chip_one)
    leave = jnp.where(chip == 0, chip_one, chip_zero)
    total = stay + over_seq(leave.astype(LOW), 2).astype(F32)
    qkv_total = finish(total.transpose(1, 0, 2).reshape(-1, 3 * unit))

    keep, send = input_part(info, dq, dk, dv, qkv_weight)
    d_row = keep + over_seq(send, 1)
    d_near = d_summed[:quarter] + d_row[0]
    d_far = d_summed[quarter:] + over_seq(d_row[1].astype(LOW), 2).astype(F32)
    d_inputs = jnp.stack([jnp.where(chip == 0, d_near, d_far), jnp.where(chip == 0, d_far, d_near)])
    return (
        outputs,
        d_inputs,
        qkv_total,
        late[0],
        late[1],
        out_total,
        early[0],
        early[1],
        early[2],
        up_total,
        early[6:].reshape(-1),
        down_total,
        early[3],
        early[4],
        early[5],
    )


def solution(mesh):
    whole, split = P(), P("batch", "seq")
    tokens = P("batch", "seq", None)
    return jax.shard_map(
        body,
        mesh=mesh,
        in_specs=(tokens, P("batch", None)) + (whole,) * 13 + (tokens,),
        out_specs=(tokens, tokens, split, whole, whole, split)
        + (whole,) * 3
        + (split, whole, split)
        + (whole,) * 3,
        check_vma=False,
    )
```

```python
import functools

import jax
import jax.numpy as jnp
from jax import lax
from jax.experimental import pallas as pl
from jax.experimental.pallas import tpu as pltpu
from jax.sharding import PartitionSpec as P

DH = 64
EPS = 1e-05
NEG = -1000000000.0
F32 = jnp.float32
LOW = jnp.bfloat16
PAIR = 2 * DH
SCALE = DH**-0.5
BLOCK = 128
SIZES = (2, 3, 4, 5, 6, 8)
VMEM = 60
ROOT_HALF = 0.5**0.5
ROOT_TWO_PI = 0.3989422804014327


def shaped(shape, dtype):
    return jax.ShapeDtypeStruct(shape, dtype)


def dot_nn(left, right):
    return jnp.dot(left, right, preferred_element_type=F32)


def dot_nt(left, right):
    return lax.dot_general(left, right, (((1,), (1,)), ((), ())), preferred_element_type=F32)


def params(mib):
    return pltpu.CompilerParams(vmem_limit_bytes=mib << 20, dimension_semantics=("arbitrary",))


def full(shape):
    return pl.BlockSpec(shape, lambda *_: (0,) * len(shape))


def cost(micros):
    return pl.CostEstimate(flops=int(micros * 1.15e9), transcendentals=0, bytes_accessed=0)


def column_sum(values):
    return jnp.sum(values, axis=0, keepdims=True)


def spot(rel, flip_x, order):
    bits = {"y": rel % 2, "z": (rel // 2) % 2, "w": rel // 4, "x": flip_x}
    index = 0
    for axis in order[1:]:
        index = index * 2 + bits[axis]
    return bits[order[0]], index


def put(value, rel, flip_x, order, send, keep):
    sent, index = spot(rel, flip_x, order)

    @pl.when(sent == 1)
    def _():
        send[pl.ds(index, 1)] = value.astype(LOW)[None]

    @pl.when(sent == 0)
    def _():
        keep[pl.ds(index, 1)] = value[None]


def put_rows(grad, rows, me, flip_x, order, send, keep):
    deep = grad.shape[0] // 8
    for b in range(8):
        rows[b] = grad[b * deep : (b + 1) * deep]
    for rel in range(8):
        sent, index = spot(rel, flip_x, order)
        value = rows[me ^ rel]
        if sent:
            send[index] = value.astype(LOW)
        else:
            keep[index] = value


def join_kernel(segments, routes, *refs):
    ins, outs = refs[: 2 * len(segments)], list(refs[2 * len(segments) :])
    for route in routes:
        send = outs.pop(0) if any(segments[m][n] > 1 for m, n in route) else None
        keep = outs.pop(0)
        sent = filled = 0
        for m, n in route:
            start, size = sum(segments[m][:n]), segments[m][n]
            total = ins[2 * m][start : start + size]
            total = total + ins[2 * m + 1][start : start + size].astype(F32)
            if size > 1:
                size //= 2
                send[sent : sent + size] = total[size:].astype(LOW)
                sent += size
            keep[filled : filled + size] = total[:size]
            filled += size


def join(messages, routes):
    segments = [list(message[0]) for message in messages]
    tail = messages[0][1].shape[1:]
    shapes, results = [], []
    for route in routes:
        sizes = [segments[m][n] for m, n in route]
        left = [size // 2 for size in sizes if size > 1]
        results.append(left)
        if left:
            shapes.append(shaped((sum(left),) + tail, LOW))
        shapes.append(shaped((sum(max(size // 2, 1) for size in sizes),) + tail, F32))
    operands = [array for message in messages for array in message[1:]]
    arrays = pl.pallas_call(
        functools.partial(join_kernel, segments, routes),
        grid=(1,),
        in_specs=[full(array.shape) for array in operands],
        out_specs=[full(shape.shape) for shape in shapes],
        out_shape=shapes,
        compiler_params=params(VMEM),
        cost_estimate=cost(1),
        name="join",
    )(*operands)
    arrays = list(arrays)
    return [(left, arrays.pop(0) if left else None, arrays.pop(0)) for left in results]


def each_window(info, block, run):
    start = pl.multiple_of(info[4 + block], BLOCK)
    kind = info[4 + (info.shape[0] - 4) // 2 + block]
    for n, size in enumerate(SIZES):

        @pl.when(kind == n)
        def _():
            run(pl.ds(start, size * BLOCK), size * BLOCK)


def windows(segment):
    tokens = segment.shape[0]
    rows = segment.reshape(tokens // BLOCK, BLOCK)
    first = jnp.sum((segment[None] < rows[:, :1]).astype(jnp.int32), axis=1) // BLOCK
    last = (jnp.sum((segment[None] <= rows[:, -1:]).astype(jnp.int32), axis=1) - 1) // BLOCK
    need = last - first + 1
    kind = sum((need > size).astype(jnp.int32) for size in SIZES[:-1])
    size = sum(
        jnp.where(kind == n, size, 0).astype(jnp.int32) for n, size in enumerate(SIZES)
    )
    return [jnp.minimum(first, tokens // BLOCK - size) * BLOCK, kind]


def both_heads(array):
    lane = lax.broadcasted_iota(jnp.int32, array.shape, 1)
    zero = jnp.zeros_like(array)
    return jnp.concatenate(
        [jnp.where(lane < DH, array, zero), jnp.where(lane < DH, zero, array)], axis=0
    )


def own_heads(turned):
    return jnp.concatenate([turned[:DH, :BLOCK], turned[DH:, BLOCK:]], axis=0)


def fill_segments(seg_row, seg_col):
    seg_col[...] = jnp.broadcast_to(seg_row[...].astype(F32), (BLOCK, seg_row.shape[1])).T


def masked_scores(key, query, seg_col, seg_row):
    same = seg_col == seg_row
    return jnp.where(jnp.concatenate([same, same], axis=1), dot_nt(key, query), NEG)


def forward_kernel(
    info, x0, x1, x2, x3, wq, wk, wv, bq, bv, seg_row,
    q_out, k_out, v_out, c0, c1, c2, c3, o_out, lse_out,
    xs, seg_col, qs, vt, ctx,
):
    place = info[0]
    tokens = xs.shape[0]
    quarter = tokens // 4

    @pl.when(pl.program_id(0) == 0)
    def _():
        for j, ref in enumerate((x0, x1, x2, x3)):
            xs[pl.ds(pl.multiple_of((place ^ j) * quarter, quarter), quarter), :] = ref[...]
        fill_segments(seg_row, seg_col)

    weights = jnp.concatenate([wq[...], wk[...], wv[...]], axis=1)
    projected = dot_nn(xs[...], weights)
    query = (projected[:, :PAIR] + bq[...].astype(F32)).astype(LOW)
    key = projected[:, PAIR : 2 * PAIR].astype(LOW)
    value = (projected[:, 2 * PAIR :] + bv[...].astype(F32)).astype(LOW)
    q_out[...] = query
    k_out[...] = key
    v_out[...] = value
    qs[...] = query * jnp.asarray(SCALE, LOW)
    vt[...] = value.T

    def step(b, _):
        start = pl.multiple_of(b * BLOCK, BLOCK)
        rows = pl.ds(start, BLOCK)

        def run(window, size):
            row = seg_row[:, rows].astype(F32)
            scores = masked_scores(k_out[window, :], both_heads(qs[rows, :]), seg_col[window, :], row)
            top = jnp.max(scores, axis=0, keepdims=True)
            expo = jnp.exp(scores - top)
            total = jnp.sum(expo, axis=0, keepdims=True)
            mixed = dot_nn(vt[:, window], expo.astype(LOW)) * (1.0 / total)
            lse_out[0, pl.ds(b, 1), :] = top + jnp.log(total)
            mixed = own_heads(mixed)
            o_out[:, rows] = mixed
            ctx[rows, :] = mixed.T.astype(LOW)

        each_window(info, b, run)
        return 0

    lax.fori_loop(0, tokens // BLOCK, step, 0)
    for j, ref in enumerate((c0, c1, c2, c3)):
        ref[...] = ctx[pl.ds(pl.multiple_of((place ^ j) * quarter, quarter), quarter), :]


def attend_forward(info, quarters, qkv_weight, query_bias, value_bias, seg):
    quarter, width = quarters[0].shape
    tokens, half = 4 * quarter, width // 2
    pairs = half // PAIR

    def weight_spec(t):
        return pl.BlockSpec((width, PAIR), lambda p, i: (0, (2 * t + i[1]) * pairs + p))

    def bias_spec():
        return pl.BlockSpec((1, PAIR), lambda p, i: (0, i[1] * pairs + p))

    col = pl.BlockSpec((tokens, PAIR), lambda p, i: (0, p))
    part = pl.BlockSpec((quarter, PAIR), lambda p, i: (0, p))
    blocks = tokens // BLOCK
    return pl.pallas_call(
        forward_kernel,
        grid_spec=pltpu.PrefetchScalarGridSpec(
            num_scalar_prefetch=1,
            grid=(pairs,),
            in_specs=[full((quarter, width))] * 4
            + [weight_spec(0), weight_spec(1), weight_spec(2), bias_spec(), bias_spec()]
            + [full((1, tokens))],
            out_specs=[col] * 3
            + [part] * 4
            + [pl.BlockSpec((PAIR, tokens), lambda p, i: (p, 0))]
            + [pl.BlockSpec((1, blocks, 2 * BLOCK), lambda p, i: (p, 0, 0))],
            scratch_shapes=[
                pltpu.VMEM((tokens, width), LOW),
                pltpu.VMEM((tokens, BLOCK), F32),
                pltpu.VMEM((tokens, PAIR), LOW),
                pltpu.VMEM((PAIR, tokens), LOW),
                pltpu.VMEM((tokens, PAIR), LOW),
            ],
        ),
        out_shape=[shaped((tokens, half), LOW)] * 3
        + [shaped((quarter, half), LOW)] * 4
        + [shaped((half, tokens), F32), shaped((pairs, blocks, 2 * BLOCK), F32)],
        compiler_params=params(VMEM),
        cost_estimate=cost(16),
        name="attend_forward",
    )(info, *quarters, qkv_weight, qkv_weight, qkv_weight, query_bias[None], value_bias[None], seg)


QKV_ORDERS = ("yzw", "zyw", "yzw")


def backward_kernel(
    order, info, q_in, k_in, v_in, o0, o1, o1b, o2, o3, o_in, lse, seg_row, x_t,
    dq_out, dk_out, dv_out, bias_out, w_send, w_keep,
    seg_col, qs, do, kt, dk, dv, w_rows,
):
    place, me = info[0], info[3]
    tokens = q_in.shape[0]
    quarter = tokens // 4
    fill_segments(seg_row, seg_col)
    for j, ref in enumerate((o0, None, o2, o3)):
        if ref is None:
            at = pl.multiple_of((place ^ 1) * quarter, quarter)
            do[pl.ds(at, quarter // 2), :] = o1[...]
            do[pl.ds(at + quarter // 2, quarter // 2), :] = o1b[...]
            continue
        do[pl.ds(pl.multiple_of((place ^ j) * quarter, quarter), quarter), :] = ref[...]
    qs[...] = q_in[...] * jnp.asarray(SCALE, LOW)
    kt[...] = k_in[...].T
    dk[...] = jnp.zeros_like(dk)
    dv[...] = jnp.zeros_like(dv)

    def step(b, _):
        start = pl.multiple_of(b * BLOCK, BLOCK)
        rows = pl.ds(start, BLOCK)

        def run(window, size):
            row = seg_row[:, rows].astype(F32)
            o_block = do[rows, :]
            query, grad = both_heads(qs[rows, :]), both_heads(o_block)
            along = o_block.T.astype(F32) * o_in[:, rows]
            delta = jnp.concatenate([column_sum(along[:DH]), column_sum(along[DH:])], axis=1)
            scores = masked_scores(k_in[window, :], query, seg_col[window, :], row)
            probs = jnp.exp(scores - lse[0, pl.ds(b, 1), :])
            d_scores = (probs * (dot_nt(v_in[window, :], grad) - delta)).astype(LOW)
            dv[window, :] += dot_nn(probs.astype(LOW), grad)
            dk[window, :] += dot_nn(d_scores, query)
            d_query = own_heads(dot_nn(kt[:, window], d_scores)) * SCALE
            dq_out[rows, :] = d_query.T.astype(LOW)

        each_window(info, b, run)
        return 0

    lax.fori_loop(0, tokens // BLOCK, step, 0)
    dk_out[...] = dk[...].astype(LOW)
    dv_out[...] = dv[...].astype(LOW)
    bias_out[0:1, :] = column_sum(dq_out[...].astype(F32))
    bias_out[1:2, :] = column_sum(dv_out[...].astype(F32))
    grad = jnp.concatenate([dq_out[...], dk_out[...], dv_out[...]], axis=1)
    grad = dot_nn(x_t[...], grad)
    put_rows(grad, w_rows, me, 0, order, w_send, w_keep)


def attend_backward(info, n, query, key, value, parts, context, lse, seg, x_t):
    tokens, half = query.shape
    quarter, blocks, width = tokens // 4, tokens // BLOCK, x_t.shape[0]
    col = pl.BlockSpec((tokens, PAIR), lambda p, i: (0, n))
    pairs = half // PAIR
    part = pl.BlockSpec((quarter, PAIR), lambda p, i: (0, n))
    first = pl.BlockSpec((None, quarter, PAIR), lambda p, i: (0, 0, n))
    packed = quarter // 2
    low, high = [
        pl.BlockSpec((packed, PAIR), lambda p, i, at=at: (half // packed, at * pairs + n))
        for at in range(2)
    ]
    weight = (4, width // 8, 3 * PAIR)
    return pl.pallas_call(
        functools.partial(backward_kernel, QKV_ORDERS[n]),
        grid_spec=pltpu.PrefetchScalarGridSpec(
            num_scalar_prefetch=1,
            grid=(1,),
            in_specs=[col] * 3
            + [part, low, high, first, part]
            + [pl.BlockSpec((PAIR, tokens), lambda p, i: (n, 0))]
            + [pl.BlockSpec((1, blocks, 2 * BLOCK), lambda p, i: (n, 0, 0))]
            + [full((1, tokens)), full((width, tokens))],
            out_specs=[full((tokens, PAIR))] * 3 + [full((2, PAIR))] + [full(weight)] * 2,
            scratch_shapes=[
                pltpu.VMEM((tokens, BLOCK), F32),
                pltpu.VMEM((tokens, PAIR), LOW),
                pltpu.VMEM((tokens, PAIR), LOW),
                pltpu.VMEM((PAIR, tokens), LOW),
                pltpu.VMEM((tokens, PAIR), F32),
                pltpu.VMEM((tokens, PAIR), F32),
                pltpu.VMEM((8, width // 8, 3 * PAIR), F32),
            ],
        ),
        out_shape=[shaped((tokens, PAIR), LOW)] * 3
        + [shaped((2, PAIR), F32), shaped(weight, LOW), shaped(weight, F32)],
        compiler_params=params(VMEM),
        cost_estimate=cost(8),
        name="attend_backward",
    )(info, query, key, value, *parts, context, lse, seg, x_t)


def normalise(values):
    centred = values - jnp.mean(values, axis=1, keepdims=True)
    root = lax.rsqrt(jnp.mean(centred * centred, axis=1, keepdims=True) + EPS)
    return centred * root, root


def norm_back(grad, gain, normal, root):
    e = grad * gain
    along = jnp.mean(e * normal, axis=1, keepdims=True)
    return root * (e - jnp.mean(e, axis=1, keepdims=True) - normal * along)


def store_columns(place, flipped, mine, send):
    size, count = flipped.shape[0] // 4, flipped.shape[1]
    for b in range(4):
        rel = place ^ b

        @pl.when(rel % 2 == 0)
        def _():
            mine[pl.ds(rel // 2, 1)] = flipped[b * size : (b + 1) * size][None]

        @pl.when(rel % 2 == 1)
        def _():
            rows = pl.ds(pl.multiple_of(rel // 2 * size, size), size)
            send[rows, :count] = flipped[b * size : (b + 1) * size]


def middle_forward_kernel(
    info, p0, p1, p2, p3, x_in, cot, wo, bo, g1, s1, up, bup, down, bdown, g2, s2,
    out, d_res, n1, r1, turned, act, slope, mine, send, vec,
    hid, hid_low, branch,
):
    place, core, chip = info[0], info[1], info[2]
    step = pl.program_id(0)
    quarter = p0.shape[0]

    @pl.when(step == 0)
    def _():
        first = core == 0

        def sides(a, b):
            a, b = a[...], b[...]
            return jnp.concatenate([jnp.where(first, a, b), jnp.where(first, b, a)], axis=1)

        ctx = jnp.concatenate([sides(p0, p1), sides(p2, p3)], axis=0)
        turned[1] = ctx.T
        x = jnp.concatenate([x_in[chip], x_in[1 - chip]], axis=0).astype(F32)
        summed = x + dot_nn(ctx, wo[...]) + bo[...].astype(F32)
        normal, root = normalise(summed)
        n1[...] = normal
        r1[...] = root
        hidden = normal * g1[...].astype(F32) + s1[...].astype(F32)
        hid[...] = hidden
        low = hidden.astype(LOW)
        hid_low[...] = low
        turned[0] = low.T
        branch[...] = jnp.zeros_like(branch)

    pre = dot_nn(hid_low[...], up[...]) + bup[...].astype(F32)
    phi = 0.5 + 0.5 * lax.erf(pre * ROOT_HALF)
    low = (pre * phi).astype(LOW)
    act[...] = low
    slope[...] = phi + pre * (jnp.exp(-0.5 * pre * pre) * ROOT_TWO_PI)
    branch[...] += dot_nn(low, down[...])

    @pl.when(step == pl.num_programs(0) - 1)
    def _():
        normal, root = normalise(hid[...] + branch[...] + bdown[...].astype(F32))
        final = (normal * g2[...].astype(F32) + s2[...].astype(F32)).astype(LOW)
        out[pl.ds(chip, 1)] = final[:quarter][None]
        out[pl.ds(1 - chip, 1)] = final[quarter:][None]
        grad = jnp.concatenate([cot[chip], cot[1 - chip]], axis=0).astype(F32)
        back = norm_back(grad, g2[...].astype(F32), normal, root)
        d_res[...] = back
        vec[0:1, :] = column_sum(back)
        vec[1:2, :] = column_sum(grad * normal)
        vec[2:3, :] = column_sum(grad)
        store_columns(place, back.astype(LOW).T, mine, send)


def middle_forward(info, parts, inputs, cotangent, wo, bo, g1, s1, up, bup, down, bdown, g2, s2):
    quarter, half = parts[0].shape
    width, inner = 2 * half, up.shape[1]
    count, steps = 2 * quarter, 4
    chunk = inner // steps
    vector = full((1, width))
    tokens = full((count, width))
    turned = full((2, width // 4, count))
    return pl.pallas_call(
        middle_forward_kernel,
        grid_spec=pltpu.PrefetchScalarGridSpec(
            num_scalar_prefetch=1,
            grid=(steps,),
            in_specs=[full((quarter, half))] * 4
            + [full((2, quarter, width))] * 2
            + [full((width, width)), vector, vector, vector]
            + [
                pl.BlockSpec((width, chunk), lambda c, i: (0, c)),
                pl.BlockSpec((1, chunk), lambda c, i: (0, c)),
                pl.BlockSpec((chunk, width), lambda c, i: (c, 0)),
            ]
            + [vector] * 3,
            out_specs=[full((2, quarter, width)), tokens, tokens, full((count, 1))]
            + [full((2, width, count))]
            + [pl.BlockSpec((count, chunk), lambda c, i: (0, c))] * 2
            + [turned, full((width // 2, count)), full((8, width))],
            scratch_shapes=[
                pltpu.VMEM((count, width), F32),
                pltpu.VMEM((count, width), LOW),
                pltpu.VMEM((count, width), F32),
            ],
        ),
        out_shape=[
            shaped((2, quarter, width), LOW),
            shaped((count, width), F32),
            shaped((count, width), F32),
            shaped((count, 1), F32),
            shaped((2, width, count), LOW),
            shaped((count, inner), LOW),
            shaped((count, inner), F32),
            shaped((2, width // 4, count), LOW),
            shaped((width // 2, count), LOW),
            shaped((8, width), F32),
        ],
        compiler_params=params(VMEM),
        cost_estimate=cost(18),
        name="middle_forward",
    )(
        info, *parts, inputs, cotangent, wo, bo[None], g1[None], s1[None],
        up, bup[None], down, bdown[None], g2[None], s2[None],
    )


def middle_backward_kernel(
    info, d_res, slope, down, up, wo, n1, r1, g1,
    to_core, mine_pre, d_up_bias, d_summed, q0, to_chip, mine, vec,
    d_branch, d_hidden,
):
    place, core = info[0], info[1]
    step = pl.program_id(0)
    quarter = q0.shape[0]
    half = q0.shape[1]
    count = d_res.shape[0]

    @pl.when(step == 0)
    def _():
        d_branch[...] = d_res[...].astype(LOW)
        d_hidden[...] = d_res[...]

    d_pre = (dot_nt(d_branch[...], down[...]) * slope[...]).astype(LOW)
    d_up_bias[...] = column_sum(d_pre.astype(F32))
    d_hidden[...] += dot_nt(d_pre, up[...])

    @pl.when(step < 2)
    def _():
        at = pl.multiple_of((1 + step) * count, count)
        to_core[pl.ds(at, count), :] = d_pre

    @pl.when(step >= 2)
    def _():
        mine_pre[0] = d_pre

    @pl.when(step == pl.num_programs(0) - 1)
    def _():
        grad = d_hidden[...]
        normal = n1[...]
        back = norm_back(grad, g1[...].astype(F32), normal, r1[...])
        d_summed[...] = back
        vec[0:1, :] = column_sum(back)
        vec[1:2, :] = column_sum(grad * normal)
        vec[2:3, :] = column_sum(grad)
        low = back.astype(LOW)
        store_columns(place, low.T, mine, to_core)
        d_ctx = dot_nt(low, wo[...]).astype(LOW)
        first = core == 0
        left, right = d_ctx[:, :half], d_ctx[:, half:]
        same = jnp.where(first, left, right)
        other = jnp.where(first, right, left)
        q0[...] = same[:quarter]
        packed = quarter // 2
        to_core[half : half + packed, :] = jnp.concatenate(
            [other[:packed], other[packed:quarter]], axis=1
        )
        to_chip[0] = same[quarter:]
        to_chip[1] = other[quarter:]


def middle_backward(info, d_res, slope, down, up, wo, n1, r1, g1):
    count, width = d_res.shape
    inner, quarter, half = up.shape[1], count // 2, width // 2
    steps = 4
    chunk = inner // steps

    def block(c, i):
        return i[0] ^ (1 - c // 2 + 2 * (c % 2))

    tokens = full((count, width))
    turned = full((2, width // 4, count))
    return pl.pallas_call(
        middle_backward_kernel,
        grid_spec=pltpu.PrefetchScalarGridSpec(
            num_scalar_prefetch=1,
            grid=(steps,),
            in_specs=[
                tokens,
                pl.BlockSpec((count, chunk), lambda c, i: (0, block(c, i))),
                pl.BlockSpec((chunk, width), lambda c, i: (block(c, i), 0)),
                pl.BlockSpec((width, chunk), lambda c, i: (0, block(c, i))),
                full((width, width)),
                tokens,
                full((count, 1)),
                full((1, width)),
            ],
            out_specs=[
                full((3 * count, width)),
                pl.BlockSpec((1, count, chunk), lambda c, i: (jnp.maximum(c - 2, 0), 0, 0)),
                pl.BlockSpec((1, chunk), lambda c, i: (0, block(c, i))),
                tokens,
            ]
            + [full((quarter, half)), full((2, quarter, half)), turned, full((8, width))],
            scratch_shapes=[pltpu.VMEM((count, width), LOW), pltpu.VMEM((count, width), F32)],
        ),
        out_shape=[
            shaped((3 * count, width), LOW),
            shaped((2, count, chunk), LOW),
            shaped((1, inner), F32),
            shaped((count, width), F32),
        ]
        + [
            shaped((quarter, half), LOW),
            shaped((2, quarter, half), LOW),
            shaped((2, width // 4, count), LOW),
            shaped((8, width), F32),
        ],
        compiler_params=params(VMEM),
        cost_estimate=cost(16),
        name="middle_backward",
    )(info, d_res, slope, down, up, wo, n1, r1, g1[None])


DOWN_ORDERS = ("zxyw", "xzyw")


def down_kernel(info, mine, theirs, act, act_pair, *outs):
    rel = pl.program_id(0)
    left = jnp.concatenate([mine[0], mine[1]], axis=0)
    grad = dot_nn(left, act[...]) + dot_nn(theirs[...], act_pair[...])
    size = grad.shape[0] // 4
    for n, order in enumerate(DOWN_ORDERS):
        for flip in range(2):
            start = (2 * flip + n) * size
            put(grad[start : start + size], rel, flip, order, outs[2 * n], outs[2 * n + 1])


def down_grad(info, mine, theirs, act, act_pair):
    _, size, count = mine.shape
    block = act.shape[1] // 8
    part = (8, size // 2, block)
    spec = pl.BlockSpec((count, block), lambda r, i: (0, r ^ i[3]))
    return pl.pallas_call(
        down_kernel,
        grid_spec=pltpu.PrefetchScalarGridSpec(
            num_scalar_prefetch=1,
            grid=(8,),
            in_specs=[full(mine.shape), full(theirs.shape), spec, spec],
            out_specs=[full(part)] * 4,
        ),
        out_shape=[shaped(part, LOW), shaped(part, F32)] * 2,
        compiler_params=params(VMEM),
        cost_estimate=cost(8),
        name="down_grad",
    )(info, mine, theirs, act, act_pair)


UP_ORDERS = ("xyzw", "yxzw")


def up_kernel(
    info, left, left_pair, mine, theirs, mine_d, theirs_d, send_a, keep_a, send_b, keep_b, rows
):
    me = info[3]
    step = pl.program_id(0)

    @pl.when(step < 4)
    def _():
        grad = dot_nn(left[0], mine[0]) + dot_nn(left_pair[0], theirs[...])
        for n, flip in ((0, 0), (1, 0), (0, 1), (1, 1)):

            @pl.when(step == 2 * flip + n)
            def _():
                send, keep = ((send_a, keep_a), (send_b, keep_b))[n]
                put_rows(grad, rows, me, flip, UP_ORDERS[n], send, keep)

    @pl.when(step == 4)
    def _():
        right = jnp.concatenate([mine_d[0], mine_d[1]], axis=0)
        grad = dot_nt(left[1], right) + dot_nt(left_pair[1], theirs_d[...])
        deep, wide = grad.shape[0] // 8, grad.shape[1] // 2
        for b in range(8):
            rows[b] = grad[b * deep : (b + 1) * deep]
        for rel in range(4):
            near, far = rows[me ^ rel], rows[me ^ (rel + 4)]
            for flip in range(2):
                cut = slice(flip * wide, (flip + 1) * wide)
                value = jnp.concatenate([near[:, cut], far[:, cut]], axis=1)
                index = 8 + 2 * flip + rel // 2
                if rel % 2:
                    send_b[index] = value.astype(LOW)
                else:
                    keep_b[index] = value


def up_grad(info, left, left_pair, mine, from_core, mine_d):
    _, width, count = left.shape
    half = width // 2

    def at(s):
        return jnp.minimum(s, 3)

    shapes = [
        shaped((lead, width // 8, half), dtype) for lead in (8, 12) for dtype in (LOW, F32)
    ]
    return pl.pallas_call(
        up_kernel,
        grid_spec=pltpu.PrefetchScalarGridSpec(
            num_scalar_prefetch=1,
            grid=(5,),
            in_specs=[full(left.shape)] * 2
            + [
                pl.BlockSpec((1, count, half), lambda s, i: (at(s) // 2, 0, at(s) % 2)),
                pl.BlockSpec((count, half), lambda s, i: (1 + at(s) // 2, at(s) % 2)),
                full(mine_d.shape),
                pl.BlockSpec((half, count), lambda s, i: (0, 0)),
            ],
            out_specs=[full(shape.shape) for shape in shapes],
            scratch_shapes=[pltpu.VMEM((8, width // 8, half), F32)],
        ),
        out_shape=shapes,
        compiler_params=params(VMEM),
        cost_estimate=cost(10),
        name="up_grad",
    )(info, left, left_pair, mine, from_core, mine_d, from_core)


def input_kernel(info, *refs):
    grads, weights, (keep, send) = refs[:9], refs[9:12], refs[12:]
    rel = pl.program_id(0)
    total = sum(
        dot_nt(jnp.concatenate([ref[...] for ref in grads[t::3]], axis=1), weights[t][...])
        for t in range(3)
    )

    @pl.when(rel < 2)
    def _():
        send[0] = total

    @pl.when(rel >= 2)
    def _():
        keep[0] = total


def input_part(info, grads, qkv_weight):
    tokens = grads[0].shape[0]
    width = qkv_weight.shape[0]
    quarter, half = tokens // 4, width // 2

    rows = pl.BlockSpec((quarter, PAIR), lambda c, i: (i[0] ^ (1 - c // 2 + 2 * (c % 2)), 0))

    def weight(t):
        return pl.BlockSpec((width, half), lambda c, i: (0, 2 * t + i[1]))

    return pl.pallas_call(
        input_kernel,
        grid_spec=pltpu.PrefetchScalarGridSpec(
            num_scalar_prefetch=1,
            grid=(4,),
            in_specs=[rows] * 9 + [weight(0), weight(1), weight(2)],
            out_specs=[
                pl.BlockSpec((1, quarter, width), lambda c, i: (jnp.maximum(c - 2, 0), 0, 0)),
                pl.BlockSpec((1, quarter, width), lambda c, i: (jnp.minimum(c, 1), 0, 0)),
            ],
        ),
        out_shape=[shaped((2, quarter, width), F32)] * 2,
        compiler_params=params(VMEM),
        cost_estimate=cost(6),
        name="input_part",
    )(info, *grads, qkv_weight, qkv_weight, qkv_weight)


UNITS = (((0, 1), (2, 3), (4,), (5,)), ((0,), (1,), (2, 3), (4, 5)))


def share_kernel(info, *refs):
    place, core = info[0], info[1]
    kept, got, (own, one, two, three) = refs[:3], refs[3:6], refs[6:]
    total = [kept[n][0] + got[n][0].astype(F32) for n in range(3)]
    units = []
    for t in range(3):
        part = jnp.concatenate([pair[:, t * PAIR : (t + 1) * PAIR] for pair in total], axis=1)
        units += jnp.split(part, 2, axis=1)
    for side in range(2):
        for target in range(4):
            for flip, ref in enumerate((own, one, two, three)):

                @pl.when(jnp.logical_and(core == side, place ^ target == flip))
                def _():
                    for n in range(2):
                        unit = units[UNITS[side][target][n % len(UNITS[side][target])]]
                        ref[n] = unit.astype(ref.dtype)


def share(info, kept, got):
    unit = (2, kept[0].shape[1], kept[0].shape[2] // 2)
    return pl.pallas_call(
        share_kernel,
        grid_spec=pltpu.PrefetchScalarGridSpec(
            num_scalar_prefetch=1,
            grid=(1,),
            in_specs=[full(kept[0].shape)] * 6,
            out_specs=[full(unit)] * 4,
        ),
        out_shape=[shaped(unit, F32)] + [shaped(unit, LOW)] * 3,
        compiler_params=params(VMEM),
        cost_estimate=cost(1),
        name="share",
    )(info, *kept, *got)


def gather_kernel(info, own, one, two, three, out):
    place = info[0]
    same = own[...] + two[...].astype(F32)
    other = one[...].astype(F32) + three[...].astype(F32)
    for target in range(4):

        @pl.when(place == target)
        def _():
            sides = (same, other) if target % 2 == 0 else (other, same)
            pieces = [
                (side_unit, sides[side][n])
                for side in range(2)
                for n, side_unit in enumerate(
                    unit % 2 + 4 * (unit // 2) + 2 * side for unit in UNITS[side][target]
                )
            ]
            pieces.sort(key=lambda piece: piece[0])
            out[...] = jnp.concatenate([piece[1] for piece in pieces], axis=1)


def gather(info, own, *others):
    shape = (own.shape[1], 3 * own.shape[2])
    return pl.pallas_call(
        gather_kernel,
        grid_spec=pltpu.PrefetchScalarGridSpec(
            num_scalar_prefetch=1,
            grid=(1,),
            in_specs=[full(own.shape)] * 4,
            out_specs=full(shape),
        ),
        out_shape=shaped(shape, F32),
        compiler_params=params(VMEM),
        cost_estimate=cost(1),
        name="gather",
    )(info, own, *others)


def turn_kernel(info, x0, x1, x2, x3, x_t):
    quarter = x0.shape[0]
    for j, ref in enumerate((x0, x1, x2, x3)):
        at = pl.multiple_of((info[0] ^ j) * quarter, quarter)
        x_t[:, pl.ds(at, quarter)] = ref[...].T


def turn(info, quarters):
    quarter, width = quarters[0].shape
    return pl.pallas_call(
        turn_kernel,
        grid_spec=pltpu.PrefetchScalarGridSpec(
            num_scalar_prefetch=1,
            grid=(1,),
            in_specs=[full((quarter, width))] * 4,
            out_specs=full((width, 4 * quarter)),
        ),
        out_shape=shaped((width, 4 * quarter), LOW),
        compiler_params=params(VMEM),
        cost_estimate=cost(1),
        name="turn",
    )(info, *quarters)


def body(
    inputs,
    segments,
    qkv_weight,
    query_bias,
    value_bias,
    out_weight,
    out_bias,
    norm1_gain,
    norm1_shift,
    up_weight,
    up_bias,
    down_weight,
    down_bias,
    norm2_gain,
    norm2_shift,
    cotangent,
):
    rows, quarter, width = inputs.shape
    half = width // 2
    seq_size = lax.axis_size("seq")
    batch_size = lax.axis_size("batch")
    fine = batch_size // 8
    place = lax.axis_index("seq")
    chip, core = place // 2, place % 2
    segment = lax.dynamic_index_in_dim(segments, chip, 0)
    info = jnp.stack([place, core, chip, lax.axis_index("batch") // fine]).astype(jnp.int32)
    info = jnp.concatenate([info] + windows(segment[0]))

    def over_seq(array, flip):
        return lax.ppermute(array, "seq", [(i, i ^ flip) for i in range(seq_size)])

    def over_batch(array, flip):
        return lax.ppermute(array, "batch", [(i, i ^ flip) for i in range(batch_size)])

    def swap(array, axis):
        if axis == "x":
            return over_seq(array, 2)
        return over_batch(array, fine << "yzw".index(axis))

    def pick(array, index, axis=0):
        return lax.dynamic_index_in_dim(array, index, axis, keepdims=False)

    def tie(*arrays):
        return lax.optimization_barrier(arrays)

    def launch(*messages):
        return [
            (order, segments, kept, swap(sent, order[0]))
            for order, segments, sent, kept in messages
        ]

    def land(products, flights, *routes):
        count = len(products)
        tied = tie(*products, *[flight[3] for flight in flights])
        landed = [flight[1:3] + (got,) for flight, got in zip(flights, tied[count:])]
        made = join(landed, [route[1:] for route in routes])
        return list(tied[:count]), [(route[0],) + new for route, new in zip(routes, made)]

    def follow(array, messages):
        array, *kept = tie(array, *[message[3] for message in messages])
        return [array] + [message[:3] + (own,) for message, own in zip(messages, kept)]

    def finish(grad):
        if fine > 1:
            groups = [[i * fine + j for j in range(fine)] for i in range(8)]
            grad = lax.psum_scatter(
                grad, "batch", scatter_dimension=0, axis_index_groups=groups, tiled=True
            )
        return grad

    own = pick(inputs, chip)
    far = over_seq(pick(inputs, 1 - chip), 2)
    near = over_seq(own, 1)
    across = over_seq(far, 1)
    quarters = (own, near, far, across)

    query, key, value, *parts, context, lse = attend_forward(
        info, quarters, qkv_weight, query_bias, value_bias, segment
    )
    parts = [parts[0]] + [over_seq(parts[j], j) for j in (1, 2, 3)]
    x_t = turn(info, quarters)
    parts[0], x_t = tie(parts[0], x_t)

    outputs, d_res, n1, r1, turned, act, slope, mine, send, vec_two = middle_forward(
        info, parts, inputs, cotangent, out_weight, out_bias, norm1_gain, norm1_shift,
        up_weight, up_bias, down_weight, down_bias, norm2_gain, norm2_shift,
    )
    pair = over_seq(turned, 1), over_seq(act, 1), over_seq(send, 1)
    back = middle_backward(
        info, d_res, slope, down_weight, up_weight, out_weight, n1, r1, norm1_gain
    )
    turned_pair, act_pair, theirs, *back = tie(*pair, *back)
    to_core, mine_pre, d_up_bias, d_summed, q0, to_chip, mine_d, vec_one = back
    mine, d_summed = tie(mine, d_summed)

    from_core, from_chip = over_seq(to_core, 1), over_seq(to_chip, 2)
    made = down_grad(info, mine, theirs, act, act_pair)
    from_core, from_chip, *made = tie(from_core, from_chip, *made)
    downs = launch(
        (DOWN_ORDERS[0], [8], made[0], made[1]), (DOWN_ORDERS[1], [8], made[2], made[3])
    )
    across = over_seq(from_chip[1], 1)
    made = up_grad(info, turned, turned_pair, mine_pre, from_core, mine_d)
    across, *made = tie(across, *made)
    ups = launch((UP_ORDERS[0], [8], made[0], made[1]), (UP_ORDERS[1], [8, 4], made[2], made[3]))
    d_parts = (q0, from_core, from_core, from_chip, across)

    def piece(n, query):
        made = attend_backward(
            info, n, query, key, value, d_parts, context, lse, segment, x_t
        )
        return made

    def opening(n, made):
        return QKV_ORDERS[n], [4], made[4], made[5]

    zero = piece(0, query)
    zero, downs = land(zero, downs, (DOWN_ORDERS[0][1:], (0, 0)), (DOWN_ORDERS[1][1:], (1, 0)))
    query, *downs = follow(query, downs)
    *downs, first = launch(*downs, opening(0, zero))

    one = piece(1, query)
    one, (up_a, up_b, down, first) = land(
        one,
        ups + downs + [first],
        (UP_ORDERS[0][1:], (0, 0)),
        (UP_ORDERS[1][1:], (1, 0), (1, 1)),
        ("yw", (2, 0), (3, 0)),
        (QKV_ORDERS[0][1:], (4, 0)),
    )
    query, up_a, up_b, down, first = follow(query, [up_a, up_b, down, first])
    flights = launch(up_a, up_b, down, opening(1, one), first)

    two = piece(2, query)
    two, (up, down, second, first) = land(
        two,
        flights,
        ("zw", (0, 0), (1, 0), (1, 1)),
        ("w", (2, 0), (2, 1)),
        (QKV_ORDERS[1][1:], (3, 0)),
        ("w", (4, 0)),
    )
    grads = [*zero[:3], *one[:3], *two[:3]]
    grads[0], up, down, second, first = follow(grads[0], [up, down, second, first])
    flights = launch(opening(2, two), up, down, second)
    bias_part = jnp.concatenate([zero[3], one[3], two[3]], axis=1)
    bias_zero = jnp.zeros_like(bias_part)
    bias_part = jnp.where(
        core == 0,
        jnp.concatenate([bias_part, bias_zero], axis=1),
        jnp.concatenate([bias_zero, bias_part], axis=1),
    )
    vectors = jnp.concatenate([vec_one[:3], vec_two[:3], d_up_bias.reshape(-1, width), bias_part])
    vectors_got = over_seq(vectors, 1)

    keep, send = input_part(info, grads, qkv_weight)
    (keep, send, vectors_got), (third, up, down, second) = land(
        [keep, send, vectors_got],
        flights,
        (QKV_ORDERS[2][1:], (0, 0)),
        ("w", (1, 0), (1, 1), (1, 2)),
        ("", (2, 0), (2, 1)),
        ("w", (3, 0)),
    )
    out_total, down_total = up[3][2], down[3]
    third, up, first = launch(third, up, first)
    vectors = vectors + vectors_got
    vectors_got = over_seq(vectors, 2)
    d_row_got = over_seq(send, 1)
    first_got, (d_row_got, vectors_got), (third, up) = first[3], *land(
        [d_row_got, vectors_got], [third, up], ("w", (0, 0)), ("", (1, 0), (1, 1))
    )
    up_total = up[3]
    vectors = vectors + vectors_got
    third, second = launch(third, second)
    vectors = vectors + swap(vectors, "y")
    vectors_got = swap(vectors, "z")
    d_row = keep + d_row_got
    d_far = over_seq(d_row[1].astype(LOW), 2)
    third_got, second_got, vectors_got, d_far = tie(third[3], second[3], vectors_got, d_far)
    own, *others = share(
        info, (first[2], second[2], third[2]), (first_got, second_got, third_got)
    )
    qkv_total = gather(info, own, *[over_seq(other, 1 + j) for j, other in enumerate(others)])
    qkv_total = finish(qkv_total)
    vectors = vectors + vectors_got
    wide = half // 2
    out_total = out_total[:, :wide] + swap(out_total[:, wide:].astype(LOW), "w").astype(F32)
    out_total = finish(out_total)
    down_total = finish(down_total.reshape(wide, half).T)
    up_total = finish(jnp.concatenate([up_total[0], up_total[1]], axis=1))

    vectors = vectors + swap(vectors, "w")
    flip = 1
    while flip < fine:
        vectors = vectors + over_batch(vectors, flip)
        flip *= 2
    d_near = d_summed[:quarter] + d_row[0]
    d_far = d_summed[quarter:] + d_far.astype(F32)
    d_inputs = jnp.stack([jnp.where(chip == 0, d_near, d_far), jnp.where(chip == 0, d_far, d_near)])
    return (
        outputs,
        d_inputs,
        qkv_total,
        vectors[-2],
        vectors[-1],
        out_total,
        vectors[0],
        vectors[1],
        vectors[2],
        up_total,
        vectors[6:-2].reshape(-1),
        down_total,
        vectors[3],
        vectors[4],
        vectors[5],
    )


def solution(mesh):
    whole, split = P(), P("batch", "seq")
    tokens = P("batch", "seq", None)
    return jax.shard_map(
        body,
        mesh=mesh,
        in_specs=(tokens, P("batch", None)) + (whole,) * 13 + (tokens,),
        out_specs=(tokens, tokens, split, whole, whole, split)
        + (whole,) * 3
        + (split, whole, split)
        + (whole,) * 3,
        check_vma=False,
    )
```

```python
import functools

import jax
import jax.numpy as jnp
from jax import lax
from jax.experimental import pallas as pl
from jax.experimental.pallas import tpu as pltpu
from jax.sharding import PartitionSpec as P

DH = 64
EPS = 1e-05
NEG = -1000000000.0
F32 = jnp.float32
LOW = jnp.bfloat16
PAIR = 2 * DH
SCALE = DH**-0.5
BLOCK = 128
SIZES = (2, 3, 5, 6, 8)
VMEM = 18
ROOT_HALF = 0.5**0.5
ROOT_TWO_PI = 0.3989422804014327


def shaped(shape, dtype):
    return jax.ShapeDtypeStruct(shape, dtype)


def dot_nn(left, right):
    return jnp.dot(left, right, preferred_element_type=F32)


def dot_nt(left, right):
    return lax.dot_general(left, right, (((1,), (1,)), ((), ())), preferred_element_type=F32)


def params(mib):
    return pltpu.CompilerParams(vmem_limit_bytes=mib << 20, dimension_semantics=("arbitrary",))


def waiting(after):
    return [pl.BlockSpec(memory_space=pl.ANY)] * len(after)


def ordered(kernel, after):
    return lambda info, *refs: kernel(info, *refs[len(after) :])


def full(shape):
    return pl.BlockSpec(shape, lambda *_: (0,) * len(shape))


def cost(micros):
    return pl.CostEstimate(flops=int(micros * 0.6e9), transcendentals=0, bytes_accessed=0)


def column_sum(values):
    return jnp.sum(values, axis=0, keepdims=True)


def spot(rel, flip_x, order):
    bits = {"y": rel % 2, "z": (rel // 2) % 2, "w": rel // 4, "x": flip_x}
    index = 0
    for axis in order[1:]:
        index = index * 2 + bits[axis]
    return bits[order[0]], index


def put(value, rel, flip_x, order, send, keep):
    sent, index = spot(rel, flip_x, order)

    @pl.when(sent == 1)
    def _():
        send[pl.ds(index, 1)] = value.astype(LOW)[None]

    @pl.when(sent == 0)
    def _():
        keep[pl.ds(index, 1)] = value[None]


def put_rows(grad, rows, me, flip_x, order, send, keep):
    deep = grad.shape[0] // 8
    for b in range(8):
        rows[b] = grad[b * deep : (b + 1) * deep]
    for rel in range(8):
        sent, index = spot(rel, flip_x, order)
        value = rows[me ^ rel]
        if sent:
            send[index] = value.astype(LOW)
        else:
            keep[index] = value


def join_kernel(skip, segments, routes, *refs):
    refs = refs[skip:]
    ins, outs = refs[: 2 * len(segments)], list(refs[2 * len(segments) : -1])
    refs[-1][...] = jnp.zeros_like(refs[-1])
    for route in routes:
        send = outs.pop(0) if any(segments[m][n] > 1 for m, n in route) else None
        keep = outs.pop(0)
        sent = filled = 0
        for m, n in route:
            start, size = sum(segments[m][:n]), segments[m][n]
            total = ins[2 * m][start : start + size]
            total = total + ins[2 * m + 1][start : start + size].astype(F32)
            if size > 1:
                size //= 2
                send[sent : sent + size] = total[size:].astype(LOW)
                sent += size
            keep[filled : filled + size] = total[:size]
            filled += size


def join(messages, routes, after):
    segments = [list(message[0]) for message in messages]
    tail = messages[0][1].shape[1:]
    shapes, results = [], []
    for route in routes:
        sizes = [segments[m][n] for m, n in route]
        left = [size // 2 for size in sizes if size > 1]
        results.append(left)
        if left:
            shapes.append(shaped((sum(left),) + tail, LOW))
        shapes.append(shaped((sum(max(size // 2, 1) for size in sizes),) + tail, F32))
    operands = [array for message in messages for array in message[1:]]
    shapes.append(shaped((8, 128), F32))
    *arrays, token = pl.pallas_call(
        functools.partial(join_kernel, len(after), segments, routes),
        grid=(1,),
        in_specs=waiting(after) + [full(array.shape) for array in operands],
        out_specs=[full(shape.shape) for shape in shapes],
        out_shape=shapes,
        compiler_params=params(VMEM),
        cost_estimate=cost(1),
        name="join",
    )(*after, *operands)
    return [(left, arrays.pop(0) if left else None, arrays.pop(0)) for left in results], token


def each_window(info, block, run):
    start = pl.multiple_of(info[4 + block], BLOCK)
    kind = info[4 + (info.shape[0] - 4) // 2 + block]
    for n, size in enumerate(SIZES):

        @pl.when(kind == n)
        def _():
            run(pl.ds(start, size * BLOCK), size * BLOCK)


def windows(segment):
    tokens = segment.shape[0]
    rows = segment.reshape(tokens // BLOCK, BLOCK)
    first = jnp.sum((segment[None] < rows[:, :1]).astype(jnp.int32), axis=1) // BLOCK
    last = (jnp.sum((segment[None] <= rows[:, -1:]).astype(jnp.int32), axis=1) - 1) // BLOCK
    need = last - first + 1
    kind = sum((need > size).astype(jnp.int32) for size in SIZES[:-1])
    size = sum(
        jnp.where(kind == n, size, 0).astype(jnp.int32) for n, size in enumerate(SIZES)
    )
    return [jnp.minimum(first, tokens // BLOCK - size) * BLOCK, kind]


def both_heads(array):
    lane = lax.broadcasted_iota(jnp.int32, array.shape, 1)
    zero = jnp.zeros_like(array)
    return jnp.concatenate(
        [jnp.where(lane < DH, array, zero), jnp.where(lane < DH, zero, array)], axis=0
    )


def own_heads(turned):
    return jnp.concatenate([turned[:DH, :BLOCK], turned[DH:, BLOCK:]], axis=0)


def fill_segments(seg_row, seg_col):
    seg_col[...] = jnp.broadcast_to(seg_row[...].astype(F32), (BLOCK, seg_row.shape[1])).T


def masked_scores(key, query, seg_col, seg_row):
    same = seg_col == seg_row
    return jnp.where(jnp.concatenate([same, same], axis=1), dot_nt(key, query), NEG)


def forward_kernel(
    info, x0, x1, x2, x3, wq, wk, wv, bq, bv, seg_row,
    q_out, k_out, v_out, c0, c1, c2, c3, o_out, lse_out,
    xs, seg_col, qs, vt, ctx,
):
    place = info[0]
    tokens = xs.shape[0]
    quarter = tokens // 4

    @pl.when(pl.program_id(0) == 0)
    def _():
        for j, ref in enumerate((x0, x1, x2, x3)):
            xs[pl.ds(pl.multiple_of((place ^ j) * quarter, quarter), quarter), :] = ref[...]
        fill_segments(seg_row, seg_col)

    weights = jnp.concatenate([wq[...], wk[...], wv[...]], axis=1)
    projected = dot_nn(xs[...], weights)
    query = (projected[:, :PAIR] + bq[...].astype(F32)).astype(LOW)
    key = projected[:, PAIR : 2 * PAIR].astype(LOW)
    value = (projected[:, 2 * PAIR :] + bv[...].astype(F32)).astype(LOW)
    q_out[...] = query
    k_out[...] = key
    v_out[...] = value
    qs[...] = query * jnp.asarray(SCALE, LOW)
    vt[...] = value.T

    def step(b, _):
        start = pl.multiple_of(b * BLOCK, BLOCK)
        rows = pl.ds(start, BLOCK)

        def run(window, size):
            row = seg_row[:, rows].astype(F32)
            scores = masked_scores(k_out[window, :], both_heads(qs[rows, :]), seg_col[window, :], row)
            top = jnp.max(scores, axis=0, keepdims=True)
            expo = jnp.exp(scores - top)
            total = jnp.sum(expo, axis=0, keepdims=True)
            mixed = dot_nn(vt[:, window], expo.astype(LOW)) * (1.0 / total)
            lse_out[0, pl.ds(b, 1), :] = top + jnp.log(total)
            mixed = own_heads(mixed)
            o_out[:, rows] = mixed
            ctx[rows, :] = mixed.T.astype(LOW)

        each_window(info, b, run)
        return 0

    lax.fori_loop(0, tokens // BLOCK, step, 0)
    for j, ref in enumerate((c0, c1, c2, c3)):
        ref[...] = ctx[pl.ds(pl.multiple_of((place ^ j) * quarter, quarter), quarter), :]


def attend_forward(info, quarters, qkv_weight, query_bias, value_bias, seg):
    quarter, width = quarters[0].shape
    tokens, half = 4 * quarter, width // 2
    pairs = half // PAIR

    def weight_spec(t):
        return pl.BlockSpec((width, PAIR), lambda p, i: (0, (2 * t + i[1]) * pairs + p))

    def bias_spec():
        return pl.BlockSpec((1, PAIR), lambda p, i: (0, i[1] * pairs + p))

    col = pl.BlockSpec((tokens, PAIR), lambda p, i: (0, p))
    part = pl.BlockSpec((quarter, PAIR), lambda p, i: (0, p))
    blocks = tokens // BLOCK
    return pl.pallas_call(
        forward_kernel,
        grid_spec=pltpu.PrefetchScalarGridSpec(
            num_scalar_prefetch=1,
            grid=(pairs,),
            in_specs=[full((quarter, width))] * 4
            + [weight_spec(0), weight_spec(1), weight_spec(2), bias_spec(), bias_spec()]
            + [full((1, tokens))],
            out_specs=[col] * 3
            + [part] * 4
            + [pl.BlockSpec((PAIR, tokens), lambda p, i: (p, 0))]
            + [pl.BlockSpec((1, blocks, 2 * BLOCK), lambda p, i: (p, 0, 0))],
            scratch_shapes=[
                pltpu.VMEM((tokens, width), LOW),
                pltpu.VMEM((tokens, BLOCK), F32),
                pltpu.VMEM((tokens, PAIR), LOW),
                pltpu.VMEM((PAIR, tokens), LOW),
                pltpu.VMEM((tokens, PAIR), LOW),
            ],
        ),
        out_shape=[shaped((tokens, half), LOW)] * 3
        + [shaped((quarter, half), LOW)] * 4
        + [shaped((half, tokens), F32), shaped((pairs, blocks, 2 * BLOCK), F32)],
        compiler_params=params(VMEM),
        cost_estimate=cost(16),
        name="attend_forward",
    )(info, *quarters, qkv_weight, qkv_weight, qkv_weight, query_bias[None], value_bias[None], seg)


QKV_ORDERS = ("yzw", "zyw", "yzw")


def backward_kernel(
    order, info, q_in, k_in, v_in, o0, o1, o1b, o2, o3, o_in, lse, seg_row, x_t,
    dq_out, dk_out, dv_out, bias_out, w_send, w_keep,
    seg_col, qs, do, kt, dk, dv, w_rows,
):
    place, me = info[0], info[3]
    tokens = q_in.shape[0]
    quarter = tokens // 4
    fill_segments(seg_row, seg_col)
    for j, ref in enumerate((o0, None, o2, o3)):
        if ref is None:
            at = pl.multiple_of((place ^ 1) * quarter, quarter)
            do[pl.ds(at, quarter // 2), :] = o1[...]
            do[pl.ds(at + quarter // 2, quarter // 2), :] = o1b[...]
            continue
        do[pl.ds(pl.multiple_of((place ^ j) * quarter, quarter), quarter), :] = ref[...]
    qs[...] = q_in[...] * jnp.asarray(SCALE, LOW)
    kt[...] = k_in[...].T
    dk[...] = jnp.zeros_like(dk)
    dv[...] = jnp.zeros_like(dv)

    def step(b, _):
        start = pl.multiple_of(b * BLOCK, BLOCK)
        rows = pl.ds(start, BLOCK)

        def run(window, size):
            row = seg_row[:, rows].astype(F32)
            o_block = do[rows, :]
            query, grad = both_heads(qs[rows, :]), both_heads(o_block)
            along = o_block.T.astype(F32) * o_in[:, rows]
            delta = jnp.concatenate([column_sum(along[:DH]), column_sum(along[DH:])], axis=1)
            scores = masked_scores(k_in[window, :], query, seg_col[window, :], row)
            probs = jnp.exp(scores - lse[0, pl.ds(b, 1), :])
            d_scores = (probs * (dot_nt(v_in[window, :], grad) - delta)).astype(LOW)
            dv[window, :] += dot_nn(probs.astype(LOW), grad)
            dk[window, :] += dot_nn(d_scores, query)
            d_query = own_heads(dot_nn(kt[:, window], d_scores)) * SCALE
            dq_out[rows, :] = d_query.T.astype(LOW)

        each_window(info, b, run)
        return 0

    lax.fori_loop(0, tokens // BLOCK, step, 0)
    dk_out[...] = dk[...].astype(LOW)
    dv_out[...] = dv[...].astype(LOW)
    bias_out[0:1, :] = column_sum(dq_out[...].astype(F32))
    bias_out[1:2, :] = column_sum(dv_out[...].astype(F32))
    grad = jnp.concatenate([dq_out[...], dk_out[...], dv_out[...]], axis=1)
    grad = dot_nn(x_t[...], grad)
    put_rows(grad, w_rows, me, 0, order, w_send, w_keep)


def attend_backward(info, n, query, key, value, parts, context, lse, seg, x_t, after):
    tokens, half = query.shape
    quarter, blocks, width = tokens // 4, tokens // BLOCK, x_t.shape[0]
    col = pl.BlockSpec((tokens, PAIR), lambda p, i: (0, n))
    pairs = half // PAIR
    part = pl.BlockSpec((quarter, PAIR), lambda p, i: (0, n))
    first = pl.BlockSpec((None, quarter, PAIR), lambda p, i: (0, 0, n))
    packed = quarter // 2
    low, high = [
        pl.BlockSpec((packed, PAIR), lambda p, i, at=at: (half // packed, at * pairs + n))
        for at in range(2)
    ]
    weight = (4, width // 8, 3 * PAIR)
    return pl.pallas_call(
        ordered(functools.partial(backward_kernel, QKV_ORDERS[n]), after),
        grid_spec=pltpu.PrefetchScalarGridSpec(
            num_scalar_prefetch=1,
            grid=(1,),
            in_specs=waiting(after)
            + [col] * 3
            + [part, low, high, first, part]
            + [pl.BlockSpec((PAIR, tokens), lambda p, i: (n, 0))]
            + [pl.BlockSpec((1, blocks, 2 * BLOCK), lambda p, i: (n, 0, 0))]
            + [full((1, tokens)), full((width, tokens))],
            out_specs=[full((tokens, PAIR))] * 3 + [full((2, PAIR))] + [full(weight)] * 2,
            scratch_shapes=[
                pltpu.VMEM((tokens, BLOCK), F32),
                pltpu.VMEM((tokens, PAIR), LOW),
                pltpu.VMEM((tokens, PAIR), LOW),
                pltpu.VMEM((PAIR, tokens), LOW),
                pltpu.VMEM((tokens, PAIR), F32),
                pltpu.VMEM((tokens, PAIR), F32),
                pltpu.VMEM((8, width // 8, 3 * PAIR), F32),
            ],
        ),
        out_shape=[shaped((tokens, PAIR), LOW)] * 3
        + [shaped((2, PAIR), F32), shaped(weight, LOW), shaped(weight, F32)],
        compiler_params=params(VMEM),
        cost_estimate=cost(8),
        name="attend_backward",
    )(info, *after, query, key, value, *parts, context, lse, seg, x_t)


def normalise(values):
    centred = values - jnp.mean(values, axis=1, keepdims=True)
    root = lax.rsqrt(jnp.mean(centred * centred, axis=1, keepdims=True) + EPS)
    return centred * root, root


def norm_back(grad, gain, normal, root):
    e = grad * gain
    along = jnp.mean(e * normal, axis=1, keepdims=True)
    return root * (e - jnp.mean(e, axis=1, keepdims=True) - normal * along)


def store_columns(place, flipped, mine, send):
    size, count = flipped.shape[0] // 4, flipped.shape[1]
    for b in range(4):
        rel = place ^ b

        @pl.when(rel % 2 == 0)
        def _():
            mine[pl.ds(rel // 2, 1)] = flipped[b * size : (b + 1) * size][None]

        @pl.when(rel % 2 == 1)
        def _():
            rows = pl.ds(pl.multiple_of(rel // 2 * size, size), size)
            send[rows, :count] = flipped[b * size : (b + 1) * size]


def middle_forward_kernel(
    info, p0, p1, p2, p3, x_in, cot, wo, bo, g1, s1, up, bup, down, bdown, g2, s2,
    out, d_res, n1, r1, turned, act, slope, mine, send, vec,
    hid, hid_low, branch,
):
    place, core, chip = info[0], info[1], info[2]
    step = pl.program_id(0)
    quarter = p0.shape[0]

    @pl.when(step == 0)
    def _():
        first = core == 0

        def sides(a, b):
            a, b = a[...], b[...]
            return jnp.concatenate([jnp.where(first, a, b), jnp.where(first, b, a)], axis=1)

        ctx = jnp.concatenate([sides(p0, p1), sides(p2, p3)], axis=0)
        turned[1] = ctx.T
        x = jnp.concatenate([x_in[chip], x_in[1 - chip]], axis=0).astype(F32)
        summed = x + dot_nn(ctx, wo[...]) + bo[...].astype(F32)
        normal, root = normalise(summed)
        n1[...] = normal
        r1[...] = root
        hidden = normal * g1[...].astype(F32) + s1[...].astype(F32)
        hid[...] = hidden
        low = hidden.astype(LOW)
        hid_low[...] = low
        turned[0] = low.T
        branch[...] = jnp.zeros_like(branch)

    pre = dot_nn(hid_low[...], up[...]) + bup[...].astype(F32)
    phi = 0.5 + 0.5 * lax.erf(pre * ROOT_HALF)
    low = (pre * phi).astype(LOW)
    act[...] = low
    slope[...] = phi + pre * (jnp.exp(-0.5 * pre * pre) * ROOT_TWO_PI)
    branch[...] += dot_nn(low, down[...])

    @pl.when(step == pl.num_programs(0) - 1)
    def _():
        normal, root = normalise(hid[...] + branch[...] + bdown[...].astype(F32))
        final = (normal * g2[...].astype(F32) + s2[...].astype(F32)).astype(LOW)
        out[pl.ds(chip, 1)] = final[:quarter][None]
        out[pl.ds(1 - chip, 1)] = final[quarter:][None]
        grad = jnp.concatenate([cot[chip], cot[1 - chip]], axis=0).astype(F32)
        back = norm_back(grad, g2[...].astype(F32), normal, root)
        d_res[...] = back
        vec[0:1, :] = column_sum(back)
        vec[1:2, :] = column_sum(grad * normal)
        vec[2:3, :] = column_sum(grad)
        store_columns(place, back.astype(LOW).T, mine, send)


def mark_kernel(*refs):
    refs[-1][...] = jnp.zeros_like(refs[-1])


def mark(*after):
    return pl.pallas_call(
        mark_kernel,
        grid=(1,),
        in_specs=waiting(after),
        out_specs=full((8, 128)),
        out_shape=shaped((8, 128), F32),
        compiler_params=params(VMEM),
        cost_estimate=cost(1),
        name="mark",
    )(*after)


def middle_forward(after, info, parts, inputs, cotangent, wo, bo, g1, s1, up, bup, down, bdown, g2, s2):
    quarter, half = parts[0].shape
    width, inner = 2 * half, up.shape[1]
    count, steps = 2 * quarter, 4
    chunk = inner // steps
    vector = full((1, width))
    tokens = full((count, width))
    turned = full((2, width // 4, count))
    return pl.pallas_call(
        ordered(middle_forward_kernel, after),
        grid_spec=pltpu.PrefetchScalarGridSpec(
            num_scalar_prefetch=1,
            grid=(steps,),
            in_specs=waiting(after)
            + [full((quarter, half))] * 4
            + [full((2, quarter, width))] * 2
            + [full((width, width)), vector, vector, vector]
            + [
                pl.BlockSpec((width, chunk), lambda c, i: (0, c)),
                pl.BlockSpec((1, chunk), lambda c, i: (0, c)),
                pl.BlockSpec((chunk, width), lambda c, i: (c, 0)),
            ]
            + [vector] * 3,
            out_specs=[full((2, quarter, width)), tokens, tokens, full((count, 1))]
            + [full((2, width, count))]
            + [pl.BlockSpec((count, chunk), lambda c, i: (0, c))] * 2
            + [turned, full((width // 2, count)), full((8, width))],
            scratch_shapes=[
                pltpu.VMEM((count, width), F32),
                pltpu.VMEM((count, width), LOW),
                pltpu.VMEM((count, width), F32),
            ],
        ),
        out_shape=[
            shaped((2, quarter, width), LOW),
            shaped((count, width), F32),
            shaped((count, width), F32),
            shaped((count, 1), F32),
            shaped((2, width, count), LOW),
            shaped((count, inner), LOW),
            shaped((count, inner), F32),
            shaped((2, width // 4, count), LOW),
            shaped((width // 2, count), LOW),
            shaped((8, width), F32),
        ],
        compiler_params=params(VMEM),
        cost_estimate=cost(18),
        name="middle_forward",
    )(
        info, *after, *parts, inputs, cotangent, wo, bo[None], g1[None], s1[None],
        up, bup[None], down, bdown[None], g2[None], s2[None],
    )


def middle_backward_kernel(
    info, d_res, slope, down, up, wo, n1, r1, g1,
    to_core, mine_pre, d_up_bias, d_summed, q0, to_chip, mine, vec,
    d_branch, d_hidden,
):
    place, core = info[0], info[1]
    step = pl.program_id(0)
    quarter = q0.shape[0]
    half = q0.shape[1]
    count = d_res.shape[0]

    @pl.when(step == 0)
    def _():
        d_branch[...] = d_res[...].astype(LOW)
        d_hidden[...] = d_res[...]

    d_pre = (dot_nt(d_branch[...], down[...]) * slope[...]).astype(LOW)
    d_up_bias[...] = column_sum(d_pre.astype(F32))
    d_hidden[...] += dot_nt(d_pre, up[...])

    @pl.when(step < 2)
    def _():
        at = pl.multiple_of((1 + step) * count, count)
        to_core[pl.ds(at, count), :] = d_pre

    @pl.when(step >= 2)
    def _():
        mine_pre[0] = d_pre

    @pl.when(step == pl.num_programs(0) - 1)
    def _():
        grad = d_hidden[...]
        normal = n1[...]
        back = norm_back(grad, g1[...].astype(F32), normal, r1[...])
        d_summed[...] = back
        vec[0:1, :] = column_sum(back)
        vec[1:2, :] = column_sum(grad * normal)
        vec[2:3, :] = column_sum(grad)
        low = back.astype(LOW)
        store_columns(place, low.T, mine, to_core)
        d_ctx = dot_nt(low, wo[...]).astype(LOW)
        first = core == 0
        left, right = d_ctx[:, :half], d_ctx[:, half:]
        same = jnp.where(first, left, right)
        other = jnp.where(first, right, left)
        q0[...] = same[:quarter]
        packed = quarter // 2
        to_core[half : half + packed, :] = jnp.concatenate(
            [other[:packed], other[packed:quarter]], axis=1
        )
        to_chip[0] = same[quarter:]
        to_chip[1] = other[quarter:]


def middle_backward(info, d_res, slope, down, up, wo, n1, r1, g1):
    count, width = d_res.shape
    inner, quarter, half = up.shape[1], count // 2, width // 2
    steps = 4
    chunk = inner // steps

    def block(c, i):
        return i[0] ^ (1 - c // 2 + 2 * (c % 2))

    tokens = full((count, width))
    turned = full((2, width // 4, count))
    return pl.pallas_call(
        middle_backward_kernel,
        grid_spec=pltpu.PrefetchScalarGridSpec(
            num_scalar_prefetch=1,
            grid=(steps,),
            in_specs=[
                tokens,
                pl.BlockSpec((count, chunk), lambda c, i: (0, block(c, i))),
                pl.BlockSpec((chunk, width), lambda c, i: (block(c, i), 0)),
                pl.BlockSpec((width, chunk), lambda c, i: (0, block(c, i))),
                full((width, width)),
                tokens,
                full((count, 1)),
                full((1, width)),
            ],
            out_specs=[
                full((3 * count, width)),
                pl.BlockSpec((1, count, chunk), lambda c, i: (jnp.maximum(c - 2, 0), 0, 0)),
                pl.BlockSpec((1, chunk), lambda c, i: (0, block(c, i))),
                tokens,
            ]
            + [full((quarter, half)), full((2, quarter, half)), turned, full((8, width))],
            scratch_shapes=[pltpu.VMEM((count, width), LOW), pltpu.VMEM((count, width), F32)],
        ),
        out_shape=[
            shaped((3 * count, width), LOW),
            shaped((2, count, chunk), LOW),
            shaped((1, inner), F32),
            shaped((count, width), F32),
        ]
        + [
            shaped((quarter, half), LOW),
            shaped((2, quarter, half), LOW),
            shaped((2, width // 4, count), LOW),
            shaped((8, width), F32),
        ],
        compiler_params=params(VMEM),
        cost_estimate=cost(16),
        name="middle_backward",
    )(info, d_res, slope, down, up, wo, n1, r1, g1[None])


DOWN_ORDERS = ("zxyw", "xzyw")


def down_kernel(info, mine, theirs, act, act_pair, *outs):
    rel = pl.program_id(0)
    left = jnp.concatenate([mine[0], mine[1]], axis=0)
    grad = dot_nn(left, act[...]) + dot_nn(theirs[...], act_pair[...])
    size = grad.shape[0] // 4
    for n, order in enumerate(DOWN_ORDERS):
        for flip in range(2):
            start = (2 * flip + n) * size
            put(grad[start : start + size], rel, flip, order, outs[2 * n], outs[2 * n + 1])


def down_grad(info, mine, theirs, act, act_pair, after):
    _, size, count = mine.shape
    block = act.shape[1] // 8
    part = (8, size // 2, block)
    spec = pl.BlockSpec((count, block), lambda r, i: (0, r ^ i[3]))
    return pl.pallas_call(
        ordered(down_kernel, after),
        grid_spec=pltpu.PrefetchScalarGridSpec(
            num_scalar_prefetch=1,
            grid=(8,),
            in_specs=waiting(after) + [full(mine.shape), full(theirs.shape), spec, spec],
            out_specs=[full(part)] * 4,
        ),
        out_shape=[shaped(part, LOW), shaped(part, F32)] * 2,
        compiler_params=params(VMEM),
        cost_estimate=cost(8),
        name="down_grad",
    )(info, *after, mine, theirs, act, act_pair)


UP_ORDERS = ("xyzw", "yxzw")


def up_kernel(
    info, left, left_pair, mine, theirs, mine_d, theirs_d, send_a, keep_a, send_b, keep_b, rows
):
    me = info[3]
    step = pl.program_id(0)

    @pl.when(step < 4)
    def _():
        grad = dot_nn(left[0], mine[0]) + dot_nn(left_pair[0], theirs[...])
        for n, flip in ((0, 0), (1, 0), (0, 1), (1, 1)):

            @pl.when(step == 2 * flip + n)
            def _():
                send, keep = ((send_a, keep_a), (send_b, keep_b))[n]
                put_rows(grad, rows, me, flip, UP_ORDERS[n], send, keep)

    @pl.when(step == 4)
    def _():
        right = jnp.concatenate([mine_d[0], mine_d[1]], axis=0)
        grad = dot_nt(left[1], right) + dot_nt(left_pair[1], theirs_d[...])
        deep, wide = grad.shape[0] // 8, grad.shape[1] // 2
        for b in range(8):
            rows[b] = grad[b * deep : (b + 1) * deep]
        for rel in range(4):
            near, far = rows[me ^ rel], rows[me ^ (rel + 4)]
            for flip in range(2):
                cut = slice(flip * wide, (flip + 1) * wide)
                value = jnp.concatenate([near[:, cut], far[:, cut]], axis=1)
                index = 8 + 2 * flip + rel // 2
                if rel % 2:
                    send_b[index] = value.astype(LOW)
                else:
                    keep_b[index] = value


def up_grad(info, left, left_pair, mine, from_core, mine_d, after):
    _, width, count = left.shape
    half = width // 2

    def at(s):
        return jnp.minimum(s, 3)

    shapes = [
        shaped((lead, width // 8, half), dtype) for lead in (8, 12) for dtype in (LOW, F32)
    ]
    return pl.pallas_call(
        ordered(up_kernel, after),
        grid_spec=pltpu.PrefetchScalarGridSpec(
            num_scalar_prefetch=1,
            grid=(5,),
            in_specs=waiting(after)
            + [full(left.shape)] * 2
            + [
                pl.BlockSpec((1, count, half), lambda s, i: (at(s) // 2, 0, at(s) % 2)),
                pl.BlockSpec((count, half), lambda s, i: (1 + at(s) // 2, at(s) % 2)),
                full(mine_d.shape),
                pl.BlockSpec((half, count), lambda s, i: (0, 0)),
            ],
            out_specs=[full(shape.shape) for shape in shapes],
            scratch_shapes=[pltpu.VMEM((8, width // 8, half), F32)],
        ),
        out_shape=shapes,
        compiler_params=params(VMEM),
        cost_estimate=cost(10),
        name="up_grad",
    )(info, *after, left, left_pair, mine, from_core, mine_d, from_core)


def input_kernel(info, *refs):
    grads, weights, (keep, send) = refs[:9], refs[9:12], refs[12:]
    rel = pl.program_id(0)
    total = sum(
        dot_nt(jnp.concatenate([ref[...] for ref in grads[t::3]], axis=1), weights[t][...])
        for t in range(3)
    )

    @pl.when(rel < 2)
    def _():
        send[0] = total

    @pl.when(rel >= 2)
    def _():
        keep[0] = total


def input_part(info, grads, qkv_weight, after):
    tokens = grads[0].shape[0]
    width = qkv_weight.shape[0]
    quarter, half = tokens // 4, width // 2

    rows = pl.BlockSpec((quarter, PAIR), lambda c, i: (i[0] ^ (1 - c // 2 + 2 * (c % 2)), 0))

    def weight(t):
        return pl.BlockSpec((width, half), lambda c, i: (0, 2 * t + i[1]))

    return pl.pallas_call(
        ordered(input_kernel, after),
        grid_spec=pltpu.PrefetchScalarGridSpec(
            num_scalar_prefetch=1,
            grid=(4,),
            in_specs=waiting(after) + [rows] * 9 + [weight(0), weight(1), weight(2)],
            out_specs=[
                pl.BlockSpec((1, quarter, width), lambda c, i: (jnp.maximum(c - 2, 0), 0, 0)),
                pl.BlockSpec((1, quarter, width), lambda c, i: (jnp.minimum(c, 1), 0, 0)),
            ],
        ),
        out_shape=[shaped((2, quarter, width), F32)] * 2,
        compiler_params=params(VMEM),
        cost_estimate=cost(6),
        name="input_part",
    )(info, *after, *grads, qkv_weight, qkv_weight, qkv_weight)


UNITS = (((0, 1), (2, 3), (4,), (5,)), ((0,), (1,), (2, 3), (4, 5)))


def share_kernel(info, *refs):
    place, core = info[0], info[1]
    kept, got, (own, one, two, three) = refs[:3], refs[3:6], refs[6:]
    total = [kept[n][0] + got[n][0].astype(F32) for n in range(3)]
    units = []
    for t in range(3):
        part = jnp.concatenate([pair[:, t * PAIR : (t + 1) * PAIR] for pair in total], axis=1)
        units += jnp.split(part, 2, axis=1)
    for side in range(2):
        for target in range(4):
            for flip, ref in enumerate((own, one, two, three)):

                @pl.when(jnp.logical_and(core == side, place ^ target == flip))
                def _():
                    for n in range(2):
                        unit = units[UNITS[side][target][n % len(UNITS[side][target])]]
                        ref[n] = unit.astype(ref.dtype)


def share(info, kept, got):
    unit = (2, kept[0].shape[1], kept[0].shape[2] // 2)
    return pl.pallas_call(
        share_kernel,
        grid_spec=pltpu.PrefetchScalarGridSpec(
            num_scalar_prefetch=1,
            grid=(1,),
            in_specs=[full(kept[0].shape)] * 6,
            out_specs=[full(unit)] * 4,
        ),
        out_shape=[shaped(unit, F32)] + [shaped(unit, LOW)] * 3,
        compiler_params=params(VMEM),
        cost_estimate=cost(1),
        name="share",
    )(info, *kept, *got)


def gather_kernel(info, own, one, two, three, out):
    place = info[0]
    same = own[...] + two[...].astype(F32)
    other = one[...].astype(F32) + three[...].astype(F32)
    for target in range(4):

        @pl.when(place == target)
        def _():
            sides = (same, other) if target % 2 == 0 else (other, same)
            pieces = [
                (side_unit, sides[side][n])
                for side in range(2)
                for n, side_unit in enumerate(
                    unit % 2 + 4 * (unit // 2) + 2 * side for unit in UNITS[side][target]
                )
            ]
            pieces.sort(key=lambda piece: piece[0])
            out[...] = jnp.concatenate([piece[1] for piece in pieces], axis=1)


def gather(info, own, *others):
    shape = (own.shape[1], 3 * own.shape[2])
    return pl.pallas_call(
        gather_kernel,
        grid_spec=pltpu.PrefetchScalarGridSpec(
            num_scalar_prefetch=1,
            grid=(1,),
            in_specs=[full(own.shape)] * 4,
            out_specs=full(shape),
        ),
        out_shape=shaped(shape, F32),
        compiler_params=params(VMEM),
        cost_estimate=cost(1),
        name="gather",
    )(info, own, *others)


def turn_kernel(info, x0, x1, x2, x3, x_t):
    quarter = x0.shape[0]
    for j, ref in enumerate((x0, x1, x2, x3)):
        at = pl.multiple_of((info[0] ^ j) * quarter, quarter)
        x_t[:, pl.ds(at, quarter)] = ref[...].T


def turn(info, quarters):
    quarter, width = quarters[0].shape
    return pl.pallas_call(
        turn_kernel,
        grid_spec=pltpu.PrefetchScalarGridSpec(
            num_scalar_prefetch=1,
            grid=(1,),
            in_specs=[full((quarter, width))] * 4,
            out_specs=full((width, 4 * quarter)),
        ),
        out_shape=shaped((width, 4 * quarter), LOW),
        compiler_params=params(VMEM),
        cost_estimate=cost(1),
        name="turn",
    )(info, *quarters)


def body(
    inputs,
    segments,
    qkv_weight,
    query_bias,
    value_bias,
    out_weight,
    out_bias,
    norm1_gain,
    norm1_shift,
    up_weight,
    up_bias,
    down_weight,
    down_bias,
    norm2_gain,
    norm2_shift,
    cotangent,
):
    rows, quarter, width = inputs.shape
    half = width // 2
    seq_size = lax.axis_size("seq")
    batch_size = lax.axis_size("batch")
    fine = batch_size // 8
    place = lax.axis_index("seq")
    chip, core = place // 2, place % 2
    segment = lax.dynamic_index_in_dim(segments, chip, 0)
    info = jnp.stack([place, core, chip, lax.axis_index("batch") // fine]).astype(jnp.int32)
    info = jnp.concatenate([info] + windows(segment[0]))

    def over_seq(array, flip):
        return lax.ppermute(array, "seq", [(i, i ^ flip) for i in range(seq_size)])

    def over_batch(array, flip):
        return lax.ppermute(array, "batch", [(i, i ^ flip) for i in range(batch_size)])

    def swap(array, axis):
        if axis == "x":
            return over_seq(array, 2)
        return over_batch(array, fine << "yzw".index(axis))

    def pick(array, index, axis=0):
        return lax.dynamic_index_in_dim(array, index, axis, keepdims=False)

    def tie(*arrays):
        return lax.optimization_barrier(arrays)

    def launch(*messages):
        return [
            (order, segments, kept, swap(sent, order[0]))
            for order, segments, sent, kept in messages
        ]

    def land(after, flights, *routes):
        made, token = join(
            [flight[1:] for flight in flights], [route[1:] for route in routes], after
        )
        return [(route[0],) + new for route, new in zip(routes, made)], token

    def finish(grad):
        if fine > 1:
            groups = [[i * fine + j for j in range(fine)] for i in range(8)]
            grad = lax.psum_scatter(
                grad, "batch", scatter_dimension=0, axis_index_groups=groups, tiled=True
            )
        return grad

    own = pick(inputs, chip)
    far = over_seq(pick(inputs, 1 - chip), 2)
    near = over_seq(own, 1)
    across = over_seq(far, 1)
    quarters = (own, near, far, across)

    query, key, value, *parts, context, lse = attend_forward(
        info, quarters, qkv_weight, query_bias, value_bias, segment
    )
    parts = [parts[0]] + [over_seq(parts[j], j) for j in (1, 2, 3)]
    x_t = turn(info, quarters)

    outputs, d_res, n1, r1, turned, act, slope, mine, send, vec_two = middle_forward(
        [x_t], info, parts, inputs, cotangent, out_weight, out_bias, norm1_gain, norm1_shift,
        up_weight, up_bias, down_weight, down_bias, norm2_gain, norm2_shift,
    )
    pair = over_seq(turned, 1), over_seq(act, 1), over_seq(send, 1)
    back = middle_backward(
        info, d_res, slope, down_weight, up_weight, out_weight, n1, r1, norm1_gain
    )
    turned_pair, act_pair, theirs = pair
    to_core, mine_pre, d_up_bias, d_summed, q0, to_chip, mine_d, vec_one = back

    token = mark(turned_pair, act_pair, theirs, vec_one)
    to_core, to_chip, token = tie(to_core, to_chip, token)
    from_core, from_chip = over_seq(to_core, 1), over_seq(to_chip, 2)
    made = down_grad(info, mine, theirs, act, act_pair, [token])
    downs = launch(
        (DOWN_ORDERS[0], [8], made[0], made[1]), (DOWN_ORDERS[1], [8], made[2], made[3])
    )
    across = over_seq(from_chip[1], 1)
    made = up_grad(info, turned, turned_pair, mine_pre, from_core, mine_d, [made[1]])
    ups = launch((UP_ORDERS[0], [8], made[0], made[1]), (UP_ORDERS[1], [8, 4], made[2], made[3]))
    d_parts = (q0, from_core, from_core, from_chip, across)

    def piece(n, after):
        made = attend_backward(
            info, n, query, key, value, d_parts, context, lse, segment, x_t, after
        )
        return list(made)

    def opening(n, made, token):
        return QKV_ORDERS[n], [4], tie(made[4], token)[0], made[5]

    zero = piece(0, [made[1]])
    downs, token = land(
        zero[3:4], downs, (DOWN_ORDERS[0][1:], (0, 0)), (DOWN_ORDERS[1][1:], (1, 0))
    )
    *downs, first = launch(*downs, opening(0, zero, token))

    one = piece(1, [token])
    (up_a, up_b, down, first), token = land(
        one[3:4],
        ups + downs + [first],
        (UP_ORDERS[0][1:], (0, 0)),
        (UP_ORDERS[1][1:], (1, 0), (1, 1)),
        ("yw", (2, 0), (3, 0)),
        (QKV_ORDERS[0][1:], (4, 0)),
    )
    flights = launch(up_a, up_b, down, opening(1, one, token), first)

    two = piece(2, [token])
    (up, down, second, first), token = land(
        two[3:4],
        flights,
        ("zw", (0, 0), (1, 0), (1, 1)),
        ("w", (2, 0), (2, 1)),
        (QKV_ORDERS[1][1:], (3, 0)),
        ("w", (4, 0)),
    )
    grads = [*zero[:3], *one[:3], *two[:3]]
    flights = launch(opening(2, two, token), up, down, second)
    bias_part = jnp.concatenate([zero[3], one[3], tie(two[3], token)[0]], axis=1)
    bias_zero = jnp.zeros_like(bias_part)
    bias_part = jnp.where(
        core == 0,
        jnp.concatenate([bias_part, bias_zero], axis=1),
        jnp.concatenate([bias_zero, bias_part], axis=1),
    )
    vectors = jnp.concatenate([vec_one[:3], vec_two[:3], d_up_bias.reshape(-1, width), bias_part])
    vectors_got = over_seq(vectors, 1)

    keep, send = input_part(info, grads, qkv_weight, [token])
    (third, up, down, second), token = land(
        [keep],
        flights,
        (QKV_ORDERS[2][1:], (0, 0)),
        ("w", (1, 0), (1, 1), (1, 2)),
        ("", (2, 0), (2, 1)),
        ("w", (3, 0)),
    )
    out_total, down_total = up[3][2], down[3]
    third, up, first = launch(third, up, first)
    send, vectors_got, token = tie(send, vectors_got, token)
    vectors = vectors + vectors_got
    vectors_got = over_seq(vectors, 2)
    d_row_got = over_seq(send, 1)
    (third, up), token = land([token], [third, up], ("w", (0, 0)), ("", (1, 0), (1, 1)))
    up_total = up[3]
    d_row_got, vectors_got, second_sent, out_total, token = tie(
        d_row_got, vectors_got, second[2], out_total, token
    )
    third, second = launch(third, second[:2] + (second_sent, second[3]))
    wide = half // 2
    out_got = swap(out_total[:, wide:].astype(LOW), "w")
    vectors = vectors + vectors_got
    vectors = vectors + swap(vectors, "y")
    vectors_got = swap(vectors, "z")
    d_row = keep + d_row_got
    d_far = over_seq(d_row[1].astype(LOW), 2)
    third_got, vectors_got, d_far, out_got = tie(third[3], vectors_got, d_far, out_got)
    own, *others = share(
        info, (first[2], second[2], third[2]), (first[3], second[3], third_got)
    )
    qkv_total = gather(info, own, *[over_seq(other, 1 + j) for j, other in enumerate(others)])
    qkv_total = finish(qkv_total)
    vectors = vectors + vectors_got
    out_total = out_total[:, :wide] + out_got.astype(F32)
    out_total = finish(out_total)
    down_total = finish(down_total.reshape(wide, half).T)
    up_total = finish(jnp.concatenate([up_total[0], up_total[1]], axis=1))

    vectors = vectors + swap(vectors, "w")
    flip = 1
    while flip < fine:
        vectors = vectors + over_batch(vectors, flip)
        flip *= 2
    d_near = d_summed[:quarter] + d_row[0]
    d_far = d_summed[quarter:] + d_far.astype(F32)
    d_inputs = jnp.stack([jnp.where(chip == 0, d_near, d_far), jnp.where(chip == 0, d_far, d_near)])
    return (
        outputs,
        d_inputs,
        qkv_total,
        vectors[-2],
        vectors[-1],
        out_total,
        vectors[0],
        vectors[1],
        vectors[2],
        up_total,
        vectors[6:-2].reshape(-1),
        down_total,
        vectors[3],
        vectors[4],
        vectors[5],
    )


def solution(mesh):
    whole, split = P(), P("batch", "seq")
    tokens = P("batch", "seq", None)
    return jax.shard_map(
        body,
        mesh=mesh,
        in_specs=(tokens, P("batch", None)) + (whole,) * 13 + (tokens,),
        out_specs=(tokens, tokens, split, whole, whole, split)
        + (whole,) * 3
        + (split, whole, split)
        + (whole,) * 3,
        check_vma=False,
    )
```

```python
import functools

import jax
import jax.numpy as jnp
from jax import lax
from jax.experimental import pallas as pl
from jax.experimental.pallas import tpu as pltpu
from jax.sharding import PartitionSpec as P

DH = 64
EPS = 1e-05
NEG = -1000000000.0
F32 = jnp.float32
LOW = jnp.bfloat16
PAIR = 2 * DH
SCALE = DH**-0.5
BLOCK = 128
SIZES = (2, 3, 5, 6, 8)
VMEM = 18
ROOT_HALF = 0.5**0.5
ROOT_TWO_PI = 0.3989422804014327


def shaped(shape, dtype):
    return jax.ShapeDtypeStruct(shape, dtype)


def dot_nn(left, right):
    return jnp.dot(left, right, preferred_element_type=F32)


def dot_nt(left, right):
    return lax.dot_general(left, right, (((1,), (1,)), ((), ())), preferred_element_type=F32)


def params(mib):
    return pltpu.CompilerParams(vmem_limit_bytes=mib << 20, dimension_semantics=("arbitrary",))


def waiting(after):
    return [pl.BlockSpec(memory_space=pl.ANY)] * len(after)


def ordered(kernel, after):
    return lambda info, *refs: kernel(info, *refs[len(after) :])


def full(shape):
    return pl.BlockSpec(shape, lambda *_: (0,) * len(shape))


def cost(micros):
    return pl.CostEstimate(flops=int(micros * 0.6e9), transcendentals=0, bytes_accessed=0)


def column_sum(values):
    return jnp.sum(values, axis=0, keepdims=True)


def spot(rel, flip_x, order):
    bits = {"y": rel % 2, "z": (rel // 2) % 2, "w": rel // 4, "x": flip_x}
    index = 0
    for axis in order[1:]:
        index = index * 2 + bits[axis]
    return bits[order[0]], index


def put(value, rel, flip_x, order, send, keep):
    sent, index = spot(rel, flip_x, order)

    @pl.when(sent == 1)
    def _():
        send[pl.ds(index, 1)] = value.astype(LOW)[None]

    @pl.when(sent == 0)
    def _():
        keep[pl.ds(index, 1)] = value[None]


def put_rows(grad, rows, me, flip_x, order, send, keep):
    deep = grad.shape[0] // 8
    for b in range(8):
        rows[b] = grad[b * deep : (b + 1) * deep]
    for rel in range(8):
        sent, index = spot(rel, flip_x, order)
        value = rows[me ^ rel]
        if sent:
            send[index] = value.astype(LOW)
        else:
            keep[index] = value


def join_kernel(skip, segments, routes, *refs):
    refs = refs[skip:]
    ins, outs = refs[: 2 * len(segments)], list(refs[2 * len(segments) : -1])
    refs[-1][...] = jnp.zeros_like(refs[-1])
    for route in routes:
        send = outs.pop(0) if any(segments[m][n] > 1 for m, n in route) else None
        keep = outs.pop(0)
        sent = filled = 0
        for m, n in route:
            start, size = sum(segments[m][:n]), segments[m][n]
            total = ins[2 * m][start : start + size]
            total = total + ins[2 * m + 1][start : start + size].astype(F32)
            if size > 1:
                size //= 2
                send[sent : sent + size] = total[size:].astype(LOW)
                sent += size
            keep[filled : filled + size] = total[:size]
            filled += size


def join(messages, routes, after):
    segments = [list(message[0]) for message in messages]
    tail = messages[0][1].shape[1:]
    shapes, results = [], []
    for route in routes:
        sizes = [segments[m][n] for m, n in route]
        left = [size // 2 for size in sizes if size > 1]
        results.append(left)
        if left:
            shapes.append(shaped((sum(left),) + tail, LOW))
        shapes.append(shaped((sum(max(size // 2, 1) for size in sizes),) + tail, F32))
    operands = [array for message in messages for array in message[1:]]
    shapes.append(shaped((8, 128), F32))
    *arrays, token = pl.pallas_call(
        functools.partial(join_kernel, len(after), segments, routes),
        grid=(1,),
        in_specs=waiting(after) + [full(array.shape) for array in operands],
        out_specs=[full(shape.shape) for shape in shapes],
        out_shape=shapes,
        compiler_params=params(VMEM),
        cost_estimate=cost(1),
        name="join",
    )(*after, *operands)
    return [(left, arrays.pop(0) if left else None, arrays.pop(0)) for left in results], token


def each_window(info, block, run):
    start = pl.multiple_of(info[4 + block], BLOCK)
    kind = info[4 + (info.shape[0] - 4) // 2 + block]
    for n, size in enumerate(SIZES):

        @pl.when(kind == n)
        def _():
            run(pl.ds(start, size * BLOCK), size * BLOCK)


def windows(segment):
    tokens = segment.shape[0]
    rows = segment.reshape(tokens // BLOCK, BLOCK)
    first = jnp.sum((segment[None] < rows[:, :1]).astype(jnp.int32), axis=1) // BLOCK
    last = (jnp.sum((segment[None] <= rows[:, -1:]).astype(jnp.int32), axis=1) - 1) // BLOCK
    need = last - first + 1
    kind = sum((need > size).astype(jnp.int32) for size in SIZES[:-1])
    size = sum(
        jnp.where(kind == n, size, 0).astype(jnp.int32) for n, size in enumerate(SIZES)
    )
    return [jnp.minimum(first, tokens // BLOCK - size) * BLOCK, kind]


def both_heads(array):
    lane = lax.broadcasted_iota(jnp.int32, array.shape, 1)
    zero = jnp.zeros_like(array)
    return jnp.concatenate(
        [jnp.where(lane < DH, array, zero), jnp.where(lane < DH, zero, array)], axis=0
    )


def own_heads(turned):
    return jnp.concatenate([turned[:DH, :BLOCK], turned[DH:, BLOCK:]], axis=0)


def fill_segments(seg_row, seg_col):
    seg_col[...] = jnp.broadcast_to(seg_row[...].astype(F32), (BLOCK, seg_row.shape[1])).T


def masked_scores(key, query, seg_col, seg_row):
    same = seg_col == seg_row
    return jnp.where(jnp.concatenate([same, same], axis=1), dot_nt(key, query), NEG)


def forward_kernel(
    info, x0, x1, x2, x3, wq, wk, wv, bq, bv, seg_row,
    q_out, k_out, v_out, c0, c1, c2, c3, o_out, lse_out,
    xs, seg_col, qs, vt, ctx,
):
    place = info[0]
    tokens = xs.shape[0]
    quarter = tokens // 4

    @pl.when(pl.program_id(0) == 0)
    def _():
        for j, ref in enumerate((x0, x1, x2, x3)):
            xs[pl.ds(pl.multiple_of((place ^ j) * quarter, quarter), quarter), :] = ref[...]
        fill_segments(seg_row, seg_col)

    weights = jnp.concatenate([wq[...], wk[...], wv[...]], axis=1)
    projected = dot_nn(xs[...], weights)
    query = (projected[:, :PAIR] + bq[...].astype(F32)).astype(LOW)
    key = projected[:, PAIR : 2 * PAIR].astype(LOW)
    value = (projected[:, 2 * PAIR :] + bv[...].astype(F32)).astype(LOW)
    q_out[...] = query
    k_out[...] = key
    v_out[...] = value
    qs[...] = query * jnp.asarray(SCALE, LOW)
    vt[...] = value.T

    def step(b, _):
        start = pl.multiple_of(b * BLOCK, BLOCK)
        rows = pl.ds(start, BLOCK)

        def run(window, size):
            row = seg_row[:, rows].astype(F32)
            scores = masked_scores(k_out[window, :], both_heads(qs[rows, :]), seg_col[window, :], row)
            top = jnp.max(scores, axis=0, keepdims=True)
            expo = jnp.exp(scores - top)
            total = jnp.sum(expo, axis=0, keepdims=True)
            mixed = dot_nn(vt[:, window], expo.astype(LOW)) * (1.0 / total)
            lse_out[0, pl.ds(b, 1), :] = top + jnp.log(total)
            mixed = own_heads(mixed)
            o_out[:, rows] = mixed
            ctx[rows, :] = mixed.T.astype(LOW)

        each_window(info, b, run)
        return 0

    lax.fori_loop(0, tokens // BLOCK, step, 0)
    for j, ref in enumerate((c0, c1, c2, c3)):
        ref[...] = ctx[pl.ds(pl.multiple_of((place ^ j) * quarter, quarter), quarter), :]


def attend_forward(info, quarters, qkv_weight, query_bias, value_bias, seg):
    quarter, width = quarters[0].shape
    tokens, half = 4 * quarter, width // 2
    pairs = half // PAIR

    def weight_spec(t):
        return pl.BlockSpec((width, PAIR), lambda p, i: (0, (2 * t + i[1]) * pairs + p))

    def bias_spec():
        return pl.BlockSpec((1, PAIR), lambda p, i: (0, i[1] * pairs + p))

    col = pl.BlockSpec((tokens, PAIR), lambda p, i: (0, p))
    part = pl.BlockSpec((quarter, PAIR), lambda p, i: (0, p))
    blocks = tokens // BLOCK
    return pl.pallas_call(
        forward_kernel,
        grid_spec=pltpu.PrefetchScalarGridSpec(
            num_scalar_prefetch=1,
            grid=(pairs,),
            in_specs=[full((quarter, width))] * 4
            + [weight_spec(0), weight_spec(1), weight_spec(2), bias_spec(), bias_spec()]
            + [full((1, tokens))],
            out_specs=[col] * 3
            + [part] * 4
            + [pl.BlockSpec((PAIR, tokens), lambda p, i: (p, 0))]
            + [pl.BlockSpec((1, blocks, 2 * BLOCK), lambda p, i: (p, 0, 0))],
            scratch_shapes=[
                pltpu.VMEM((tokens, width), LOW),
                pltpu.VMEM((tokens, BLOCK), F32),
                pltpu.VMEM((tokens, PAIR), LOW),
                pltpu.VMEM((PAIR, tokens), LOW),
                pltpu.VMEM((tokens, PAIR), LOW),
            ],
        ),
        out_shape=[shaped((tokens, half), LOW)] * 3
        + [shaped((quarter, half), LOW)] * 4
        + [shaped((half, tokens), F32), shaped((pairs, blocks, 2 * BLOCK), F32)],
        compiler_params=params(VMEM),
        cost_estimate=cost(16),
        name="attend_forward",
    )(info, *quarters, qkv_weight, qkv_weight, qkv_weight, query_bias[None], value_bias[None], seg)


QKV_ORDERS = ("zyw", "zyw", "yzw")


def backward_kernel(
    n, info, q_in, k_in, v_in, o0, o1, o1b, o2, o3, o_in, lse, seg_row, x_t, vec,
    dq_out, dk_out, dv_out, vec_out, w_send, w_keep,
    seg_col, qs, do, kt, dk, dv, w_rows,
):
    place, core, me = info[0], info[1], info[3]
    tokens = q_in.shape[0]
    quarter = tokens // 4
    fill_segments(seg_row, seg_col)
    for j, ref in enumerate((o0, None, o2, o3)):
        if ref is None:
            at = pl.multiple_of((place ^ 1) * quarter, quarter)
            do[pl.ds(at, quarter // 2), :] = o1[...]
            do[pl.ds(at + quarter // 2, quarter // 2), :] = o1b[...]
            continue
        do[pl.ds(pl.multiple_of((place ^ j) * quarter, quarter), quarter), :] = ref[...]
    qs[...] = q_in[...] * jnp.asarray(SCALE, LOW)
    kt[...] = k_in[...].T
    dk[...] = jnp.zeros_like(dk)
    dv[...] = jnp.zeros_like(dv)

    def step(b, _):
        start = pl.multiple_of(b * BLOCK, BLOCK)
        rows = pl.ds(start, BLOCK)

        def run(window, size):
            row = seg_row[:, rows].astype(F32)
            o_block = do[rows, :]
            query, grad = both_heads(qs[rows, :]), both_heads(o_block)
            along = o_block.T.astype(F32) * o_in[:, rows]
            delta = jnp.concatenate([column_sum(along[:DH]), column_sum(along[DH:])], axis=1)
            scores = masked_scores(k_in[window, :], query, seg_col[window, :], row)
            probs = jnp.exp(scores - lse[0, pl.ds(b, 1), :])
            d_scores = (probs * (dot_nt(v_in[window, :], grad) - delta)).astype(LOW)
            dv[window, :] += dot_nn(probs.astype(LOW), grad)
            dk[window, :] += dot_nn(d_scores, query)
            d_query = own_heads(dot_nn(kt[:, window], d_scores)) * SCALE
            dq_out[rows, :] = d_query.T.astype(LOW)

        each_window(info, b, run)
        return 0

    lax.fori_loop(0, tokens // BLOCK, step, 0)
    dk_out[...] = dk[...].astype(LOW)
    dv_out[...] = dv[...].astype(LOW)
    vec_out[...] = vec[...]
    half = vec.shape[1] // 2
    for side in range(2):

        @pl.when(core == side)
        def _():
            cut = slice(side * half + n * PAIR, side * half + (n + 1) * PAIR)
            vec_out[10:11, cut] = column_sum(dq_out[...].astype(F32))
            vec_out[11:12, cut] = column_sum(dv_out[...].astype(F32))

    grad = jnp.concatenate([dq_out[...], dk_out[...], dv_out[...]], axis=1)
    grad = dot_nn(x_t[...], grad)
    put_rows(grad, w_rows, me, 0, QKV_ORDERS[n], w_send, w_keep)


def attend_backward(info, n, query, key, value, parts, context, lse, seg, x_t, vectors, after):
    tokens, half = query.shape
    quarter, blocks, width = tokens // 4, tokens // BLOCK, x_t.shape[0]
    col = pl.BlockSpec((tokens, PAIR), lambda p, i: (0, n))
    pairs = half // PAIR
    part = pl.BlockSpec((quarter, PAIR), lambda p, i: (0, n))
    first = pl.BlockSpec((None, quarter, PAIR), lambda p, i: (0, 0, n))
    packed = quarter // 2
    low, high = [
        pl.BlockSpec((packed, PAIR), lambda p, i, at=at: (half // packed, at * pairs + n))
        for at in range(2)
    ]
    weight = (4, width // 8, 3 * PAIR)
    dtypes = (LOW, F32)
    return pl.pallas_call(
        ordered(functools.partial(backward_kernel, n), after),
        grid_spec=pltpu.PrefetchScalarGridSpec(
            num_scalar_prefetch=1,
            grid=(1,),
            in_specs=waiting(after)
            + [col] * 3
            + [part, low, high, first, part]
            + [pl.BlockSpec((PAIR, tokens), lambda p, i: (n, 0))]
            + [pl.BlockSpec((1, blocks, 2 * BLOCK), lambda p, i: (n, 0, 0))]
            + [full((1, tokens)), full((width, tokens)), full(vectors.shape)],
            out_specs=[full((tokens, PAIR))] * 3
            + [full(vectors.shape)]
            + [full(weight)] * len(dtypes),
            scratch_shapes=[
                pltpu.VMEM((tokens, BLOCK), F32),
                pltpu.VMEM((tokens, PAIR), LOW),
                pltpu.VMEM((tokens, PAIR), LOW),
                pltpu.VMEM((PAIR, tokens), LOW),
                pltpu.VMEM((tokens, PAIR), F32),
                pltpu.VMEM((tokens, PAIR), F32),
                pltpu.VMEM((8, width // 8, 3 * PAIR), F32),
            ],
        ),
        out_shape=[shaped((tokens, PAIR), LOW)] * 3
        + [shaped(vectors.shape, F32)]
        + [shaped(weight, dtype) for dtype in dtypes],
        compiler_params=params(VMEM),
        cost_estimate=cost(8),
        name="attend_backward",
    )(info, *after, query, key, value, *parts, context, lse, seg, x_t, vectors)


def normalise(values):
    centred = values - jnp.mean(values, axis=1, keepdims=True)
    root = lax.rsqrt(jnp.mean(centred * centred, axis=1, keepdims=True) + EPS)
    return centred * root, root


def norm_back(grad, gain, normal, root):
    e = grad * gain
    along = jnp.mean(e * normal, axis=1, keepdims=True)
    return root * (e - jnp.mean(e, axis=1, keepdims=True) - normal * along)


def store_columns(place, flipped, mine, send):
    size, count = flipped.shape[0] // 4, flipped.shape[1]
    for b in range(4):
        rel = place ^ b

        @pl.when(rel % 2 == 0)
        def _():
            mine[pl.ds(rel // 2, 1)] = flipped[b * size : (b + 1) * size][None]

        @pl.when(rel % 2 == 1)
        def _():
            rows = pl.ds(pl.multiple_of(rel // 2 * size, size), size)
            send[rows, :count] = flipped[b * size : (b + 1) * size]


def middle_forward_kernel(
    info, p0, p1, p2, p3, x_in, cot, wo, bo, g1, s1, up, bup, down, bdown, g2, s2,
    out, d_res, n1, r1, turned, act, slope, mine, send, vec,
    hid, hid_low, branch,
):
    place, core, chip = info[0], info[1], info[2]
    step = pl.program_id(0)
    quarter = p0.shape[0]

    @pl.when(step == 0)
    def _():
        first = core == 0

        def sides(a, b):
            a, b = a[...], b[...]
            return jnp.concatenate([jnp.where(first, a, b), jnp.where(first, b, a)], axis=1)

        ctx = jnp.concatenate([sides(p0, p1), sides(p2, p3)], axis=0)
        turned[1] = ctx.T
        x = jnp.concatenate([x_in[chip], x_in[1 - chip]], axis=0).astype(F32)
        summed = x + dot_nn(ctx, wo[...]) + bo[...].astype(F32)
        normal, root = normalise(summed)
        n1[...] = normal
        r1[...] = root
        hidden = normal * g1[...].astype(F32) + s1[...].astype(F32)
        hid[...] = hidden
        low = hidden.astype(LOW)
        hid_low[...] = low
        turned[0] = low.T
        branch[...] = jnp.zeros_like(branch)

    pre = dot_nn(hid_low[...], up[...]) + bup[...].astype(F32)
    phi = 0.5 + 0.5 * lax.erf(pre * ROOT_HALF)
    low = (pre * phi).astype(LOW)
    act[...] = low
    slope[...] = phi + pre * (jnp.exp(-0.5 * pre * pre) * ROOT_TWO_PI)
    branch[...] += dot_nn(low, down[...])

    @pl.when(step == pl.num_programs(0) - 1)
    def _():
        normal, root = normalise(hid[...] + branch[...] + bdown[...].astype(F32))
        final = (normal * g2[...].astype(F32) + s2[...].astype(F32)).astype(LOW)
        out[pl.ds(chip, 1)] = final[:quarter][None]
        out[pl.ds(1 - chip, 1)] = final[quarter:][None]
        grad = jnp.concatenate([cot[chip], cot[1 - chip]], axis=0).astype(F32)
        back = norm_back(grad, g2[...].astype(F32), normal, root)
        d_res[...] = back
        vec[0:1, :] = column_sum(back)
        vec[1:2, :] = column_sum(grad * normal)
        vec[2:3, :] = column_sum(grad)
        store_columns(place, back.astype(LOW).T, mine, send)


def mark_kernel(*refs):
    refs[-1][...] = jnp.zeros_like(refs[-1])


def mark(*after):
    return pl.pallas_call(
        mark_kernel,
        grid=(1,),
        in_specs=waiting(after),
        out_specs=full((8, 128)),
        out_shape=shaped((8, 128), F32),
        compiler_params=params(VMEM),
        cost_estimate=cost(1),
        name="mark",
    )(*after)


def middle_forward(after, info, parts, inputs, cotangent, wo, bo, g1, s1, up, bup, down, bdown, g2, s2):
    quarter, half = parts[0].shape
    width, inner = 2 * half, up.shape[1]
    count, steps = 2 * quarter, 4
    chunk = inner // steps
    vector = full((1, width))
    tokens = full((count, width))
    turned = full((2, width // 4, count))
    return pl.pallas_call(
        ordered(middle_forward_kernel, after),
        grid_spec=pltpu.PrefetchScalarGridSpec(
            num_scalar_prefetch=1,
            grid=(steps,),
            in_specs=waiting(after)
            + [full((quarter, half))] * 4
            + [full((2, quarter, width))] * 2
            + [full((width, width)), vector, vector, vector]
            + [
                pl.BlockSpec((width, chunk), lambda c, i: (0, c)),
                pl.BlockSpec((1, chunk), lambda c, i: (0, c)),
                pl.BlockSpec((chunk, width), lambda c, i: (c, 0)),
            ]
            + [vector] * 3,
            out_specs=[full((2, quarter, width)), tokens, tokens, full((count, 1))]
            + [full((2, width, count))]
            + [pl.BlockSpec((count, chunk), lambda c, i: (0, c))] * 2
            + [turned, full((width // 2, count)), full((8, width))],
            scratch_shapes=[
                pltpu.VMEM((count, width), F32),
                pltpu.VMEM((count, width), LOW),
                pltpu.VMEM((count, width), F32),
            ],
        ),
        out_shape=[
            shaped((2, quarter, width), LOW),
            shaped((count, width), F32),
            shaped((count, width), F32),
            shaped((count, 1), F32),
            shaped((2, width, count), LOW),
            shaped((count, inner), LOW),
            shaped((count, inner), F32),
            shaped((2, width // 4, count), LOW),
            shaped((width // 2, count), LOW),
            shaped((8, width), F32),
        ],
        compiler_params=params(VMEM),
        cost_estimate=cost(18),
        name="middle_forward",
    )(
        info, *after, *parts, inputs, cotangent, wo, bo[None], g1[None], s1[None],
        up, bup[None], down, bdown[None], g2[None], s2[None],
    )


def middle_backward_kernel(
    info, d_res, slope, down, up, wo, n1, r1, g1, vec_two,
    to_core, mine_pre, d_summed, q0, to_chip, mine, vec,
    d_branch, d_hidden,
):
    place, core = info[0], info[1]
    step = pl.program_id(0)
    quarter = q0.shape[0]
    half = q0.shape[1]
    count = d_res.shape[0]

    @pl.when(step == 0)
    def _():
        d_branch[...] = d_res[...].astype(LOW)
        d_hidden[...] = d_res[...]

    d_pre = (dot_nt(d_branch[...], down[...]) * slope[...]).astype(LOW)
    block = place ^ (1 - step // 2 + 2 * (step % 2))
    vec[pl.ds(6 + block, 1), :] = column_sum(d_pre.astype(F32))
    d_hidden[...] += dot_nt(d_pre, up[...])

    @pl.when(step < 2)
    def _():
        at = pl.multiple_of((1 + step) * count, count)
        to_core[pl.ds(at, count), :] = d_pre

    @pl.when(step >= 2)
    def _():
        mine_pre[0] = d_pre

    @pl.when(step == pl.num_programs(0) - 1)
    def _():
        grad = d_hidden[...]
        normal = n1[...]
        back = norm_back(grad, g1[...].astype(F32), normal, r1[...])
        d_summed[...] = back
        vec[3:6, :] = vec_two[0:3, :]
        vec[10:16, :] = jnp.zeros_like(vec[10:16, :])
        vec[0:1, :] = column_sum(back)
        vec[1:2, :] = column_sum(grad * normal)
        vec[2:3, :] = column_sum(grad)
        low = back.astype(LOW)
        store_columns(place, low.T, mine, to_core)
        d_ctx = dot_nt(low, wo[...]).astype(LOW)
        first = core == 0
        left, right = d_ctx[:, :half], d_ctx[:, half:]
        same = jnp.where(first, left, right)
        other = jnp.where(first, right, left)
        q0[...] = same[:quarter]
        packed = quarter // 2
        to_core[half : half + packed, :] = jnp.concatenate(
            [other[:packed], other[packed:quarter]], axis=1
        )
        to_chip[0] = same[quarter:]
        to_chip[1] = other[quarter:]


def middle_backward(info, d_res, slope, down, up, wo, n1, r1, g1, vec_two):
    count, width = d_res.shape
    inner, quarter, half = up.shape[1], count // 2, width // 2
    steps = 4
    chunk = inner // steps

    def block(c, i):
        return i[0] ^ (1 - c // 2 + 2 * (c % 2))

    tokens = full((count, width))
    turned = full((2, width // 4, count))
    return pl.pallas_call(
        middle_backward_kernel,
        grid_spec=pltpu.PrefetchScalarGridSpec(
            num_scalar_prefetch=1,
            grid=(steps,),
            in_specs=[
                tokens,
                pl.BlockSpec((count, chunk), lambda c, i: (0, block(c, i))),
                pl.BlockSpec((chunk, width), lambda c, i: (block(c, i), 0)),
                pl.BlockSpec((width, chunk), lambda c, i: (0, block(c, i))),
                full((width, width)),
                tokens,
                full((count, 1)),
                full((1, width)),
                full(vec_two.shape),
            ],
            out_specs=[
                full((3 * count, width)),
                pl.BlockSpec((1, count, chunk), lambda c, i: (jnp.maximum(c - 2, 0), 0, 0)),
                tokens,
            ]
            + [full((quarter, half)), full((2, quarter, half)), turned, full((16, width))],
            scratch_shapes=[pltpu.VMEM((count, width), LOW), pltpu.VMEM((count, width), F32)],
        ),
        out_shape=[
            shaped((3 * count, width), LOW),
            shaped((2, count, chunk), LOW),
            shaped((count, width), F32),
        ]
        + [
            shaped((quarter, half), LOW),
            shaped((2, quarter, half), LOW),
            shaped((2, width // 4, count), LOW),
            shaped((16, width), F32),
        ],
        compiler_params=params(VMEM),
        cost_estimate=cost(16),
        name="middle_backward",
    )(info, d_res, slope, down, up, wo, n1, r1, g1[None], vec_two)


DOWN_ORDERS = ("zxwy", "xzwy")


def down_kernel(info, mine, theirs, act, act_pair, *outs):
    rel = pl.program_id(0)
    left = jnp.concatenate([mine[0], mine[1]], axis=0)
    grad = dot_nn(left, act[...]) + dot_nn(theirs[...], act_pair[...])
    size = grad.shape[0] // 4
    for n, order in enumerate(DOWN_ORDERS):
        for flip in range(2):
            start = (2 * flip + n) * size
            put(grad[start : start + size], rel, flip, order, outs[2 * n], outs[2 * n + 1])


def down_grad(info, mine, theirs, act, act_pair, after):
    _, size, count = mine.shape
    block = act.shape[1] // 8
    part = (8, size // 2, block)
    spec = pl.BlockSpec((count, block), lambda r, i: (0, r ^ i[3]))
    return pl.pallas_call(
        ordered(down_kernel, after),
        grid_spec=pltpu.PrefetchScalarGridSpec(
            num_scalar_prefetch=1,
            grid=(8,),
            in_specs=waiting(after) + [full(mine.shape), full(theirs.shape), spec, spec],
            out_specs=[full(part)] * 4,
        ),
        out_shape=[shaped(part, LOW), shaped(part, F32)] * 2,
        compiler_params=params(VMEM),
        cost_estimate=cost(8),
        name="down_grad",
    )(info, *after, mine, theirs, act, act_pair)


UP_ORDERS = ("xyzw", "yxzw")


def up_kernel(
    info, left, left_pair, mine, theirs, mine_d, theirs_d, send_a, keep_a, send_b, keep_b, rows
):
    me = info[3]
    step = pl.program_id(0)

    @pl.when(step < 4)
    def _():
        grad = dot_nn(left[0], mine[0]) + dot_nn(left_pair[0], theirs[...])
        for n, flip in ((0, 0), (1, 0), (0, 1), (1, 1)):

            @pl.when(step == 2 * flip + n)
            def _():
                send, keep = ((send_a, keep_a), (send_b, keep_b))[n]
                put_rows(grad, rows, me, flip, UP_ORDERS[n], send, keep)

    @pl.when(step == 4)
    def _():
        right = jnp.concatenate([mine_d[0], mine_d[1]], axis=0)
        grad = dot_nt(left[1], right) + dot_nt(left_pair[1], theirs_d[...])
        deep, wide = grad.shape[0] // 8, grad.shape[1] // 2
        for b in range(8):
            rows[b] = grad[b * deep : (b + 1) * deep]
        for rel in range(4):
            near, far = rows[me ^ rel], rows[me ^ (rel + 4)]
            for flip in range(2):
                cut = slice(flip * wide, (flip + 1) * wide)
                value = jnp.concatenate([near[:, cut], far[:, cut]], axis=1)
                index = 8 + 2 * flip + rel // 2
                if rel % 2:
                    send_b[index] = value.astype(LOW)
                else:
                    keep_b[index] = value


def up_grad(info, left, left_pair, mine, from_core, mine_d, after):
    _, width, count = left.shape
    half = width // 2

    def at(s):
        return jnp.minimum(s, 3)

    shapes = [
        shaped((lead, width // 8, half), dtype) for lead in (8, 12) for dtype in (LOW, F32)
    ]
    return pl.pallas_call(
        ordered(up_kernel, after),
        grid_spec=pltpu.PrefetchScalarGridSpec(
            num_scalar_prefetch=1,
            grid=(5,),
            in_specs=waiting(after)
            + [full(left.shape)] * 2
            + [
                pl.BlockSpec((1, count, half), lambda s, i: (at(s) // 2, 0, at(s) % 2)),
                pl.BlockSpec((count, half), lambda s, i: (1 + at(s) // 2, at(s) % 2)),
                full(mine_d.shape),
                pl.BlockSpec((half, count), lambda s, i: (0, 0)),
            ],
            out_specs=[full(shape.shape) for shape in shapes],
            scratch_shapes=[pltpu.VMEM((8, width // 8, half), F32)],
        ),
        out_shape=shapes,
        compiler_params=params(VMEM),
        cost_estimate=cost(10),
        name="up_grad",
    )(info, *after, left, left_pair, mine, from_core, mine_d, from_core)


def input_kernel(info, *refs):
    grads, weights, (keep, send) = refs[:9], refs[9:12], refs[12:]
    rel = pl.program_id(0)
    total = sum(
        dot_nt(jnp.concatenate([ref[...] for ref in grads[t::3]], axis=1), weights[t][...])
        for t in range(3)
    )

    @pl.when(rel < 2)
    def _():
        send[0] = total

    @pl.when(rel >= 2)
    def _():
        keep[0] = total


def input_part(info, grads, qkv_weight, after):
    tokens = grads[0].shape[0]
    width = qkv_weight.shape[0]
    quarter, half = tokens // 4, width // 2

    rows = pl.BlockSpec((quarter, PAIR), lambda c, i: (i[0] ^ (1 - c // 2 + 2 * (c % 2)), 0))

    def weight(t):
        return pl.BlockSpec((width, half), lambda c, i: (0, 2 * t + i[1]))

    return pl.pallas_call(
        ordered(input_kernel, after),
        grid_spec=pltpu.PrefetchScalarGridSpec(
            num_scalar_prefetch=1,
            grid=(4,),
            in_specs=waiting(after) + [rows] * 9 + [weight(0), weight(1), weight(2)],
            out_specs=[
                pl.BlockSpec((1, quarter, width), lambda c, i: (jnp.maximum(c - 2, 0), 0, 0)),
                pl.BlockSpec((1, quarter, width), lambda c, i: (jnp.minimum(c, 1), 0, 0)),
            ],
        ),
        out_shape=[shaped((2, quarter, width), F32)] * 2,
        compiler_params=params(VMEM),
        cost_estimate=cost(6),
        name="input_part",
    )(info, *after, *grads, qkv_weight, qkv_weight, qkv_weight)


UNITS = (((0, 1), (2, 3), (4,), (5,)), ((0,), (1,), (2, 3), (4, 5)))


def share_kernel(info, zero, first, kept, got, own, one, two, three):
    place, core = info[0], info[1]
    total = [zero[zero.shape[0] - 1], first[first.shape[0] - 1], kept[0] + got[0].astype(F32)]
    units = []
    for t in range(3):
        part = jnp.concatenate([pair[:, t * PAIR : (t + 1) * PAIR] for pair in total], axis=1)
        units += jnp.split(part, 2, axis=1)
    for side in range(2):
        for target in range(4):
            for flip, ref in enumerate((own, one, two, three)):

                @pl.when(jnp.logical_and(core == side, place ^ target == flip))
                def _():
                    for n in range(2):
                        unit = units[UNITS[side][target][n % len(UNITS[side][target])]]
                        ref[n] = unit.astype(ref.dtype)


def share(info, zero, one, kept, got, after):
    unit = (2, got.shape[1], got.shape[2] // 2)
    return pl.pallas_call(
        ordered(share_kernel, after),
        grid_spec=pltpu.PrefetchScalarGridSpec(
            num_scalar_prefetch=1,
            grid=(1,),
            in_specs=waiting(after)
            + [full(array.shape) for array in (zero, one, kept, got)],
            out_specs=[full(unit)] * 4,
        ),
        out_shape=[shaped(unit, F32)] + [shaped(unit, LOW)] * 3,
        compiler_params=params(VMEM),
        cost_estimate=cost(1),
        name="share",
    )(info, *after, zero, one, kept, got)


def gather_kernel(info, own, one, two, three, out):
    place = info[0]
    same = own[...] + two[...].astype(F32)
    other = one[...].astype(F32) + three[...].astype(F32)
    for target in range(4):

        @pl.when(place == target)
        def _():
            sides = (same, other) if target % 2 == 0 else (other, same)
            pieces = [
                (side_unit, sides[side][n])
                for side in range(2)
                for n, side_unit in enumerate(
                    unit % 2 + 4 * (unit // 2) + 2 * side for unit in UNITS[side][target]
                )
            ]
            pieces.sort(key=lambda piece: piece[0])
            out[...] = jnp.concatenate([piece[1] for piece in pieces], axis=1)


def gather(info, own, *others):
    shape = (own.shape[1], 3 * own.shape[2])
    return pl.pallas_call(
        gather_kernel,
        grid_spec=pltpu.PrefetchScalarGridSpec(
            num_scalar_prefetch=1,
            grid=(1,),
            in_specs=[full(own.shape)] * 4,
            out_specs=full(shape),
        ),
        out_shape=shaped(shape, F32),
        compiler_params=params(VMEM),
        cost_estimate=cost(1),
        name="gather",
    )(info, own, *others)


def turn_kernel(info, x0, x1, x2, x3, x_t):
    quarter = x0.shape[0]
    for j, ref in enumerate((x0, x1, x2, x3)):
        at = pl.multiple_of((info[0] ^ j) * quarter, quarter)
        x_t[:, pl.ds(at, quarter)] = ref[...].T


def turn(info, quarters):
    quarter, width = quarters[0].shape
    return pl.pallas_call(
        turn_kernel,
        grid_spec=pltpu.PrefetchScalarGridSpec(
            num_scalar_prefetch=1,
            grid=(1,),
            in_specs=[full((quarter, width))] * 4,
            out_specs=full((width, 4 * quarter)),
        ),
        out_shape=shaped((width, 4 * quarter), LOW),
        compiler_params=params(VMEM),
        cost_estimate=cost(1),
        name="turn",
    )(info, *quarters)


def body(
    inputs,
    segments,
    qkv_weight,
    query_bias,
    value_bias,
    out_weight,
    out_bias,
    norm1_gain,
    norm1_shift,
    up_weight,
    up_bias,
    down_weight,
    down_bias,
    norm2_gain,
    norm2_shift,
    cotangent,
):
    rows, quarter, width = inputs.shape
    half = width // 2
    seq_size = lax.axis_size("seq")
    batch_size = lax.axis_size("batch")
    fine = batch_size // 8
    place = lax.axis_index("seq")
    chip, core = place // 2, place % 2
    segment = lax.dynamic_index_in_dim(segments, chip, 0)
    info = jnp.stack([place, core, chip, lax.axis_index("batch") // fine]).astype(jnp.int32)
    info = jnp.concatenate([info] + windows(segment[0]))

    def over_seq(array, flip):
        return lax.ppermute(array, "seq", [(i, i ^ flip) for i in range(seq_size)])

    def over_batch(array, flip):
        return lax.ppermute(array, "batch", [(i, i ^ flip) for i in range(batch_size)])

    def swap(array, axis):
        if axis == "x":
            return over_seq(array, 2)
        return over_batch(array, fine << "yzw".index(axis))

    def pick(array, index, axis=0):
        return lax.dynamic_index_in_dim(array, index, axis, keepdims=False)

    def tie(*arrays):
        return lax.optimization_barrier(arrays)

    def launch(*messages):
        return [
            (order, segments, kept, swap(sent, order[0]))
            for order, segments, sent, kept in messages
        ]

    def land(after, flights, *routes):
        made, token = join(
            [flight[1:] for flight in flights], [route[1:] for route in routes], after
        )
        return [(route[0],) + new for route, new in zip(routes, made)], token

    def finish(grad):
        if fine > 1:
            groups = [[i * fine + j for j in range(fine)] for i in range(8)]
            grad = lax.psum_scatter(
                grad, "batch", scatter_dimension=0, axis_index_groups=groups, tiled=True
            )
        return grad

    own = pick(inputs, chip)
    far = over_seq(pick(inputs, 1 - chip), 2)
    near = over_seq(own, 1)
    across = over_seq(far, 1)
    quarters = (own, near, far, across)

    query, key, value, *parts, context, lse = attend_forward(
        info, quarters, qkv_weight, query_bias, value_bias, segment
    )
    parts = [parts[0]] + [over_seq(parts[j], j) for j in (1, 2, 3)]
    x_t = turn(info, quarters)

    outputs, d_res, n1, r1, turned, act, slope, mine, send, vec_two = middle_forward(
        [x_t], info, parts, inputs, cotangent, out_weight, out_bias, norm1_gain, norm1_shift,
        up_weight, up_bias, down_weight, down_bias, norm2_gain, norm2_shift,
    )
    pair = over_seq(turned, 1), over_seq(act, 1), over_seq(send, 1)
    back = middle_backward(
        info, d_res, slope, down_weight, up_weight, out_weight, n1, r1, norm1_gain, vec_two
    )
    turned_pair, act_pair, theirs = pair
    to_core, mine_pre, d_summed, q0, to_chip, mine_d, vectors = back

    token = mark(turned_pair, act_pair, theirs, vectors)
    to_core, to_chip, token = tie(to_core, to_chip, token)
    from_core, from_chip = over_seq(to_core, 1), over_seq(to_chip, 2)
    made = down_grad(info, mine, theirs, act, act_pair, [token])
    downs = launch(
        (DOWN_ORDERS[0], [8], made[0], made[1]), (DOWN_ORDERS[1], [8], made[2], made[3])
    )
    across = over_seq(from_chip[1], 1)
    made = up_grad(info, turned, turned_pair, mine_pre, from_core, mine_d, [made[1]])
    ups = launch((UP_ORDERS[0], [8], made[0], made[1]), (UP_ORDERS[1], [8, 4], made[2], made[3]))
    d_parts = (q0, from_core, from_core, from_chip, across)

    def piece(n, vectors, after):
        made = attend_backward(
            info, n, query, key, value, d_parts, context, lse, segment, x_t, vectors, after
        )
        return list(made)

    def opening(n, made, token):
        sent, token = tie(made[4], token)
        return (QKV_ORDERS[n], [4], sent, made[5]), token

    zero = piece(0, vectors, [made[1]])
    downs, token = land(
        zero[3:4], downs, (DOWN_ORDERS[0][1:], (0, 0)), (DOWN_ORDERS[1][1:], (1, 0))
    )
    opened, token = opening(0, zero, token)
    *downs, first = launch(*downs, opened)

    one = piece(1, zero[3], [token])
    (up_a, up_b, down), token = land(
        one[3:4],
        ups + downs + [first],
        (UP_ORDERS[0][1:], (0, 0), (4, 0)),
        (UP_ORDERS[1][1:], (1, 0), (1, 1)),
        ("wy", (2, 0), (3, 0)),
    )
    opened, token = opening(1, one, token)
    flights = launch(up_a, up_b, down, opened)

    two = piece(2, one[3], [token])
    (up, first, down), token = land(
        two[3:4],
        flights,
        ("zw", (0, 0), (1, 0), (1, 1)),
        ("w", (0, 1)),
        ("y", (2, 0), (2, 1), (3, 0)),
    )
    grads = [*zero[:3], *one[:3], *two[:3]]
    opened, token = opening(2, two, token)
    vectors, token = tie(two[3], token)
    flights = launch(opened, up, first, down)
    vectors_got = over_seq(vectors, 1)

    keep, send = input_part(info, grads, qkv_weight, [token])
    (third, up, down), token = land(
        [keep],
        flights,
        (QKV_ORDERS[2][1:], (0, 0)),
        ("w", (1, 0), (1, 1), (3, 2), (1, 2)),
        ("", (3, 0), (3, 1), (2, 0)),
    )
    down_total, out_total = down[3], up[3][3]
    third, up = launch(third, up)
    send, vectors_got, token = tie(send, vectors_got, token)
    d_row = keep + over_seq(send, 1)
    d_far = over_seq(d_row[1].astype(LOW), 2)
    vectors = vectors + vectors_got
    vectors = vectors + over_seq(vectors, 2)
    vectors = vectors + swap(vectors, "y")
    (third, up), token = land([token, vectors], [third, up], ("w", (0, 0)), ("", (1, 0), (1, 1), (1, 2)))
    up_total = up[3]
    vectors, out_total, token = tie(vectors, out_total, token)
    (third,) = launch(third)
    wide = half // 2
    out_got = swap(out_total[:, wide:].astype(LOW), "w")
    vectors_got = swap(vectors, "z")
    own, *others = share(info, down[3], up[3], third[2], third[3], [token, vectors_got, d_far])
    vectors_got, own = tie(vectors_got, own)
    vectors = vectors + vectors_got
    qkv_total = gather(info, own, *[over_seq(other, 1 + j) for j, other in enumerate(others)])
    qkv_total = finish(qkv_total)
    out_total = out_total[:, :wide] + out_got.astype(F32)
    out_total = finish(out_total)
    down_total = finish(down_total[:2].reshape(wide, half).T)
    up_total = finish(jnp.concatenate([up_total[0], up_total[1]], axis=1))

    vectors = vectors + swap(vectors, "w")
    flip = 1
    while flip < fine:
        vectors = vectors + over_batch(vectors, flip)
        flip *= 2
    d_near = d_summed[:quarter] + d_row[0]
    d_far = d_summed[quarter:] + d_far.astype(F32)
    d_inputs = jnp.stack([jnp.where(chip == 0, d_near, d_far), jnp.where(chip == 0, d_far, d_near)])
    return (
        outputs,
        d_inputs,
        qkv_total,
        vectors[10],
        vectors[11],
        out_total,
        vectors[0],
        vectors[1],
        vectors[2],
        up_total,
        vectors[6:10].reshape(-1),
        down_total,
        vectors[3],
        vectors[4],
        vectors[5],
    )


def solution(mesh):
    whole, split = P(), P("batch", "seq")
    tokens = P("batch", "seq", None)
    return jax.shard_map(
        body,
        mesh=mesh,
        in_specs=(tokens, P("batch", None)) + (whole,) * 13 + (tokens,),
        out_specs=(tokens, tokens, split, whole, whole, split)
        + (whole,) * 3
        + (split, whole, split)
        + (whole,) * 3,
        check_vma=False,
    )
```

```python
import functools

import jax
import jax.numpy as jnp
from jax import lax
from jax.experimental import pallas as pl
from jax.experimental.pallas import tpu as pltpu
from jax.sharding import PartitionSpec as P

DH = 64
EPS = 1e-05
NEG = -1000000000.0
F32 = jnp.float32
LOW = jnp.bfloat16
PAIR = 2 * DH
SCALE = DH**-0.5
BLOCK = 256
UNIT = 128
SIZES = (5, 8)
VMEM = 18
CHUNKS = 1
ROOT_HALF = 0.5**0.5
ROOT_TWO_PI = 0.3989422804014327


def shaped(shape, dtype):
    return jax.ShapeDtypeStruct(shape, dtype)


def dot_nn(left, right):
    return jnp.dot(left, right, preferred_element_type=F32)


def dot_nt(left, right):
    return lax.dot_general(left, right, (((1,), (1,)), ((), ())), preferred_element_type=F32)


def params(mib):
    return pltpu.CompilerParams(vmem_limit_bytes=mib << 20, dimension_semantics=("arbitrary",))


def waiting(after):
    return [pl.BlockSpec(memory_space=pl.ANY)] * len(after)


def ordered(kernel, after):
    return lambda info, *refs: kernel(info, *refs[len(after) :])


def full(shape):
    return pl.BlockSpec(shape, lambda *_: (0,) * len(shape))


def cost(micros):
    return pl.CostEstimate(flops=int(micros * 0.6e9), transcendentals=0, bytes_accessed=0)


def column_sum(values):
    return jnp.sum(values, axis=0, keepdims=True)


def spot(rel, flip_x, order):
    bits = {"y": rel % 2, "z": (rel // 2) % 2, "w": rel // 4, "x": flip_x}
    index = 0
    for axis in order[1:]:
        index = index * 2 + bits[axis]
    return bits[order[0]], index


def put(value, rel, flip_x, order, send, keep):
    sent, index = spot(rel, flip_x, order)

    @pl.when(sent == 1)
    def _():
        send[pl.ds(index, 1)] = value.astype(LOW)[None]

    @pl.when(sent == 0)
    def _():
        keep[pl.ds(index, 1)] = value[None]


def put_rows(grad, rows, me, flip_x, order, send, keep):
    deep = grad.shape[0] // 8
    for b in range(8):
        rows[b] = grad[b * deep : (b + 1) * deep]
    for rel in range(8):
        sent, index = spot(rel, flip_x, order)
        value = rows[me ^ rel]
        if sent:
            send[index] = value.astype(LOW)
        else:
            keep[index] = value


def join_kernel(skip, segments, routes, *refs):
    refs = refs[skip:]
    ins, outs = refs[: 2 * len(segments)], list(refs[2 * len(segments) : -1])
    refs[-1][...] = jnp.zeros_like(refs[-1])
    for route in routes:
        send = outs.pop(0) if any(segments[m][n] > 1 for m, n in route) else None
        keep = outs.pop(0)
        sent = filled = 0
        for m, n in route:
            start, size = sum(segments[m][:n]), segments[m][n]
            total = ins[2 * m][start : start + size]
            total = total + ins[2 * m + 1][start : start + size].astype(F32)
            if size > 1:
                size //= 2
                send[sent : sent + size] = total[size:].astype(LOW)
                sent += size
            keep[filled : filled + size] = total[:size]
            filled += size


def join(messages, routes, after):
    segments = [list(message[0]) for message in messages]
    tail = messages[0][1].shape[1:]
    shapes, results = [], []
    for route in routes:
        sizes = [segments[m][n] for m, n in route]
        left = [size // 2 for size in sizes if size > 1]
        results.append(left)
        if left:
            shapes.append(shaped((sum(left),) + tail, LOW))
        shapes.append(shaped((sum(max(size // 2, 1) for size in sizes),) + tail, F32))
    operands = [array for message in messages for array in message[1:]]
    shapes.append(shaped((8, 128), F32))
    *arrays, token = pl.pallas_call(
        functools.partial(join_kernel, len(after), segments, routes),
        grid=(1,),
        in_specs=waiting(after) + [full(array.shape) for array in operands],
        out_specs=[full(shape.shape) for shape in shapes],
        out_shape=shapes,
        compiler_params=params(VMEM),
        cost_estimate=cost(1),
        name="join",
    )(*after, *operands)
    return [(left, arrays.pop(0) if left else None, arrays.pop(0)) for left in results], token


def each_window(info, block, run):
    start = pl.multiple_of(info[4 + block], UNIT)
    kind = info[4 + (info.shape[0] - 4) // 2 + block]
    for n, size in enumerate(SIZES):

        @pl.when(kind == n)
        def _():
            run(pl.ds(start, size * UNIT), size * UNIT)


def windows(segment):
    tokens = segment.shape[0]
    rows = segment.reshape(tokens // BLOCK, BLOCK)
    first = jnp.sum((segment[None] < rows[:, :1]).astype(jnp.int32), axis=1) // UNIT
    last = (jnp.sum((segment[None] <= rows[:, -1:]).astype(jnp.int32), axis=1) - 1) // UNIT
    need = last - first + 1
    kind = sum(((need > size).astype(jnp.int32) for size in SIZES[:-1]), jnp.zeros_like(need))
    size = sum(jnp.where(kind == n, size, 0).astype(jnp.int32) for n, size in enumerate(SIZES))
    return [jnp.minimum(first, tokens // UNIT - size) * UNIT, kind]


def both_heads(array):
    lane = lax.broadcasted_iota(jnp.int32, array.shape, 1)
    zero = jnp.zeros_like(array)
    return jnp.concatenate(
        [jnp.where(lane < DH, array, zero), jnp.where(lane < DH, zero, array)], axis=0
    )


def own_heads(turned):
    return jnp.concatenate([turned[:DH, :BLOCK], turned[DH:, BLOCK:]], axis=0)


def fill_segments(seg_row, seg_col):
    seg_col[...] = jnp.broadcast_to(seg_row[...].astype(F32), (UNIT, seg_row.shape[1])).T


def masked_scores(key, query, seg_col, seg_row):
    parts = [seg_col == seg_row[:, n : n + UNIT] for n in range(0, BLOCK, UNIT)]
    return jnp.where(jnp.concatenate(parts + parts, axis=1), dot_nt(key, query), NEG)


def forward_kernel(
    project, info, *refs,
):
    if project:
        x0, x1, x2, x3, wq, wk, wv, bq, bv, seg_row, *refs = refs
        q_all, k_all, v_all, *outs = refs[:8]
        o_out, lse_out = outs[3:]
        parts, first = outs[:3], 1
        xs, seg_col, qs, vt, ctx = refs[8:]
    else:
        q_all, k_all, v_all, seg_row, *refs = refs
        parts, first = refs[:1], 0
        o_out, lse_out, seg_col, qs, vt, ctx = refs[1:]
    place = info[0]
    tokens = q_all.shape[0]
    quarter = tokens // 4
    each = quarter // BLOCK

    @pl.when(pl.program_id(0) == 0)
    def _():
        if project:
            for j, ref in enumerate((x0, x1, x2, x3)):
                xs[pl.ds(pl.multiple_of((place ^ j) * quarter, quarter), quarter), :] = ref[...]
        fill_segments(seg_row, seg_col)

    if project:
        weights = jnp.concatenate([wq[...], wk[...], wv[...]], axis=1)
        projected = dot_nn(xs[...], weights)
        query = (projected[:, :PAIR] + bq[...].astype(F32)).astype(LOW)
        value = (projected[:, 2 * PAIR :] + bv[...].astype(F32)).astype(LOW)
        q_all[...] = query
        k_all[...] = projected[:, PAIR : 2 * PAIR].astype(LOW)
        v_all[...] = value
    else:
        query, value = q_all[...], v_all[...]
    qs[...] = query * jnp.asarray(SCALE, LOW)
    vt[...] = value.T

    def step(i, _):
        b = (place ^ (first + i // each)) * each + i % each
        rows = pl.ds(pl.multiple_of(b * BLOCK, BLOCK), BLOCK)
        here = pl.ds(pl.multiple_of(i * BLOCK, BLOCK), BLOCK)

        def run(window, size):
            row = seg_row[:, rows].astype(F32)
            scores = masked_scores(k_all[window, :], both_heads(qs[rows, :]), seg_col[window, :], row)
            top = jnp.max(scores, axis=0, keepdims=True)
            expo = jnp.exp(scores - top)
            total = jnp.sum(expo, axis=0, keepdims=True)
            mixed = dot_nn(vt[:, window], expo.astype(LOW)) * (1.0 / total)
            lse_out[0, pl.ds(i, 1), :] = top + jnp.log(total)
            mixed = own_heads(mixed)
            o_out[:, here] = mixed
            ctx[here, :] = mixed.T.astype(LOW)

        each_window(info, b, run)
        return 0

    lax.fori_loop(0, len(parts) * each, step, 0)
    for n, ref in enumerate(parts):
        ref[...] = ctx[n * quarter : (n + 1) * quarter, :]


def attend_forward(info, quarters, qkv_weight, query_bias, value_bias, seg):
    quarter, width = quarters[0].shape
    tokens, half = 4 * quarter, width // 2
    pairs, each = half // PAIR, quarter // BLOCK

    def weight_spec(t):
        return pl.BlockSpec((width, PAIR), lambda p, i: (0, (2 * t + i[1]) * pairs + p))

    def bias_spec():
        return pl.BlockSpec((1, PAIR), lambda p, i: (0, i[1] * pairs + p))

    col = pl.BlockSpec((tokens, PAIR), lambda p, i: (0, p))
    part = pl.BlockSpec((quarter, PAIR), lambda p, i: (0, p))

    def results(count):
        return (
            [part] * count
            + [
                pl.BlockSpec((PAIR, count * quarter), lambda p, i: (p, 0)),
                pl.BlockSpec((1, count * each, 2 * BLOCK), lambda p, i: (p, 0, 0)),
            ],
            [shaped((quarter, half), LOW)] * count
            + [
                shaped((half, count * quarter), F32),
                shaped((pairs, count * each, 2 * BLOCK), F32),
            ],
        )

    def scratch(count):
        return [
            pltpu.VMEM((tokens, UNIT), F32),
            pltpu.VMEM((tokens, PAIR), LOW),
            pltpu.VMEM((PAIR, tokens), LOW),
            pltpu.VMEM((count * quarter, PAIR), LOW),
        ]

    specs, shapes = results(3)
    query, key, value, *parts, context, lse = pl.pallas_call(
        functools.partial(forward_kernel, True),
        grid_spec=pltpu.PrefetchScalarGridSpec(
            num_scalar_prefetch=1,
            grid=(pairs,),
            in_specs=[full((quarter, width))] * 4
            + [weight_spec(0), weight_spec(1), weight_spec(2), bias_spec(), bias_spec()]
            + [full((1, tokens))],
            out_specs=[col] * 3 + specs,
            scratch_shapes=[pltpu.VMEM((tokens, width), LOW)] + scratch(3),
        ),
        out_shape=[shaped((tokens, half), LOW)] * 3 + shapes,
        compiler_params=params(VMEM),
        cost_estimate=cost(16),
        name="attend_forward",
    )(info, *quarters, qkv_weight, qkv_weight, qkv_weight, query_bias[None], value_bias[None], seg)
    specs, shapes = results(1)
    own, own_context, own_lse = pl.pallas_call(
        functools.partial(forward_kernel, False),
        grid_spec=pltpu.PrefetchScalarGridSpec(
            num_scalar_prefetch=1,
            grid=(pairs,),
            in_specs=[col] * 3 + [full((1, tokens))],
            out_specs=specs,
            scratch_shapes=scratch(1),
        ),
        out_shape=shapes,
        compiler_params=params(VMEM),
        cost_estimate=cost(5),
        name="attend_own",
    )(info, query, key, value, seg)
    return query, key, value, [own] + parts, (own_context, context), (own_lse, lse)


QKV_ORDERS = ("zyw", "zyw", "yzw")


def backward_kernel(
    n, info, q_in, k_in, v_in, o0, o1, o1b, o2, o3, o_own, o_far, lse_own, lse_far, seg_row, x_t, vec,
    dq_out, dk_out, dv_out, vec_out, w_send, w_keep,
    seg_col, qs, do, kt, dk, dv, w_rows, o_all, lse,
):
    place, core, me = info[0], info[1], info[3]
    tokens = q_in.shape[0]
    quarter = tokens // 4
    fill_segments(seg_row, seg_col)
    each = quarter // BLOCK
    o_all[:, :quarter] = o_own[...]
    o_all[:, quarter:] = o_far[...]
    lse[:each] = lse_own[0]
    lse[each:] = lse_far[0]
    for j, ref in enumerate((o0, None, o2, o3)):
        if ref is None:
            at = pl.multiple_of((place ^ 1) * quarter, quarter)
            do[pl.ds(at, quarter // 2), :] = o1[...]
            do[pl.ds(at + quarter // 2, quarter // 2), :] = o1b[...]
            continue
        do[pl.ds(pl.multiple_of((place ^ j) * quarter, quarter), quarter), :] = ref[...]
    qs[...] = q_in[...] * jnp.asarray(SCALE, LOW)
    kt[...] = k_in[...].T
    dk[...] = jnp.zeros_like(dk)
    dv[...] = jnp.zeros_like(dv)

    def step(b, _):
        start = pl.multiple_of(b * BLOCK, BLOCK)
        rows = pl.ds(start, BLOCK)

        def run(window, size):
            row = seg_row[:, rows].astype(F32)
            o_block = do[rows, :]
            query, grad = both_heads(qs[rows, :]), both_heads(o_block)
            i = (place ^ (b // each)) * each + b % each
            here = pl.ds(pl.multiple_of(i * BLOCK, BLOCK), BLOCK)
            along = o_block.T.astype(F32) * o_all[:, here]
            delta = jnp.concatenate([column_sum(along[:DH]), column_sum(along[DH:])], axis=1)
            scores = masked_scores(k_in[window, :], query, seg_col[window, :], row)
            probs = jnp.exp(scores - lse[pl.ds(i, 1), :])
            d_scores = (probs * (dot_nt(v_in[window, :], grad) - delta)).astype(LOW)
            dv[window, :] += dot_nn(probs.astype(LOW), grad)
            dk[window, :] += dot_nn(d_scores, query)
            d_query = own_heads(dot_nn(kt[:, window], d_scores)) * SCALE
            dq_out[rows, :] = d_query.T.astype(LOW)

        each_window(info, b, run)
        return 0

    lax.fori_loop(0, tokens // BLOCK, step, 0)
    dk_out[...] = dk[...].astype(LOW)
    dv_out[...] = dv[...].astype(LOW)
    vec_out[...] = vec[...]
    half = vec.shape[1] // 2
    for side in range(2):

        @pl.when(core == side)
        def _():
            cut = slice(side * half + n * PAIR, side * half + (n + 1) * PAIR)
            vec_out[10:11, cut] = column_sum(dq_out[...].astype(F32))
            vec_out[11:12, cut] = column_sum(dv_out[...].astype(F32))

    grad = jnp.concatenate([dq_out[...], dk_out[...], dv_out[...]], axis=1)
    grad = dot_nn(x_t[...], grad)
    put_rows(grad, w_rows, me, 0, QKV_ORDERS[n], w_send, w_keep)


def attend_backward(info, n, query, key, value, parts, context, lse, seg, x_t, vectors, after):
    tokens, half = query.shape
    quarter, blocks, width = tokens // 4, tokens // BLOCK, x_t.shape[0]
    col = pl.BlockSpec((tokens, PAIR), lambda p, i: (0, n))
    pairs = half // PAIR
    part = pl.BlockSpec((quarter, PAIR), lambda p, i: (0, n))
    first = pl.BlockSpec((None, quarter, PAIR), lambda p, i: (0, 0, n))
    packed = quarter // 2
    low, high = [
        pl.BlockSpec((packed, PAIR), lambda p, i, at=at: (half // packed, at * pairs + n))
        for at in range(2)
    ]
    weight = (4, width // 8, 3 * PAIR)
    dtypes = (LOW, F32)
    return pl.pallas_call(
        ordered(functools.partial(backward_kernel, n), after),
        grid_spec=pltpu.PrefetchScalarGridSpec(
            num_scalar_prefetch=1,
            grid=(1,),
            in_specs=waiting(after)
            + [col] * 3
            + [part, low, high, first, part]
            + [pl.BlockSpec((PAIR, array.shape[1]), lambda p, i: (n, 0)) for array in context]
            + [pl.BlockSpec((1,) + array.shape[1:], lambda p, i: (n, 0, 0)) for array in lse]
            + [full((1, tokens)), full((width, tokens)), full(vectors.shape)],
            out_specs=[full((tokens, PAIR))] * 3
            + [full(vectors.shape)]
            + [full(weight)] * len(dtypes),
            scratch_shapes=[
                pltpu.VMEM((tokens, UNIT), F32),
                pltpu.VMEM((tokens, PAIR), LOW),
                pltpu.VMEM((tokens, PAIR), LOW),
                pltpu.VMEM((PAIR, tokens), LOW),
                pltpu.VMEM((tokens, PAIR), F32),
                pltpu.VMEM((tokens, PAIR), F32),
                pltpu.VMEM((8, width // 8, 3 * PAIR), F32),
                pltpu.VMEM((PAIR, tokens), F32),
                pltpu.VMEM((blocks, 2 * BLOCK), F32),
            ],
        ),
        out_shape=[shaped((tokens, PAIR), LOW)] * 3
        + [shaped(vectors.shape, F32)]
        + [shaped(weight, dtype) for dtype in dtypes],
        compiler_params=params(VMEM),
        cost_estimate=cost(8),
        name="attend_backward",
    )(info, *after, query, key, value, *parts, *context, *lse, seg, x_t, vectors)


def normalise(values):
    centred = values - jnp.mean(values, axis=1, keepdims=True)
    root = lax.rsqrt(jnp.mean(centred * centred, axis=1, keepdims=True) + EPS)
    return centred * root, root


def norm_back(grad, gain, normal, root):
    e = grad * gain
    along = jnp.mean(e * normal, axis=1, keepdims=True)
    return root * (e - jnp.mean(e, axis=1, keepdims=True) - normal * along)


def store_columns(place, flipped, mine, send):
    size, count = flipped.shape[0] // 4, flipped.shape[1]
    for b in range(4):
        rel = place ^ b

        @pl.when(rel % 2 == 0)
        def _():
            mine[pl.ds(rel // 2, 1)] = flipped[b * size : (b + 1) * size][None]

        @pl.when(rel % 2 == 1)
        def _():
            rows = pl.ds(pl.multiple_of(rel // 2 * size, size), size)
            send[rows, :count] = flipped[b * size : (b + 1) * size]


def middle_forward_kernel(
    info, p0, p1, p2, p3, x_in, cot, wo, bo, g1, s1, up, bup, down, bdown, g2, s2,
    out, d_res, n1, r1, turned, act, slope, mine, send, vec,
    hid, hid_low, branch,
):
    place, core, chip = info[0], info[1], info[2]
    step = pl.program_id(0)
    quarter = p0.shape[0]

    @pl.when(step == 0)
    def _():
        first = core == 0

        def sides(a, b):
            a, b = a[...], b[...]
            return jnp.concatenate([jnp.where(first, a, b), jnp.where(first, b, a)], axis=1)

        ctx = jnp.concatenate([sides(p0, p1), sides(p2, p3)], axis=0)
        turned[1] = ctx.T
        x = jnp.concatenate([x_in[chip], x_in[1 - chip]], axis=0).astype(F32)
        summed = x + dot_nn(ctx, wo[...]) + bo[...].astype(F32)
        normal, root = normalise(summed)
        n1[...] = normal
        r1[...] = root
        hidden = normal * g1[...].astype(F32) + s1[...].astype(F32)
        hid[...] = hidden
        low = hidden.astype(LOW)
        hid_low[...] = low
        turned[0] = low.T
        branch[...] = jnp.zeros_like(branch)

    size = hid.shape[0] // CHUNKS
    chunks = [slice(n * size, (n + 1) * size) for n in range(CHUNKS)]
    pres = [dot_nn(hid_low[rows, :], up[...]) + bup[...].astype(F32) for rows in chunks]
    for rows, pre in zip(chunks, pres):
        phi = 0.5 + 0.5 * lax.erf(pre * ROOT_HALF)
        low = (pre * phi).astype(LOW)
        act[rows, :] = low
        slope[rows, :] = phi + pre * (jnp.exp(-0.5 * pre * pre) * ROOT_TWO_PI)
        branch[rows, :] += dot_nn(low, down[...])

    @pl.when(step == pl.num_programs(0) - 1)
    def _():
        normal, root = normalise(hid[...] + branch[...] + bdown[...].astype(F32))
        final = (normal * g2[...].astype(F32) + s2[...].astype(F32)).astype(LOW)
        out[pl.ds(chip, 1)] = final[:quarter][None]
        out[pl.ds(1 - chip, 1)] = final[quarter:][None]
        grad = jnp.concatenate([cot[chip], cot[1 - chip]], axis=0).astype(F32)
        back = norm_back(grad, g2[...].astype(F32), normal, root)
        d_res[...] = back
        vec[0:1, :] = column_sum(back)
        vec[1:2, :] = column_sum(grad * normal)
        vec[2:3, :] = column_sum(grad)
        store_columns(place, back.astype(LOW).T, mine, send)


def mark_kernel(*refs):
    refs[-1][...] = jnp.zeros_like(refs[-1])


def mark(*after):
    return pl.pallas_call(
        mark_kernel,
        grid=(1,),
        in_specs=waiting(after),
        out_specs=full((8, 128)),
        out_shape=shaped((8, 128), F32),
        compiler_params=params(VMEM),
        cost_estimate=cost(1),
        name="mark",
    )(*after)


def middle_forward(after, info, parts, inputs, cotangent, wo, bo, g1, s1, up, bup, down, bdown, g2, s2):
    quarter, half = parts[0].shape
    width, inner = 2 * half, up.shape[1]
    count, steps = 2 * quarter, 4
    chunk = inner // steps
    vector = full((1, width))
    tokens = full((count, width))
    turned = full((2, width // 4, count))
    return pl.pallas_call(
        ordered(middle_forward_kernel, after),
        grid_spec=pltpu.PrefetchScalarGridSpec(
            num_scalar_prefetch=1,
            grid=(steps,),
            in_specs=waiting(after)
            + [full((quarter, half))] * 4
            + [full((2, quarter, width))] * 2
            + [full((width, width)), vector, vector, vector]
            + [
                pl.BlockSpec((width, chunk), lambda c, i: (0, c)),
                pl.BlockSpec((1, chunk), lambda c, i: (0, c)),
                pl.BlockSpec((chunk, width), lambda c, i: (c, 0)),
            ]
            + [vector] * 3,
            out_specs=[full((2, quarter, width)), tokens, tokens, full((count, 1))]
            + [full((2, width, count))]
            + [pl.BlockSpec((count, chunk), lambda c, i: (0, c))] * 2
            + [turned, full((width // 2, count)), full((8, width))],
            scratch_shapes=[
                pltpu.VMEM((count, width), F32),
                pltpu.VMEM((count, width), LOW),
                pltpu.VMEM((count, width), F32),
            ],
        ),
        out_shape=[
            shaped((2, quarter, width), LOW),
            shaped((count, width), F32),
            shaped((count, width), F32),
            shaped((count, 1), F32),
            shaped((2, width, count), LOW),
            shaped((count, inner), LOW),
            shaped((count, inner), F32),
            shaped((2, width // 4, count), LOW),
            shaped((width // 2, count), LOW),
            shaped((8, width), F32),
        ],
        compiler_params=params(VMEM),
        cost_estimate=cost(18),
        name="middle_forward",
    )(
        info, *after, *parts, inputs, cotangent, wo, bo[None], g1[None], s1[None],
        up, bup[None], down, bdown[None], g2[None], s2[None],
    )


def middle_backward_kernel(
    info, d_res, slope, down, up, wo, n1, r1, g1, vec_two,
    to_core, mine_pre, d_summed, q0, to_chip, mine, vec,
    d_branch, d_hidden,
):
    place, core = info[0], info[1]
    step = pl.program_id(0)
    quarter = q0.shape[0]
    half = q0.shape[1]
    count = d_res.shape[0]

    @pl.when(step == 0)
    def _():
        d_branch[...] = d_res[...].astype(LOW)
        d_hidden[...] = d_res[...]

    d_pre = (dot_nt(d_branch[...], down[...]) * slope[...]).astype(LOW)
    block = place ^ (1 - step // 2 + 2 * (step % 2))
    vec[pl.ds(6 + block, 1), :] = column_sum(d_pre.astype(F32))
    d_hidden[...] += dot_nt(d_pre, up[...])

    @pl.when(step < 2)
    def _():
        at = pl.multiple_of((1 + step) * count, count)
        to_core[pl.ds(at, count), :] = d_pre

    @pl.when(step >= 2)
    def _():
        mine_pre[0] = d_pre

    @pl.when(step == pl.num_programs(0) - 1)
    def _():
        grad = d_hidden[...]
        normal = n1[...]
        back = norm_back(grad, g1[...].astype(F32), normal, r1[...])
        d_summed[...] = back
        vec[3:6, :] = vec_two[0:3, :]
        vec[10:16, :] = jnp.zeros_like(vec[10:16, :])
        vec[0:1, :] = column_sum(back)
        vec[1:2, :] = column_sum(grad * normal)
        vec[2:3, :] = column_sum(grad)
        low = back.astype(LOW)
        store_columns(place, low.T, mine, to_core)
        d_ctx = dot_nt(low, wo[...]).astype(LOW)
        first = core == 0
        left, right = d_ctx[:, :half], d_ctx[:, half:]
        same = jnp.where(first, left, right)
        other = jnp.where(first, right, left)
        q0[...] = same[:quarter]
        packed = quarter // 2
        to_core[half : half + packed, :] = jnp.concatenate(
            [other[:packed], other[packed:quarter]], axis=1
        )
        to_chip[0] = same[quarter:]
        to_chip[1] = other[quarter:]


def middle_backward(info, d_res, slope, down, up, wo, n1, r1, g1, vec_two):
    count, width = d_res.shape
    inner, quarter, half = up.shape[1], count // 2, width // 2
    steps = 4
    chunk = inner // steps

    def block(c, i):
        return i[0] ^ (1 - c // 2 + 2 * (c % 2))

    tokens = full((count, width))
    turned = full((2, width // 4, count))
    return pl.pallas_call(
        middle_backward_kernel,
        grid_spec=pltpu.PrefetchScalarGridSpec(
            num_scalar_prefetch=1,
            grid=(steps,),
            in_specs=[
                tokens,
                pl.BlockSpec((count, chunk), lambda c, i: (0, block(c, i))),
                pl.BlockSpec((chunk, width), lambda c, i: (block(c, i), 0)),
                pl.BlockSpec((width, chunk), lambda c, i: (0, block(c, i))),
                full((width, width)),
                tokens,
                full((count, 1)),
                full((1, width)),
                full(vec_two.shape),
            ],
            out_specs=[
                full((3 * count, width)),
                pl.BlockSpec((1, count, chunk), lambda c, i: (jnp.maximum(c - 2, 0), 0, 0)),
                tokens,
            ]
            + [full((quarter, half)), full((2, quarter, half)), turned, full((16, width))],
            scratch_shapes=[pltpu.VMEM((count, width), LOW), pltpu.VMEM((count, width), F32)],
        ),
        out_shape=[
            shaped((3 * count, width), LOW),
            shaped((2, count, chunk), LOW),
            shaped((count, width), F32),
        ]
        + [
            shaped((quarter, half), LOW),
            shaped((2, quarter, half), LOW),
            shaped((2, width // 4, count), LOW),
            shaped((16, width), F32),
        ],
        compiler_params=params(VMEM),
        cost_estimate=cost(16),
        name="middle_backward",
    )(info, d_res, slope, down, up, wo, n1, r1, g1[None], vec_two)


DOWN_ORDERS = ("zxwy", "xzwy")


def down_kernel(info, mine, theirs, act, act_pair, *outs):
    rel = pl.program_id(0)
    left = jnp.concatenate([mine[0], mine[1]], axis=0)
    grad = dot_nn(left, act[...]) + dot_nn(theirs[...], act_pair[...])
    size = grad.shape[0] // 4
    for n, order in enumerate(DOWN_ORDERS):
        for flip in range(2):
            start = (2 * flip + n) * size
            put(grad[start : start + size], rel, flip, order, outs[2 * n], outs[2 * n + 1])


def down_grad(info, mine, theirs, act, act_pair, after):
    _, size, count = mine.shape
    block = act.shape[1] // 8
    part = (8, size // 2, block)
    spec = pl.BlockSpec((count, block), lambda r, i: (0, r ^ i[3]))
    return pl.pallas_call(
        ordered(down_kernel, after),
        grid_spec=pltpu.PrefetchScalarGridSpec(
            num_scalar_prefetch=1,
            grid=(8,),
            in_specs=waiting(after) + [full(mine.shape), full(theirs.shape), spec, spec],
            out_specs=[full(part)] * 4,
        ),
        out_shape=[shaped(part, LOW), shaped(part, F32)] * 2,
        compiler_params=params(VMEM),
        cost_estimate=cost(8),
        name="down_grad",
    )(info, *after, mine, theirs, act, act_pair)


UP_ORDERS = ("xyzw", "yxzw")


def up_kernel(
    info, left, left_pair, mine, theirs, mine_d, theirs_d, send_a, keep_a, send_b, keep_b, rows
):
    me = info[3]
    step = pl.program_id(0)

    @pl.when(step < 4)
    def _():
        grad = dot_nn(left[0], mine[0]) + dot_nn(left_pair[0], theirs[...])
        for n, flip in ((0, 0), (1, 0), (0, 1), (1, 1)):

            @pl.when(step == 2 * flip + n)
            def _():
                send, keep = ((send_a, keep_a), (send_b, keep_b))[n]
                put_rows(grad, rows, me, flip, UP_ORDERS[n], send, keep)

    @pl.when(step == 4)
    def _():
        right = jnp.concatenate([mine_d[0], mine_d[1]], axis=0)
        grad = dot_nt(left[1], right) + dot_nt(left_pair[1], theirs_d[...])
        deep, wide = grad.shape[0] // 8, grad.shape[1] // 2
        for b in range(8):
            rows[b] = grad[b * deep : (b + 1) * deep]
        for rel in range(4):
            near, far = rows[me ^ rel], rows[me ^ (rel + 4)]
            for flip in range(2):
                cut = slice(flip * wide, (flip + 1) * wide)
                value = jnp.concatenate([near[:, cut], far[:, cut]], axis=1)
                index = 8 + 2 * flip + rel // 2
                if rel % 2:
                    send_b[index] = value.astype(LOW)
                else:
                    keep_b[index] = value


def up_grad(info, left, left_pair, mine, from_core, mine_d, after):
    _, width, count = left.shape
    half = width // 2

    def at(s):
        return jnp.minimum(s, 3)

    shapes = [
        shaped((lead, width // 8, half), dtype) for lead in (8, 12) for dtype in (LOW, F32)
    ]
    return pl.pallas_call(
        ordered(up_kernel, after),
        grid_spec=pltpu.PrefetchScalarGridSpec(
            num_scalar_prefetch=1,
            grid=(5,),
            in_specs=waiting(after)
            + [full(left.shape)] * 2
            + [
                pl.BlockSpec((1, count, half), lambda s, i: (at(s) // 2, 0, at(s) % 2)),
                pl.BlockSpec((count, half), lambda s, i: (1 + at(s) // 2, at(s) % 2)),
                full(mine_d.shape),
                pl.BlockSpec((half, count), lambda s, i: (0, 0)),
            ],
            out_specs=[full(shape.shape) for shape in shapes],
            scratch_shapes=[pltpu.VMEM((8, width // 8, half), F32)],
        ),
        out_shape=shapes,
        compiler_params=params(VMEM),
        cost_estimate=cost(10),
        name="up_grad",
    )(info, *after, left, left_pair, mine, from_core, mine_d, from_core)


def input_kernel(info, *refs):
    grads, weights, (keep, send) = refs[:9], refs[9:12], refs[12:]
    rel = pl.program_id(0)
    total = sum(
        dot_nt(jnp.concatenate([ref[...] for ref in grads[t::3]], axis=1), weights[t][...])
        for t in range(3)
    )

    @pl.when(rel < 2)
    def _():
        send[0] = total

    @pl.when(rel >= 2)
    def _():
        keep[0] = total


def input_part(info, grads, qkv_weight, after):
    tokens = grads[0].shape[0]
    width = qkv_weight.shape[0]
    quarter, half = tokens // 4, width // 2

    rows = pl.BlockSpec((quarter, PAIR), lambda c, i: (i[0] ^ (1 - c // 2 + 2 * (c % 2)), 0))

    def weight(t):
        return pl.BlockSpec((width, half), lambda c, i: (0, 2 * t + i[1]))

    return pl.pallas_call(
        ordered(input_kernel, after),
        grid_spec=pltpu.PrefetchScalarGridSpec(
            num_scalar_prefetch=1,
            grid=(4,),
            in_specs=waiting(after) + [rows] * 9 + [weight(0), weight(1), weight(2)],
            out_specs=[
                pl.BlockSpec((1, quarter, width), lambda c, i: (jnp.maximum(c - 2, 0), 0, 0)),
                pl.BlockSpec((1, quarter, width), lambda c, i: (jnp.minimum(c, 1), 0, 0)),
            ],
        ),
        out_shape=[shaped((2, quarter, width), F32)] * 2,
        compiler_params=params(VMEM),
        cost_estimate=cost(6),
        name="input_part",
    )(info, *after, *grads, qkv_weight, qkv_weight, qkv_weight)


UNITS = (((0, 1), (2, 3), (4,), (5,)), ((0,), (1,), (2, 3), (4, 5)))


def share_kernel(info, zero, first, kept, got, own, one, two, three):
    place, core = info[0], info[1]
    total = [zero[zero.shape[0] - 1], first[first.shape[0] - 1], kept[0] + got[0].astype(F32)]
    units = []
    for t in range(3):
        part = jnp.concatenate([pair[:, t * PAIR : (t + 1) * PAIR] for pair in total], axis=1)
        units += jnp.split(part, 2, axis=1)
    for side in range(2):
        for target in range(4):
            for flip, ref in enumerate((own, one, two, three)):

                @pl.when(jnp.logical_and(core == side, place ^ target == flip))
                def _():
                    for n in range(2):
                        unit = units[UNITS[side][target][n % len(UNITS[side][target])]]
                        ref[n] = unit.astype(ref.dtype)


def share(info, zero, one, kept, got, after):
    unit = (2, got.shape[1], got.shape[2] // 2)
    return pl.pallas_call(
        ordered(share_kernel, after),
        grid_spec=pltpu.PrefetchScalarGridSpec(
            num_scalar_prefetch=1,
            grid=(1,),
            in_specs=waiting(after)
            + [full(array.shape) for array in (zero, one, kept, got)],
            out_specs=[full(unit)] * 4,
        ),
        out_shape=[shaped(unit, F32)] + [shaped(unit, LOW)] * 3,
        compiler_params=params(VMEM),
        cost_estimate=cost(1),
        name="share",
    )(info, *after, zero, one, kept, got)


def gather_kernel(info, own, one, two, three, out):
    place = info[0]
    same = own[...] + two[...].astype(F32)
    other = one[...].astype(F32) + three[...].astype(F32)
    for target in range(4):

        @pl.when(place == target)
        def _():
            sides = (same, other) if target % 2 == 0 else (other, same)
            pieces = [
                (side_unit, sides[side][n])
                for side in range(2)
                for n, side_unit in enumerate(
                    unit % 2 + 4 * (unit // 2) + 2 * side for unit in UNITS[side][target]
                )
            ]
            pieces.sort(key=lambda piece: piece[0])
            out[...] = jnp.concatenate([piece[1] for piece in pieces], axis=1)


def gather(info, own, *others):
    shape = (own.shape[1], 3 * own.shape[2])
    return pl.pallas_call(
        gather_kernel,
        grid_spec=pltpu.PrefetchScalarGridSpec(
            num_scalar_prefetch=1,
            grid=(1,),
            in_specs=[full(own.shape)] * 4,
            out_specs=full(shape),
        ),
        out_shape=shaped(shape, F32),
        compiler_params=params(VMEM),
        cost_estimate=cost(1),
        name="gather",
    )(info, own, *others)


def turn_kernel(info, x0, x1, x2, x3, x_t):
    quarter = x0.shape[0]
    for j, ref in enumerate((x0, x1, x2, x3)):
        at = pl.multiple_of((info[0] ^ j) * quarter, quarter)
        x_t[:, pl.ds(at, quarter)] = ref[...].T


def turn(info, quarters):
    quarter, width = quarters[0].shape
    return pl.pallas_call(
        turn_kernel,
        grid_spec=pltpu.PrefetchScalarGridSpec(
            num_scalar_prefetch=1,
            grid=(1,),
            in_specs=[full((quarter, width))] * 4,
            out_specs=full((width, 4 * quarter)),
        ),
        out_shape=shaped((width, 4 * quarter), LOW),
        compiler_params=params(VMEM),
        cost_estimate=cost(1),
        name="turn",
    )(info, *quarters)


def body(
    inputs,
    segments,
    qkv_weight,
    query_bias,
    value_bias,
    out_weight,
    out_bias,
    norm1_gain,
    norm1_shift,
    up_weight,
    up_bias,
    down_weight,
    down_bias,
    norm2_gain,
    norm2_shift,
    cotangent,
):
    rows, quarter, width = inputs.shape
    half = width // 2
    seq_size = lax.axis_size("seq")
    batch_size = lax.axis_size("batch")
    fine = batch_size // 8
    place = lax.axis_index("seq")
    chip, core = place // 2, place % 2
    segment = lax.dynamic_index_in_dim(segments, chip, 0)
    info = jnp.stack([place, core, chip, lax.axis_index("batch") // fine]).astype(jnp.int32)
    info = jnp.concatenate([info] + windows(segment[0]))

    def over_seq(array, flip):
        return lax.ppermute(array, "seq", [(i, i ^ flip) for i in range(seq_size)])

    def over_batch(array, flip):
        return lax.ppermute(array, "batch", [(i, i ^ flip) for i in range(batch_size)])

    def swap(array, axis):
        if axis == "x":
            return over_seq(array, 2)
        return over_batch(array, fine << "yzw".index(axis))

    def pick(array, index, axis=0):
        return lax.dynamic_index_in_dim(array, index, axis, keepdims=False)

    def tie(*arrays):
        return lax.optimization_barrier(arrays)

    def launch(*messages):
        return [
            (order, segments, kept, swap(sent, order[0]))
            for order, segments, sent, kept in messages
        ]

    def land(after, flights, *routes):
        made, token = join(
            [flight[1:] for flight in flights], [route[1:] for route in routes], after
        )
        return [(route[0],) + new for route, new in zip(routes, made)], token

    def finish(grad):
        if fine > 1:
            groups = [[i * fine + j for j in range(fine)] for i in range(8)]
            grad = lax.psum_scatter(
                grad, "batch", scatter_dimension=0, axis_index_groups=groups, tiled=True
            )
        return grad

    own = pick(inputs, chip)
    far = over_seq(pick(inputs, 1 - chip), 2)
    near = over_seq(own, 1)
    across = over_seq(far, 1)
    quarters = (own, near, far, across)

    query, key, value, parts, context, lse = attend_forward(
        info, quarters, qkv_weight, query_bias, value_bias, segment
    )
    parts = [parts[0]] + [over_seq(parts[j], j) for j in (1, 2, 3)]
    x_t = turn(info, quarters)

    outputs, d_res, n1, r1, turned, act, slope, mine, send, vec_two = middle_forward(
        [x_t], info, parts, inputs, cotangent, out_weight, out_bias, norm1_gain, norm1_shift,
        up_weight, up_bias, down_weight, down_bias, norm2_gain, norm2_shift,
    )
    pair = over_seq(turned, 1), over_seq(act, 1), over_seq(send, 1)
    back = middle_backward(
        info, d_res, slope, down_weight, up_weight, out_weight, n1, r1, norm1_gain, vec_two
    )
    turned_pair, act_pair, theirs = pair
    to_core, mine_pre, d_summed, q0, to_chip, mine_d, vectors = back

    token = mark(turned_pair, act_pair, theirs, vectors)
    to_core, to_chip, token = tie(to_core, to_chip, token)
    from_core, from_chip = over_seq(to_core, 1), over_seq(to_chip, 2)
    made = down_grad(info, mine, theirs, act, act_pair, [token])
    downs = launch(
        (DOWN_ORDERS[0], [8], made[0], made[1]), (DOWN_ORDERS[1], [8], made[2], made[3])
    )
    across = over_seq(from_chip[1], 1)
    made = up_grad(info, turned, turned_pair, mine_pre, from_core, mine_d, [made[1]])
    ups = launch((UP_ORDERS[0], [8], made[0], made[1]), (UP_ORDERS[1], [8, 4], made[2], made[3]))
    d_parts = (q0, from_core, from_core, from_chip, across)

    def piece(n, vectors, after):
        made = attend_backward(
            info, n, query, key, value, d_parts, context, lse, segment, x_t, vectors, after
        )
        return list(made)

    def opening(n, made, token):
        sent, token = tie(made[4], token)
        return (QKV_ORDERS[n], [4], sent, made[5]), token

    zero = piece(0, vectors, [made[1]])
    downs, token = land(
        zero[3:4], downs, (DOWN_ORDERS[0][1:], (0, 0)), (DOWN_ORDERS[1][1:], (1, 0))
    )
    opened, token = opening(0, zero, token)
    *downs, first = launch(*downs, opened)

    one = piece(1, zero[3], [token])
    (up_a, up_b, down), token = land(
        one[3:4],
        ups + downs + [first],
        (UP_ORDERS[0][1:], (0, 0), (4, 0)),
        (UP_ORDERS[1][1:], (1, 0), (1, 1)),
        ("wy", (2, 0), (3, 0)),
    )
    opened, token = opening(1, one, token)
    flights = launch(up_a, up_b, down, opened)

    two = piece(2, one[3], [token])
    (up, first, down), token = land(
        two[3:4],
        flights,
        ("zw", (0, 0), (1, 0), (1, 1)),
        ("w", (0, 1)),
        ("y", (2, 0), (2, 1), (3, 0)),
    )
    grads = [*zero[:3], *one[:3], *two[:3]]
    opened, token = opening(2, two, token)
    vectors, token = tie(two[3], token)
    flights = launch(opened, up, first, down)
    vectors_got = over_seq(vectors, 1)

    keep, send = input_part(info, grads, qkv_weight, [token])
    (third, up, down), token = land(
        [keep],
        flights,
        (QKV_ORDERS[2][1:], (0, 0)),
        ("w", (1, 0), (1, 1), (3, 2), (1, 2)),
        ("", (3, 0), (3, 1), (2, 0)),
    )
    down_total, out_total = down[3], up[3][3]
    third, up = launch(third, up)
    send, vectors_got, token = tie(send, vectors_got, token)
    d_row = keep + over_seq(send, 1)
    d_far = over_seq(d_row[1].astype(LOW), 2)
    vectors = vectors + vectors_got
    vectors = vectors + over_seq(vectors, 2)
    vectors = vectors + swap(vectors, "y")
    (third, up), token = land([token, vectors], [third, up], ("w", (0, 0)), ("", (1, 0), (1, 1), (1, 2)))
    up_total = up[3]
    vectors, out_total, token = tie(vectors, out_total, token)
    (third,) = launch(third)
    wide = half // 2
    out_got = swap(out_total[:, wide:].astype(LOW), "w")
    vectors_got = swap(vectors, "z")
    own, *others = share(info, down[3], up[3], third[2], third[3], [token, vectors_got, d_far])
    vectors_got, own = tie(vectors_got, own)
    vectors = vectors + vectors_got
    qkv_total = gather(info, own, *[over_seq(other, 1 + j) for j, other in enumerate(others)])
    qkv_total = finish(qkv_total)
    out_total = out_total[:, :wide] + out_got.astype(F32)
    out_total = finish(out_total)
    down_total = finish(down_total[:2].reshape(wide, half).T)
    up_total = finish(jnp.concatenate([up_total[0], up_total[1]], axis=1))

    vectors = vectors + swap(vectors, "w")
    flip = 1
    while flip < fine:
        vectors = vectors + over_batch(vectors, flip)
        flip *= 2
    d_near = d_summed[:quarter] + d_row[0]
    d_far = d_summed[quarter:] + d_far.astype(F32)
    d_inputs = jnp.stack([jnp.where(chip == 0, d_near, d_far), jnp.where(chip == 0, d_far, d_near)])
    return (
        outputs,
        d_inputs,
        qkv_total,
        vectors[10],
        vectors[11],
        out_total,
        vectors[0],
        vectors[1],
        vectors[2],
        up_total,
        vectors[6:10].reshape(-1),
        down_total,
        vectors[3],
        vectors[4],
        vectors[5],
    )


def solution(mesh):
    whole, split = P(), P("batch", "seq")
    tokens = P("batch", "seq", None)
    return jax.shard_map(
        body,
        mesh=mesh,
        in_specs=(tokens, P("batch", None)) + (whole,) * 13 + (tokens,),
        out_specs=(tokens, tokens, split, whole, whole, split)
        + (whole,) * 3
        + (split, whole, split)
        + (whole,) * 3,
        check_vma=False,
    )
```

```python
import functools

import jax
import jax.numpy as jnp
from jax import lax
from jax.experimental import pallas as pl
from jax.experimental.pallas import tpu as pltpu
from jax.sharding import PartitionSpec as P

DH = 64
EPS = 1e-05
NEG = -1000000000.0
F32 = jnp.float32
LOW = jnp.bfloat16
PAIR = 2 * DH
SCALE = DH**-0.5
BLOCK = 256
UNIT = 128
SIZES = (5, 8)
VMEM = 18
CHUNKS = 1
ROOT_HALF = 0.5**0.5
ROOT_TWO_PI = 0.3989422804014327


def shaped(shape, dtype):
    return jax.ShapeDtypeStruct(shape, dtype)


def dot_nn(left, right):
    return jnp.dot(left, right, preferred_element_type=F32)


def dot_nt(left, right):
    return lax.dot_general(left, right, (((1,), (1,)), ((), ())), preferred_element_type=F32)


def params(mib):
    return pltpu.CompilerParams(vmem_limit_bytes=mib << 20, dimension_semantics=("arbitrary",))


def waiting(after):
    return [pl.BlockSpec(memory_space=pl.ANY)] * len(after)


def ordered(kernel, after):
    return lambda info, *refs: kernel(info, *refs[len(after) :])


def full(shape):
    return pl.BlockSpec(shape, lambda *_: (0,) * len(shape))


def cost(micros):
    return pl.CostEstimate(flops=int(micros * 0.6e9), transcendentals=0, bytes_accessed=0)


def column_sum(values):
    return jnp.sum(values, axis=0, keepdims=True)


def spot(rel, flip_x, order):
    bits = {"y": rel % 2, "z": (rel // 2) % 2, "w": rel // 4, "x": flip_x}
    index = 0
    for axis in order[1:]:
        index = index * 2 + bits[axis]
    return bits[order[0]], index


def put(value, rel, flip_x, order, send, keep):
    sent, index = spot(rel, flip_x, order)

    @pl.when(sent == 1)
    def _():
        send[pl.ds(index, 1)] = value.astype(LOW)[None]

    @pl.when(sent == 0)
    def _():
        keep[pl.ds(index, 1)] = value[None]


def put_rows(grad, rows, me, flip_x, order, send, keep):
    deep = grad.shape[0] // 8
    for b in range(8):
        rows[b] = grad[b * deep : (b + 1) * deep]
    for rel in range(8):
        sent, index = spot(rel, flip_x, order)
        value = rows[me ^ rel]
        if sent:
            send[index] = value.astype(LOW)
        else:
            keep[index] = value


def leaves(segments, route):
    return any(m >= len(segments) or segments[m][n] > 1 for m, n in route)


def join_kernel(skip, segments, fresh, routes, *refs):
    refs = refs[skip:]
    count = 2 * len(segments)
    ins, new = refs[:count], refs[count : count + 2 * fresh]
    outs = list(refs[count + 2 * fresh : -1])
    refs[-1][...] = jnp.zeros_like(refs[-1])
    for route in routes:
        more = leaves(segments, route)
        send = outs.pop(0) if more else None
        keep = outs.pop(0)
        sent = filled = 0
        for m, n in route:
            if m >= len(segments):
                at = 2 * (m - len(segments))
                size = new[at].shape[0]
                send[sent : sent + size] = new[at][...]
                keep[filled : filled + size] = new[at + 1][...]
                sent += size
                filled += size
                continue
            start, size = sum(segments[m][:n]), segments[m][n]
            total = ins[2 * m][start : start + size]
            total = total + ins[2 * m + 1][start : start + size].astype(F32)
            if size > 1:
                size //= 2
                send[sent : sent + size] = total[size:].astype(LOW)
                sent += size
            elif more:
                wide = total.shape[2] // 2
                turned = jnp.concatenate([total[0, :, wide:], total[0, :, :wide]], axis=1)
                send[sent] = turned.astype(LOW)
                sent += 1
            keep[filled : filled + size] = total[:size]
            filled += size


def join(messages, routes, after, fresh):
    segments = [list(message[0]) for message in messages]
    tail = messages[0][1].shape[1:]
    shapes, results = [], []
    for route in routes:
        left = [
            fresh[m - len(segments)][0].shape[0]
            if m >= len(segments)
            else max(segments[m][n] // 2, 1)
            for m, n in route
        ]
        more = leaves(segments, route)
        results.append(left if more else [])
        if more:
            shapes.append(shaped((sum(left),) + tail, LOW))
        shapes.append(shaped((sum(left),) + tail, F32))
    operands = [array for message in messages for array in message[1:]]
    operands += [array for pair in fresh for array in pair]
    shapes.append(shaped((8, 128), F32))
    *arrays, token = pl.pallas_call(
        functools.partial(join_kernel, len(after), segments, len(fresh), routes),
        grid=(1,),
        in_specs=waiting(after) + [full(array.shape) for array in operands],
        out_specs=[full(shape.shape) for shape in shapes],
        out_shape=shapes,
        compiler_params=params(VMEM),
        cost_estimate=cost(1),
        name="join",
    )(*after, *operands)
    return [(left, arrays.pop(0) if left else None, arrays.pop(0)) for left in results], token


def each_window(info, block, run):
    start = pl.multiple_of(info[4 + block], UNIT)
    kind = info[4 + (info.shape[0] - 4) // 2 + block]
    for n, size in enumerate(SIZES):

        @pl.when(kind == n)
        def _():
            run(pl.ds(start, size * UNIT), size * UNIT)


def windows(segment):
    tokens = segment.shape[0]
    rows = segment.reshape(tokens // BLOCK, BLOCK)
    first = jnp.sum((segment[None] < rows[:, :1]).astype(jnp.int32), axis=1) // UNIT
    last = (jnp.sum((segment[None] <= rows[:, -1:]).astype(jnp.int32), axis=1) - 1) // UNIT
    need = last - first + 1
    kind = sum(((need > size).astype(jnp.int32) for size in SIZES[:-1]), jnp.zeros_like(need))
    size = sum(jnp.where(kind == n, size, 0).astype(jnp.int32) for n, size in enumerate(SIZES))
    return [jnp.minimum(first, tokens // UNIT - size) * UNIT, kind]


def both_heads(array):
    lane = lax.broadcasted_iota(jnp.int32, array.shape, 1)
    zero = jnp.zeros_like(array)
    return jnp.concatenate(
        [jnp.where(lane < DH, array, zero), jnp.where(lane < DH, zero, array)], axis=0
    )


def own_heads(turned):
    return jnp.concatenate([turned[:DH, :BLOCK], turned[DH:, BLOCK:]], axis=0)


def fill_segments(seg_row, seg_col):
    seg_col[...] = jnp.broadcast_to(seg_row[...].astype(F32), (UNIT, seg_row.shape[1])).T


def masked_scores(key, query, seg_col, seg_row):
    parts = [seg_col == seg_row[:, n : n + UNIT] for n in range(0, BLOCK, UNIT)]
    return jnp.where(jnp.concatenate(parts + parts, axis=1), dot_nt(key, query), NEG)


def forward_kernel(
    project, info, *refs,
):
    if project:
        x0, x1, x2, x3, wq, wk, wv, bq, bv, seg_row, *refs = refs
        q_all, k_all, v_all, *outs = refs[:8]
        o_out, lse_out = outs[3:]
        parts, first = outs[:3], 1
        xs, seg_col, qs, vt, ctx = refs[8:]
    else:
        q_all, k_all, v_all, seg_row, *refs = refs
        parts, first = refs[:1], 0
        o_out, lse_out, seg_col, qs, vt, ctx = refs[1:]
    place = info[0]
    tokens = q_all.shape[0]
    quarter = tokens // 4
    each = quarter // BLOCK

    @pl.when(pl.program_id(0) == 0)
    def _():
        if project:
            for j, ref in enumerate((x0, x1, x2, x3)):
                xs[pl.ds(pl.multiple_of((place ^ j) * quarter, quarter), quarter), :] = ref[...]
        fill_segments(seg_row, seg_col)

    if project:
        weights = jnp.concatenate([wq[...], wk[...], wv[...]], axis=1)
        projected = dot_nn(xs[...], weights)
        query = (projected[:, :PAIR] + bq[...].astype(F32)).astype(LOW)
        value = (projected[:, 2 * PAIR :] + bv[...].astype(F32)).astype(LOW)
        q_all[...] = query
        k_all[...] = projected[:, PAIR : 2 * PAIR].astype(LOW)
        v_all[...] = value
    else:
        query, value = q_all[...], v_all[...]
    qs[...] = query * jnp.asarray(SCALE, LOW)
    vt[...] = value.T

    def step(i, _):
        b = (place ^ (first + i // each)) * each + i % each
        rows = pl.ds(pl.multiple_of(b * BLOCK, BLOCK), BLOCK)
        here = pl.ds(pl.multiple_of(i * BLOCK, BLOCK), BLOCK)

        def run(window, size):
            row = seg_row[:, rows].astype(F32)
            scores = masked_scores(k_all[window, :], both_heads(qs[rows, :]), seg_col[window, :], row)
            top = jnp.max(scores, axis=0, keepdims=True)
            expo = jnp.exp(scores - top)
            total = jnp.sum(expo, axis=0, keepdims=True)
            mixed = dot_nn(vt[:, window], expo.astype(LOW)) * (1.0 / total)
            lse_out[0, pl.ds(i, 1), :] = top + jnp.log(total)
            mixed = own_heads(mixed)
            o_out[:, here] = mixed
            ctx[here, :] = mixed.T.astype(LOW)

        each_window(info, b, run)
        return 0

    lax.fori_loop(0, len(parts) * each, step, 0)
    for n, ref in enumerate(parts):
        ref[...] = ctx[n * quarter : (n + 1) * quarter, :]


def attend_forward(info, quarters, qkv_weight, query_bias, value_bias, seg):
    quarter, width = quarters[0].shape
    tokens, half = 4 * quarter, width // 2
    pairs, each = half // PAIR, quarter // BLOCK

    def weight_spec(t):
        return pl.BlockSpec((width, PAIR), lambda p, i: (0, (2 * t + i[1]) * pairs + p))

    def bias_spec():
        return pl.BlockSpec((1, PAIR), lambda p, i: (0, i[1] * pairs + p))

    col = pl.BlockSpec((tokens, PAIR), lambda p, i: (0, p))
    part = pl.BlockSpec((quarter, PAIR), lambda p, i: (0, p))

    def results(count):
        return (
            [part] * count
            + [
                pl.BlockSpec((PAIR, count * quarter), lambda p, i: (p, 0)),
                pl.BlockSpec((1, count * each, 2 * BLOCK), lambda p, i: (p, 0, 0)),
            ],
            [shaped((quarter, half), LOW)] * count
            + [
                shaped((half, count * quarter), F32),
                shaped((pairs, count * each, 2 * BLOCK), F32),
            ],
        )

    def scratch(count):
        return [
            pltpu.VMEM((tokens, UNIT), F32),
            pltpu.VMEM((tokens, PAIR), LOW),
            pltpu.VMEM((PAIR, tokens), LOW),
            pltpu.VMEM((count * quarter, PAIR), LOW),
        ]

    specs, shapes = results(3)
    query, key, value, *parts, context, lse = pl.pallas_call(
        functools.partial(forward_kernel, True),
        grid_spec=pltpu.PrefetchScalarGridSpec(
            num_scalar_prefetch=1,
            grid=(pairs,),
            in_specs=[full((quarter, width))] * 4
            + [weight_spec(0), weight_spec(1), weight_spec(2), bias_spec(), bias_spec()]
            + [full((1, tokens))],
            out_specs=[col] * 3 + specs,
            scratch_shapes=[pltpu.VMEM((tokens, width), LOW)] + scratch(3),
        ),
        out_shape=[shaped((tokens, half), LOW)] * 3 + shapes,
        compiler_params=params(VMEM),
        cost_estimate=cost(16),
        name="attend_forward",
    )(info, *quarters, qkv_weight, qkv_weight, qkv_weight, query_bias[None], value_bias[None], seg)
    specs, shapes = results(1)
    own, own_context, own_lse = pl.pallas_call(
        functools.partial(forward_kernel, False),
        grid_spec=pltpu.PrefetchScalarGridSpec(
            num_scalar_prefetch=1,
            grid=(pairs,),
            in_specs=[col] * 3 + [full((1, tokens))],
            out_specs=specs,
            scratch_shapes=scratch(1),
        ),
        out_shape=shapes,
        compiler_params=params(VMEM),
        cost_estimate=cost(5),
        name="attend_own",
    )(info, query, key, value, seg)
    return query, key, value, [own] + parts, (own_context, context), (own_lse, lse)


QKV_ORDERS = ("zyw", "zyw", "yzw")


def backward_kernel(
    n, info, q_in, k_in, v_in, o0, o1, o1b, o2, o3, o_own, o_far, lse_own, lse_far, seg_row, x_t, vec,
    dq_out, dk_out, dv_out, vec_out, w_send, w_keep,
    seg_col, qs, do, kt, dk, dv, w_rows, o_all, lse,
):
    place, core, me = info[0], info[1], info[3]
    tokens = q_in.shape[0]
    quarter = tokens // 4
    fill_segments(seg_row, seg_col)
    each = quarter // BLOCK
    o_all[:, :quarter] = o_own[...]
    o_all[:, quarter:] = o_far[...]
    lse[:each] = lse_own[0]
    lse[each:] = lse_far[0]
    for j, ref in enumerate((o0, None, o2, o3)):
        if ref is None:
            at = pl.multiple_of((place ^ 1) * quarter, quarter)
            do[pl.ds(at, quarter // 2), :] = o1[...]
            do[pl.ds(at + quarter // 2, quarter // 2), :] = o1b[...]
            continue
        do[pl.ds(pl.multiple_of((place ^ j) * quarter, quarter), quarter), :] = ref[...]
    qs[...] = q_in[...] * jnp.asarray(SCALE, LOW)
    kt[...] = k_in[...].T
    dk[...] = jnp.zeros_like(dk)
    dv[...] = jnp.zeros_like(dv)

    def step(b, _):
        start = pl.multiple_of(b * BLOCK, BLOCK)
        rows = pl.ds(start, BLOCK)

        def run(window, size):
            row = seg_row[:, rows].astype(F32)
            o_block = do[rows, :]
            query, grad = both_heads(qs[rows, :]), both_heads(o_block)
            i = (place ^ (b // each)) * each + b % each
            here = pl.ds(pl.multiple_of(i * BLOCK, BLOCK), BLOCK)
            along = o_block.T.astype(F32) * o_all[:, here]
            delta = jnp.concatenate([column_sum(along[:DH]), column_sum(along[DH:])], axis=1)
            scores = masked_scores(k_in[window, :], query, seg_col[window, :], row)
            probs = jnp.exp(scores - lse[pl.ds(i, 1), :])
            d_scores = (probs * (dot_nt(v_in[window, :], grad) - delta)).astype(LOW)
            dv[window, :] += dot_nn(probs.astype(LOW), grad)
            dk[window, :] += dot_nn(d_scores, query)
            d_query = own_heads(dot_nn(kt[:, window], d_scores)) * SCALE
            dq_out[rows, :] = d_query.T.astype(LOW)

        each_window(info, b, run)
        return 0

    lax.fori_loop(0, tokens // BLOCK, step, 0)
    dk_out[...] = dk[...].astype(LOW)
    dv_out[...] = dv[...].astype(LOW)
    vec_out[...] = vec[...]
    half = vec.shape[1] // 2
    for side in range(2):

        @pl.when(core == side)
        def _():
            cut = slice(side * half + n * PAIR, side * half + (n + 1) * PAIR)
            vec_out[10:11, cut] = column_sum(dq_out[...].astype(F32))
            vec_out[11:12, cut] = column_sum(dv_out[...].astype(F32))

    grad = jnp.concatenate([dq_out[...], dk_out[...], dv_out[...]], axis=1)
    grad = dot_nn(x_t[...], grad)
    put_rows(grad, w_rows, me, 0, QKV_ORDERS[n], w_send, w_keep)


def attend_backward(info, n, query, key, value, parts, context, lse, seg, x_t, vectors, after):
    tokens, half = query.shape
    quarter, blocks, width = tokens // 4, tokens // BLOCK, x_t.shape[0]
    col = pl.BlockSpec((tokens, PAIR), lambda p, i: (0, n))
    pairs = half // PAIR
    part = pl.BlockSpec((quarter, PAIR), lambda p, i: (0, n))
    first = pl.BlockSpec((None, quarter, PAIR), lambda p, i: (0, 0, n))
    packed = quarter // 2
    low, high = [
        pl.BlockSpec((packed, PAIR), lambda p, i, at=at: (half // packed, at * pairs + n))
        for at in range(2)
    ]
    weight = (4, width // 8, 3 * PAIR)
    dtypes = (LOW, F32)
    return pl.pallas_call(
        ordered(functools.partial(backward_kernel, n), after),
        grid_spec=pltpu.PrefetchScalarGridSpec(
            num_scalar_prefetch=1,
            grid=(1,),
            in_specs=waiting(after)
            + [col] * 3
            + [part, low, high, first, part]
            + [pl.BlockSpec((PAIR, array.shape[1]), lambda p, i: (n, 0)) for array in context]
            + [pl.BlockSpec((1,) + array.shape[1:], lambda p, i: (n, 0, 0)) for array in lse]
            + [full((1, tokens)), full((width, tokens)), full(vectors.shape)],
            out_specs=[full((tokens, PAIR))] * 3
            + [full(vectors.shape)]
            + [full(weight)] * len(dtypes),
            scratch_shapes=[
                pltpu.VMEM((tokens, UNIT), F32),
                pltpu.VMEM((tokens, PAIR), LOW),
                pltpu.VMEM((tokens, PAIR), LOW),
                pltpu.VMEM((PAIR, tokens), LOW),
                pltpu.VMEM((tokens, PAIR), F32),
                pltpu.VMEM((tokens, PAIR), F32),
                pltpu.VMEM((8, width // 8, 3 * PAIR), F32),
                pltpu.VMEM((PAIR, tokens), F32),
                pltpu.VMEM((blocks, 2 * BLOCK), F32),
            ],
        ),
        out_shape=[shaped((tokens, PAIR), LOW)] * 3
        + [shaped(vectors.shape, F32)]
        + [shaped(weight, dtype) for dtype in dtypes],
        compiler_params=params(VMEM),
        cost_estimate=cost(8),
        name="attend_backward",
    )(info, *after, query, key, value, *parts, *context, *lse, seg, x_t, vectors)


def normalise(values):
    centred = values - jnp.mean(values, axis=1, keepdims=True)
    root = lax.rsqrt(jnp.mean(centred * centred, axis=1, keepdims=True) + EPS)
    return centred * root, root


def norm_back(grad, gain, normal, root):
    e = grad * gain
    along = jnp.mean(e * normal, axis=1, keepdims=True)
    return root * (e - jnp.mean(e, axis=1, keepdims=True) - normal * along)


def store_columns(place, flipped, mine, send):
    size, count = flipped.shape[0] // 4, flipped.shape[1]
    for b in range(4):
        rel = place ^ b

        @pl.when(rel % 2 == 0)
        def _():
            mine[pl.ds(rel // 2, 1)] = flipped[b * size : (b + 1) * size][None]

        @pl.when(rel % 2 == 1)
        def _():
            rows = pl.ds(pl.multiple_of(rel // 2 * size, size), size)
            send[rows, :count] = flipped[b * size : (b + 1) * size]


def middle_forward_kernel(
    info, p0, p1, p2, p3, x_in, cot, wo, bo, g1, s1, up, bup, down, bdown, g2, s2,
    out, d_res, n1, r1, turned, act, slope, mine, send, vec,
    hid, hid_low, branch,
):
    place, core, chip = info[0], info[1], info[2]
    step = pl.program_id(0)
    quarter = p0.shape[0]

    @pl.when(step == 0)
    def _():
        first = core == 0

        def sides(a, b):
            a, b = a[...], b[...]
            return jnp.concatenate([jnp.where(first, a, b), jnp.where(first, b, a)], axis=1)

        ctx = jnp.concatenate([sides(p0, p1), sides(p2, p3)], axis=0)
        turned[1] = ctx.T
        x = jnp.concatenate([x_in[chip], x_in[1 - chip]], axis=0).astype(F32)
        summed = x + dot_nn(ctx, wo[...]) + bo[...].astype(F32)
        normal, root = normalise(summed)
        n1[...] = normal
        r1[...] = root
        hidden = normal * g1[...].astype(F32) + s1[...].astype(F32)
        hid[...] = hidden
        low = hidden.astype(LOW)
        hid_low[...] = low
        turned[0] = low.T
        branch[...] = jnp.zeros_like(branch)

    size = hid.shape[0] // CHUNKS
    chunks = [slice(n * size, (n + 1) * size) for n in range(CHUNKS)]
    pres = [dot_nn(hid_low[rows, :], up[...]) + bup[...].astype(F32) for rows in chunks]
    for rows, pre in zip(chunks, pres):
        phi = 0.5 + 0.5 * lax.erf(pre * ROOT_HALF)
        low = (pre * phi).astype(LOW)
        act[rows, :] = low
        slope[rows, :] = phi + pre * (jnp.exp(-0.5 * pre * pre) * ROOT_TWO_PI)
        branch[rows, :] += dot_nn(low, down[...])

    @pl.when(step == pl.num_programs(0) - 1)
    def _():
        normal, root = normalise(hid[...] + branch[...] + bdown[...].astype(F32))
        final = (normal * g2[...].astype(F32) + s2[...].astype(F32)).astype(LOW)
        out[pl.ds(chip, 1)] = final[:quarter][None]
        out[pl.ds(1 - chip, 1)] = final[quarter:][None]
        grad = jnp.concatenate([cot[chip], cot[1 - chip]], axis=0).astype(F32)
        back = norm_back(grad, g2[...].astype(F32), normal, root)
        d_res[...] = back
        vec[0:1, :] = column_sum(back)
        vec[1:2, :] = column_sum(grad * normal)
        vec[2:3, :] = column_sum(grad)
        store_columns(place, back.astype(LOW).T, mine, send)


def mark_kernel(*refs):
    refs[-1][...] = jnp.zeros_like(refs[-1])


def mark(*after):
    return pl.pallas_call(
        mark_kernel,
        grid=(1,),
        in_specs=waiting(after),
        out_specs=full((8, 128)),
        out_shape=shaped((8, 128), F32),
        compiler_params=params(VMEM),
        cost_estimate=cost(1),
        name="mark",
    )(*after)


def middle_forward(after, info, parts, inputs, cotangent, wo, bo, g1, s1, up, bup, down, bdown, g2, s2):
    quarter, half = parts[0].shape
    width, inner = 2 * half, up.shape[1]
    count, steps = 2 * quarter, 4
    chunk = inner // steps
    vector = full((1, width))
    tokens = full((count, width))
    turned = full((2, width // 4, count))
    return pl.pallas_call(
        ordered(middle_forward_kernel, after),
        grid_spec=pltpu.PrefetchScalarGridSpec(
            num_scalar_prefetch=1,
            grid=(steps,),
            in_specs=waiting(after)
            + [full((quarter, half))] * 4
            + [full((2, quarter, width))] * 2
            + [full((width, width)), vector, vector, vector]
            + [
                pl.BlockSpec((width, chunk), lambda c, i: (0, c)),
                pl.BlockSpec((1, chunk), lambda c, i: (0, c)),
                pl.BlockSpec((chunk, width), lambda c, i: (c, 0)),
            ]
            + [vector] * 3,
            out_specs=[full((2, quarter, width)), tokens, tokens, full((count, 1))]
            + [full((2, width, count))]
            + [pl.BlockSpec((count, chunk), lambda c, i: (0, c))] * 2
            + [turned, full((width // 2, count)), full((8, width))],
            scratch_shapes=[
                pltpu.VMEM((count, width), F32),
                pltpu.VMEM((count, width), LOW),
                pltpu.VMEM((count, width), F32),
            ],
        ),
        out_shape=[
            shaped((2, quarter, width), LOW),
            shaped((count, width), F32),
            shaped((count, width), F32),
            shaped((count, 1), F32),
            shaped((2, width, count), LOW),
            shaped((count, inner), LOW),
            shaped((count, inner), F32),
            shaped((2, width // 4, count), LOW),
            shaped((width // 2, count), LOW),
            shaped((8, width), F32),
        ],
        compiler_params=params(VMEM),
        cost_estimate=cost(18),
        name="middle_forward",
    )(
        info, *after, *parts, inputs, cotangent, wo, bo[None], g1[None], s1[None],
        up, bup[None], down, bdown[None], g2[None], s2[None],
    )


def middle_backward_kernel(
    info, d_res, slope, down, up, wo, n1, r1, g1, vec_two,
    to_core, mine_pre, d_summed, q0, to_chip, mine, vec,
    d_branch, d_hidden,
):
    place, core = info[0], info[1]
    step = pl.program_id(0)
    quarter = q0.shape[0]
    half = q0.shape[1]
    count = d_res.shape[0]

    @pl.when(step == 0)
    def _():
        d_branch[...] = d_res[...].astype(LOW)
        d_hidden[...] = d_res[...]

    d_pre = (dot_nt(d_branch[...], down[...]) * slope[...]).astype(LOW)
    block = place ^ (1 - step // 2 + 2 * (step % 2))
    vec[pl.ds(6 + block, 1), :] = column_sum(d_pre.astype(F32))
    d_hidden[...] += dot_nt(d_pre, up[...])

    @pl.when(step < 2)
    def _():
        at = pl.multiple_of((1 + step) * count, count)
        to_core[pl.ds(at, count), :] = d_pre

    @pl.when(step >= 2)
    def _():
        mine_pre[0] = d_pre

    @pl.when(step == pl.num_programs(0) - 1)
    def _():
        grad = d_hidden[...]
        normal = n1[...]
        back = norm_back(grad, g1[...].astype(F32), normal, r1[...])
        d_summed[...] = back
        vec[3:6, :] = vec_two[0:3, :]
        vec[10:16, :] = jnp.zeros_like(vec[10:16, :])
        vec[0:1, :] = column_sum(back)
        vec[1:2, :] = column_sum(grad * normal)
        vec[2:3, :] = column_sum(grad)
        low = back.astype(LOW)
        store_columns(place, low.T, mine, to_core)
        d_ctx = dot_nt(low, wo[...]).astype(LOW)
        first = core == 0
        left, right = d_ctx[:, :half], d_ctx[:, half:]
        same = jnp.where(first, left, right)
        other = jnp.where(first, right, left)
        q0[...] = same[:quarter]
        packed = quarter // 2
        to_core[half : half + packed, :] = jnp.concatenate(
            [other[:packed], other[packed:quarter]], axis=1
        )
        to_chip[0] = same[quarter:]
        to_chip[1] = other[quarter:]


def middle_backward(info, d_res, slope, down, up, wo, n1, r1, g1, vec_two):
    count, width = d_res.shape
    inner, quarter, half = up.shape[1], count // 2, width // 2
    steps = 4
    chunk = inner // steps

    def block(c, i):
        return i[0] ^ (1 - c // 2 + 2 * (c % 2))

    tokens = full((count, width))
    turned = full((2, width // 4, count))
    return pl.pallas_call(
        middle_backward_kernel,
        grid_spec=pltpu.PrefetchScalarGridSpec(
            num_scalar_prefetch=1,
            grid=(steps,),
            in_specs=[
                tokens,
                pl.BlockSpec((count, chunk), lambda c, i: (0, block(c, i))),
                pl.BlockSpec((chunk, width), lambda c, i: (block(c, i), 0)),
                pl.BlockSpec((width, chunk), lambda c, i: (0, block(c, i))),
                full((width, width)),
                tokens,
                full((count, 1)),
                full((1, width)),
                full(vec_two.shape),
            ],
            out_specs=[
                full((3 * count, width)),
                pl.BlockSpec((1, count, chunk), lambda c, i: (jnp.maximum(c - 2, 0), 0, 0)),
                tokens,
            ]
            + [full((quarter, half)), full((2, quarter, half)), turned, full((16, width))],
            scratch_shapes=[pltpu.VMEM((count, width), LOW), pltpu.VMEM((count, width), F32)],
        ),
        out_shape=[
            shaped((3 * count, width), LOW),
            shaped((2, count, chunk), LOW),
            shaped((count, width), F32),
        ]
        + [
            shaped((quarter, half), LOW),
            shaped((2, quarter, half), LOW),
            shaped((2, width // 4, count), LOW),
            shaped((16, width), F32),
        ],
        compiler_params=params(VMEM),
        cost_estimate=cost(16),
        name="middle_backward",
    )(info, d_res, slope, down, up, wo, n1, r1, g1[None], vec_two)


DOWN_ORDERS = ("zxwy", "xzwy")


def down_kernel(info, mine, theirs, act, act_pair, *outs):
    rel = pl.program_id(0)
    left = jnp.concatenate([mine[0], mine[1]], axis=0)
    grad = dot_nn(left, act[...]) + dot_nn(theirs[...], act_pair[...])
    size = grad.shape[0] // 4
    for n, order in enumerate(DOWN_ORDERS):
        for flip in range(2):
            start = (2 * flip + n) * size
            put(grad[start : start + size], rel, flip, order, outs[2 * n], outs[2 * n + 1])


def down_grad(info, mine, theirs, act, act_pair, after):
    _, size, count = mine.shape
    block = act.shape[1] // 8
    part = (8, size // 2, block)
    spec = pl.BlockSpec((count, block), lambda r, i: (0, r ^ i[3]))
    return pl.pallas_call(
        ordered(down_kernel, after),
        grid_spec=pltpu.PrefetchScalarGridSpec(
            num_scalar_prefetch=1,
            grid=(8,),
            in_specs=waiting(after) + [full(mine.shape), full(theirs.shape), spec, spec],
            out_specs=[full(part)] * 4,
        ),
        out_shape=[shaped(part, LOW), shaped(part, F32)] * 2,
        compiler_params=params(VMEM),
        cost_estimate=cost(8),
        name="down_grad",
    )(info, *after, mine, theirs, act, act_pair)


UP_ORDERS = ("xyzw", "yxwz")


def up_kernel(
    info, left, left_pair, mine, theirs, mine_d, theirs_d, send_a, keep_a, send_b, keep_b, rows
):
    me = info[3]
    step = pl.program_id(0)

    @pl.when(step < 4)
    def _():
        grad = dot_nn(left[0], mine[0]) + dot_nn(left_pair[0], theirs[...])
        for n, flip in ((0, 0), (1, 0), (0, 1), (1, 1)):

            @pl.when(step == 2 * flip + n)
            def _():
                send, keep = ((send_a, keep_a), (send_b, keep_b))[n]
                put_rows(grad, rows, me, flip, UP_ORDERS[n], send, keep)

    @pl.when(step == 4)
    def _():
        right = jnp.concatenate([mine_d[0], mine_d[1]], axis=0)
        grad = dot_nt(left[1], right) + dot_nt(left_pair[1], theirs_d[...])
        deep, wide = grad.shape[0] // 8, grad.shape[1] // 2
        for b in range(8):
            rows[b] = grad[b * deep : (b + 1) * deep]
        for rel in range(4):
            near, far = rows[me ^ rel], rows[me ^ (rel + 4)]
            for flip in range(2):
                cut = slice(flip * wide, (flip + 1) * wide)
                value = jnp.concatenate([near[:, cut], far[:, cut]], axis=1)
                index = 8 + 2 * flip + rel // 2
                if rel % 2:
                    send_b[index] = value.astype(LOW)
                else:
                    keep_b[index] = value


def up_grad(info, left, left_pair, mine, from_core, mine_d, after):
    _, width, count = left.shape
    half = width // 2

    def at(s):
        return jnp.minimum(s, 3)

    shapes = [
        shaped((lead, width // 8, half), dtype) for lead in (8, 12) for dtype in (LOW, F32)
    ]
    return pl.pallas_call(
        ordered(up_kernel, after),
        grid_spec=pltpu.PrefetchScalarGridSpec(
            num_scalar_prefetch=1,
            grid=(5,),
            in_specs=waiting(after)
            + [full(left.shape)] * 2
            + [
                pl.BlockSpec((1, count, half), lambda s, i: (at(s) // 2, 0, at(s) % 2)),
                pl.BlockSpec((count, half), lambda s, i: (1 + at(s) // 2, at(s) % 2)),
                full(mine_d.shape),
                pl.BlockSpec((half, count), lambda s, i: (0, 0)),
            ],
            out_specs=[full(shape.shape) for shape in shapes],
            scratch_shapes=[pltpu.VMEM((8, width // 8, half), F32)],
        ),
        out_shape=shapes,
        compiler_params=params(VMEM),
        cost_estimate=cost(10),
        name="up_grad",
    )(info, *after, left, left_pair, mine, from_core, mine_d, from_core)


def input_kernel(info, *refs):
    grads, weights, (near, far, send) = refs[:9], refs[9:12], refs[12:]
    rel = pl.program_id(0)
    total = sum(
        dot_nt(jnp.concatenate([ref[...] for ref in grads[t::3]], axis=1), weights[t][...])
        for t in range(3)
    )

    @pl.when(rel < 2)
    def _():
        send[0] = total

    @pl.when(rel == 2)
    def _():
        near[...] = total

    @pl.when(rel == 3)
    def _():
        far[...] = total


def input_part(info, grads, qkv_weight, after):
    tokens = grads[0].shape[0]
    width = qkv_weight.shape[0]
    quarter, half = tokens // 4, width // 2

    rows = pl.BlockSpec((quarter, PAIR), lambda c, i: (i[0] ^ (1 - c // 2 + 2 * (c % 2)), 0))

    def weight(t):
        return pl.BlockSpec((width, half), lambda c, i: (0, 2 * t + i[1]))

    return pl.pallas_call(
        ordered(input_kernel, after),
        grid_spec=pltpu.PrefetchScalarGridSpec(
            num_scalar_prefetch=1,
            grid=(4,),
            in_specs=waiting(after) + [rows] * 9 + [weight(0), weight(1), weight(2)],
            out_specs=[
                full((quarter, width)),
                full((quarter, width)),
                pl.BlockSpec((1, quarter, width), lambda c, i: (jnp.minimum(c, 1), 0, 0)),
            ],
        ),
        out_shape=[shaped((quarter, width), F32)] * 2 + [shaped((2, quarter, width), F32)],
        compiler_params=params(VMEM),
        cost_estimate=cost(6),
        name="input_part",
    )(info, *after, *grads, qkv_weight, qkv_weight, qkv_weight)


UNITS = (((0, 1), (2, 3), (4,), (5,)), ((0,), (1,), (2, 3), (4, 5)))


def share_kernel(info, zero, first, kept, got, own, one, two, three):
    place, core = info[0], info[1]
    total = [zero[zero.shape[0] - 1], first[first.shape[0] - 1], kept[0] + got[0].astype(F32)]
    units = []
    for t in range(3):
        part = jnp.concatenate([pair[:, t * PAIR : (t + 1) * PAIR] for pair in total], axis=1)
        units += jnp.split(part, 2, axis=1)
    for side in range(2):
        for target in range(4):
            for flip, ref in enumerate((own, one, two, three)):

                @pl.when(jnp.logical_and(core == side, place ^ target == flip))
                def _():
                    for n in range(2):
                        unit = units[UNITS[side][target][n % len(UNITS[side][target])]]
                        ref[n] = unit.astype(ref.dtype)


def share(info, zero, one, kept, got, after):
    unit = (2, got.shape[1], got.shape[2] // 2)
    return pl.pallas_call(
        ordered(share_kernel, after),
        grid_spec=pltpu.PrefetchScalarGridSpec(
            num_scalar_prefetch=1,
            grid=(1,),
            in_specs=waiting(after)
            + [full(array.shape) for array in (zero, one, kept, got)],
            out_specs=[full(unit)] * 4,
        ),
        out_shape=[shaped(unit, F32)] + [shaped(unit, LOW)] * 3,
        compiler_params=params(VMEM),
        cost_estimate=cost(1),
        name="share",
    )(info, *after, zero, one, kept, got)


def gather_kernel(info, own, one, two, three, out):
    place = info[0]
    same = own[...] + two[...].astype(F32)
    other = one[...].astype(F32) + three[...].astype(F32)
    for target in range(4):

        @pl.when(place == target)
        def _():
            sides = (same, other) if target % 2 == 0 else (other, same)
            pieces = [
                (side_unit, sides[side][n])
                for side in range(2)
                for n, side_unit in enumerate(
                    unit % 2 + 4 * (unit // 2) + 2 * side for unit in UNITS[side][target]
                )
            ]
            pieces.sort(key=lambda piece: piece[0])
            out[...] = jnp.concatenate([piece[1] for piece in pieces], axis=1)


def gather(info, own, *others):
    shape = (own.shape[1], 3 * own.shape[2])
    return pl.pallas_call(
        gather_kernel,
        grid_spec=pltpu.PrefetchScalarGridSpec(
            num_scalar_prefetch=1,
            grid=(1,),
            in_specs=[full(own.shape)] * 4,
            out_specs=full(shape),
        ),
        out_shape=shaped(shape, F32),
        compiler_params=params(VMEM),
        cost_estimate=cost(1),
        name="gather",
    )(info, own, *others)


def turn_kernel(info, x0, x1, x2, x3, x_t):
    quarter = x0.shape[0]
    for j, ref in enumerate((x0, x1, x2, x3)):
        at = pl.multiple_of((info[0] ^ j) * quarter, quarter)
        x_t[:, pl.ds(at, quarter)] = ref[...].T


def turn(info, quarters):
    quarter, width = quarters[0].shape
    return pl.pallas_call(
        turn_kernel,
        grid_spec=pltpu.PrefetchScalarGridSpec(
            num_scalar_prefetch=1,
            grid=(1,),
            in_specs=[full((quarter, width))] * 4,
            out_specs=full((width, 4 * quarter)),
        ),
        out_shape=shaped((width, 4 * quarter), LOW),
        compiler_params=params(VMEM),
        cost_estimate=cost(1),
        name="turn",
    )(info, *quarters)


def body(
    inputs,
    segments,
    qkv_weight,
    query_bias,
    value_bias,
    out_weight,
    out_bias,
    norm1_gain,
    norm1_shift,
    up_weight,
    up_bias,
    down_weight,
    down_bias,
    norm2_gain,
    norm2_shift,
    cotangent,
):
    rows, quarter, width = inputs.shape
    half = width // 2
    seq_size = lax.axis_size("seq")
    batch_size = lax.axis_size("batch")
    fine = batch_size // 8
    place = lax.axis_index("seq")
    chip, core = place // 2, place % 2
    segment = lax.dynamic_index_in_dim(segments, chip, 0)
    info = jnp.stack([place, core, chip, lax.axis_index("batch") // fine]).astype(jnp.int32)
    info = jnp.concatenate([info] + windows(segment[0]))

    def over_seq(array, flip):
        return lax.ppermute(array, "seq", [(i, i ^ flip) for i in range(seq_size)])

    def over_batch(array, flip):
        return lax.ppermute(array, "batch", [(i, i ^ flip) for i in range(batch_size)])

    def swap(array, axis):
        if axis == "x":
            return over_seq(array, 2)
        return over_batch(array, fine << "yzw".index(axis))

    def pick(array, index, axis=0):
        return lax.dynamic_index_in_dim(array, index, axis, keepdims=False)

    def tie(*arrays):
        return lax.optimization_barrier(arrays)

    def launch(*messages):
        return [
            (order, segments, kept, swap(sent, order[0]))
            for order, segments, sent, kept in messages
        ]

    def land(after, flights, *routes, fresh=()):
        made, token = join(
            [flight[1:] for flight in flights], [route[1:] for route in routes], after, fresh
        )
        return [(route[0],) + new for route, new in zip(routes, made)], token

    def finish(grad):
        if fine > 1:
            groups = [[i * fine + j for j in range(fine)] for i in range(8)]
            grad = lax.psum_scatter(
                grad, "batch", scatter_dimension=0, axis_index_groups=groups, tiled=True
            )
        return grad

    own = pick(inputs, chip)
    far = over_seq(pick(inputs, 1 - chip), 2)
    near = over_seq(own, 1)
    across = over_seq(far, 1)
    quarters = (own, near, far, across)

    query, key, value, parts, context, lse = attend_forward(
        info, quarters, qkv_weight, query_bias, value_bias, segment
    )
    parts = [parts[0]] + [over_seq(parts[j], j) for j in (1, 2, 3)]
    x_t = turn(info, quarters)

    outputs, d_res, n1, r1, turned, act, slope, mine, send, vec_two = middle_forward(
        [x_t], info, parts, inputs, cotangent, out_weight, out_bias, norm1_gain, norm1_shift,
        up_weight, up_bias, down_weight, down_bias, norm2_gain, norm2_shift,
    )
    pair = over_seq(turned, 1), over_seq(act, 1), over_seq(send, 1)
    back = middle_backward(
        info, d_res, slope, down_weight, up_weight, out_weight, n1, r1, norm1_gain, vec_two
    )
    turned_pair, act_pair, theirs = pair
    to_core, mine_pre, d_summed, q0, to_chip, mine_d, vectors = back

    token = mark(turned_pair, act_pair, theirs, vectors)
    to_core, to_chip, token = tie(to_core, to_chip, token)
    from_core, from_chip = over_seq(to_core, 1), over_seq(to_chip, 2)
    made = down_grad(info, mine, theirs, act, act_pair, [token])
    downs = launch(
        (DOWN_ORDERS[0], [8], made[0], made[1]), (DOWN_ORDERS[1], [8], made[2], made[3])
    )
    across = over_seq(from_chip[1], 1)
    made = up_grad(info, turned, turned_pair, mine_pre, from_core, mine_d, [made[1]])
    ups = launch((UP_ORDERS[0], [8], made[0], made[1]), (UP_ORDERS[1], [8, 4], made[2], made[3]))
    d_parts = (q0, from_core, from_core, from_chip, across)

    def piece(n, vectors, after):
        made = attend_backward(
            info, n, query, key, value, d_parts, context, lse, segment, x_t, vectors, after
        )
        return list(made)

    def opening(n, made, token):
        sent, token = tie(made[4], token)
        return (QKV_ORDERS[n], [4], sent, made[5]), token

    zero = piece(0, vectors, [made[1]])
    downs, token = land(
        zero[3:4],
        downs,
        (DOWN_ORDERS[0][1:], (0, 0)),
        (DOWN_ORDERS[1][1:], (1, 0)),
    )
    opened, token = opening(0, zero, token)
    *downs, first = launch(*downs, opened)

    one = piece(1, zero[3], [token])
    (up_a, up_b, down), token = land(
        one[3:4],
        ups + downs + [first],
        (UP_ORDERS[0][1:], (0, 0), (4, 0)),
        (UP_ORDERS[1][1:], (1, 0), (1, 1)),
        ("wy", (2, 0), (3, 0)),
    )
    opened, token = opening(1, one, token)
    flights = launch(up_a, up_b, down, opened)

    two = piece(2, one[3], [token])
    (up_a, up_b, others), token = land(
        two[3:4],
        flights,
        ("zw", (0, 0), (1, 1)),
        ("wz", (1, 0), (0, 1)),
        ("y", (2, 0), (2, 1), (3, 0), (4, 0)),
        fresh=[two[4:6]],
    )
    grads = [*zero[:3], *one[:3], *two[:3]]
    vectors, token = tie(two[3], token)
    flights = launch(others, up_a, up_b)
    vectors_got = over_seq(vectors, 1)

    near, far, send = input_part(info, grads, qkv_weight, [token])
    (up_a, up_b, down), token = land(
        [near],
        flights,
        ("w", (1, 0), (0, 2), (1, 1)),
        ("z", (2, 0), (0, 3)),
        ("", (0, 0), (0, 1), (2, 1)),
    )
    down_total = down[3]
    up_a, up_b = launch(up_a, up_b)
    send, vectors_got, token = tie(send, vectors_got, token)
    d_row_got = over_seq(send, 1)
    far = (far + d_row_got[1]).astype(LOW)
    d_far = over_seq(far, 2)
    vectors = vectors + vectors_got
    vectors = vectors + over_seq(vectors, 2)
    vectors = vectors + swap(vectors, "y")
    (up, third), token = land(
        [token, vectors, far],
        [up_a, up_b],
        ("", (0, 0), (1, 0), (0, 2), (0, 1)),
        ("w", (1, 1)),
    )
    up_total = up[3]
    wide = half // 2
    vectors, token = tie(vectors, token)
    (third,) = launch(third)
    vectors_got = swap(vectors, "z")
    own, *others = share(info, down[3], up[3], third[2], third[3], [token, vectors_got, d_far])
    vectors_got, own = tie(vectors_got, own)
    vectors = vectors + vectors_got
    qkv_total = gather(info, own, *[over_seq(other, 1 + j) for j, other in enumerate(others)])
    qkv_total = finish(qkv_total)
    out_total = finish(up_total[2, :, :wide])
    down_total = finish(down_total[:2].reshape(wide, half).T)
    up_total = finish(jnp.concatenate([up_total[0], up_total[1]], axis=1))

    vectors = vectors + swap(vectors, "w")
    flip = 1
    while flip < fine:
        vectors = vectors + over_batch(vectors, flip)
        flip *= 2
    d_near = d_summed[:quarter] + (near + d_row_got[0])
    d_far = d_summed[quarter:] + d_far.astype(F32)
    d_inputs = jnp.stack([jnp.where(chip == 0, d_near, d_far), jnp.where(chip == 0, d_far, d_near)])
    return (
        outputs,
        d_inputs,
        qkv_total,
        vectors[10],
        vectors[11],
        out_total,
        vectors[0],
        vectors[1],
        vectors[2],
        up_total,
        vectors[6:10].reshape(-1),
        down_total,
        vectors[3],
        vectors[4],
        vectors[5],
    )


def solution(mesh):
    whole, split = P(), P("batch", "seq")
    tokens = P("batch", "seq", None)
    return jax.shard_map(
        body,
        mesh=mesh,
        in_specs=(tokens, P("batch", None)) + (whole,) * 13 + (tokens,),
        out_specs=(tokens, tokens, split, whole, whole, split)
        + (whole,) * 3
        + (split, whole, split)
        + (whole,) * 3,
        check_vma=False,
    )
```

```python
import functools

import jax
import jax.numpy as jnp
from jax import lax
from jax.experimental import pallas as pl
from jax.experimental.pallas import tpu as pltpu
from jax.sharding import PartitionSpec as P

DH = 64
EPS = 1e-05
NEG = -1000000000.0
F32 = jnp.float32
LOW = jnp.bfloat16
PAIR = 2 * DH
SCALE = DH**-0.5
BLOCK = 256
UNIT = 128
WINDOWED = (0, 2)
SIZES = (5, 8)
VMEM = 18
CHUNKS = 2
ROOT_HALF = 0.5**0.5
ROOT_TWO_PI = 0.3989422804014327


def shaped(shape, dtype):
    return jax.ShapeDtypeStruct(shape, dtype)


def dot_nn(left, right):
    return jnp.dot(left, right, preferred_element_type=F32)


def dot_nt(left, right):
    return lax.dot_general(left, right, (((1,), (1,)), ((), ())), preferred_element_type=F32)


def params(mib):
    return pltpu.CompilerParams(vmem_limit_bytes=mib << 20, dimension_semantics=("arbitrary",))


def waiting(after):
    return [pl.BlockSpec(memory_space=pl.ANY)] * len(after)


def ordered(kernel, after):
    return lambda info, *refs: kernel(info, *refs[len(after) :])


def full(shape):
    return pl.BlockSpec(shape, lambda *_: (0,) * len(shape))


def cost(micros):
    return pl.CostEstimate(flops=int(micros * 0.6e9), transcendentals=0, bytes_accessed=0)


def column_sum(values):
    return jnp.sum(values, axis=0, keepdims=True)


def spot(rel, flip_x, order):
    bits = {"y": rel % 2, "z": (rel // 2) % 2, "w": rel // 4, "x": flip_x}
    index = 0
    for axis in order[1:]:
        index = index * 2 + bits[axis]
    return bits[order[0]], index


def put(value, rel, flip_x, order, send, keep):
    sent, index = spot(rel, flip_x, order)

    @pl.when(sent == 1)
    def _():
        send[pl.ds(index, 1)] = value.astype(LOW)[None]

    @pl.when(sent == 0)
    def _():
        keep[pl.ds(index, 1)] = value[None]


def put_rows(grad, rows, me, flip_x, order, send, keep):
    deep = grad.shape[0] // 8
    for b in range(8):
        rows[b] = grad[b * deep : (b + 1) * deep]
    for rel in range(8):
        sent, index = spot(rel, flip_x, order)
        value = rows[me ^ rel]
        if sent:
            send[index] = value.astype(LOW)
        else:
            keep[index] = value


def leaves(segments, route):
    return any(m >= len(segments) or segments[m][n] > 1 for m, n in route)


def join_kernel(skip, segments, fresh, routes, *refs):
    refs = refs[skip:]
    count = 2 * len(segments)
    ins, new = refs[:count], refs[count : count + 2 * fresh]
    outs = list(refs[count + 2 * fresh : -1])
    refs[-1][...] = jnp.zeros_like(refs[-1])
    for route in routes:
        more = leaves(segments, route)
        send = outs.pop(0) if more else None
        keep = outs.pop(0)
        sent = filled = 0
        for m, n in route:
            if m >= len(segments):
                at = 2 * (m - len(segments))
                size = new[at].shape[0]
                send[sent : sent + size] = new[at][...]
                keep[filled : filled + size] = new[at + 1][...]
                sent += size
                filled += size
                continue
            start, size = sum(segments[m][:n]), segments[m][n]
            total = ins[2 * m][start : start + size]
            total = total + ins[2 * m + 1][start : start + size].astype(F32)
            if size > 1:
                size //= 2
                send[sent : sent + size] = total[size:].astype(LOW)
                sent += size
            elif more:
                wide = total.shape[2] // 2
                turned = jnp.concatenate([total[0, :, wide:], total[0, :, :wide]], axis=1)
                send[sent] = turned.astype(LOW)
                sent += 1
            keep[filled : filled + size] = total[:size]
            filled += size


def join(messages, routes, after, fresh):
    segments = [list(message[0]) for message in messages]
    tail = messages[0][1].shape[1:]
    shapes, results = [], []
    for route in routes:
        left = [
            fresh[m - len(segments)][0].shape[0]
            if m >= len(segments)
            else max(segments[m][n] // 2, 1)
            for m, n in route
        ]
        more = leaves(segments, route)
        results.append(left if more else [])
        if more:
            shapes.append(shaped((sum(left),) + tail, LOW))
        shapes.append(shaped((sum(left),) + tail, F32))
    operands = [array for message in messages for array in message[1:]]
    operands += [array for pair in fresh for array in pair]
    shapes.append(shaped((8, 128), F32))
    *arrays, token = pl.pallas_call(
        functools.partial(join_kernel, len(after), segments, len(fresh), routes),
        grid=(1,),
        in_specs=waiting(after) + [full(array.shape) for array in operands],
        out_specs=[full(shape.shape) for shape in shapes],
        out_shape=shapes,
        compiler_params=params(VMEM),
        cost_estimate=cost(1),
        name="join",
    )(*after, *operands)
    return [(left, arrays.pop(0) if left else None, arrays.pop(0)) for left in results], token


def each_window(info, block, run):
    start = pl.multiple_of(info[4 + block], UNIT)
    kind = info[4 + (info.shape[0] - 4) // 2 + block]
    for n, size in enumerate(SIZES):

        @pl.when(kind == n)
        def _():
            run(pl.ds(start, size * UNIT), size * UNIT)


def windows(segment):
    tokens = segment.shape[0]
    rows = segment.reshape(tokens // BLOCK, BLOCK)
    first = jnp.sum((segment[None] < rows[:, :1]).astype(jnp.int32), axis=1) // UNIT
    last = (jnp.sum((segment[None] <= rows[:, -1:]).astype(jnp.int32), axis=1) - 1) // UNIT
    need = last - first + 1
    kind = sum(((need > size).astype(jnp.int32) for size in SIZES[:-1]), jnp.zeros_like(need))
    size = sum(jnp.where(kind == n, size, 0).astype(jnp.int32) for n, size in enumerate(SIZES))
    return [jnp.minimum(first, tokens // UNIT - size) * UNIT, kind]


def both_heads(array):
    lane = lax.broadcasted_iota(jnp.int32, array.shape, 1)
    zero = jnp.zeros_like(array)
    return jnp.concatenate(
        [jnp.where(lane < DH, array, zero), jnp.where(lane < DH, zero, array)], axis=0
    )


def own_heads(turned):
    return jnp.concatenate([turned[:DH, :BLOCK], turned[DH:, BLOCK:]], axis=0)


def fill_segments(seg_row, seg_col):
    seg_col[...] = jnp.broadcast_to(seg_row[...].astype(F32), (UNIT, seg_row.shape[1])).T


def masked_scores(key, query, seg_col, seg_row):
    parts = [seg_col == seg_row[:, n : n + UNIT] for n in range(0, BLOCK, UNIT)]
    return jnp.where(jnp.concatenate(parts + parts, axis=1), dot_nt(key, query), NEG)


def forward_kernel(
    project, info, *refs,
):
    if project:
        x0, x1, x2, x3, wq, wk, wv, bq, bv, seg_row, *refs = refs
        q_all, k_all, v_all, *outs = refs[:8]
        o_out, lse_out = outs[3:]
        parts, first = outs[:3], 1
        xs, seg_col, qs, vt, ctx = refs[8:]
    else:
        q_all, k_all, v_all, seg_row, *refs = refs
        parts, first = refs[:1], 0
        o_out, lse_out, seg_col, qs, vt, ctx = refs[1:]
    place = info[0]
    tokens = q_all.shape[0]
    quarter = tokens // 4
    each = quarter // BLOCK

    @pl.when(pl.program_id(0) == 0)
    def _():
        if project:
            for j, ref in enumerate((x0, x1, x2, x3)):
                xs[pl.ds(pl.multiple_of((place ^ j) * quarter, quarter), quarter), :] = ref[...]
        fill_segments(seg_row, seg_col)

    if project:
        weights = jnp.concatenate([wq[...], wk[...], wv[...]], axis=1)
        projected = dot_nn(xs[...], weights)
        query = (projected[:, :PAIR] + bq[...].astype(F32)).astype(LOW)
        value = (projected[:, 2 * PAIR :] + bv[...].astype(F32)).astype(LOW)
        q_all[...] = query
        k_all[...] = projected[:, PAIR : 2 * PAIR].astype(LOW)
        v_all[...] = value
    else:
        query, value = q_all[...], v_all[...]
    qs[...] = query * jnp.asarray(SCALE, LOW)
    vt[...] = value.T

    def step(i, _):
        b = (place ^ (first + i // each)) * each + i % each
        rows = pl.ds(pl.multiple_of(b * BLOCK, BLOCK), BLOCK)
        here = pl.ds(pl.multiple_of(i * BLOCK, BLOCK), BLOCK)

        def run(window, size):
            row = seg_row[:, rows].astype(F32)
            scores = masked_scores(k_all[window, :], both_heads(qs[rows, :]), seg_col[window, :], row)
            top = jnp.max(scores, axis=0, keepdims=True)
            expo = jnp.exp(scores - top)
            total = jnp.sum(expo, axis=0, keepdims=True)
            mixed = dot_nn(vt[:, window], expo.astype(LOW)) * (1.0 / total)
            lse_out[0, pl.ds(i, 1), :] = top + jnp.log(total)
            mixed = own_heads(mixed)
            o_out[:, here] = mixed
            ctx[here, :] = mixed.T.astype(LOW)

        if project:
            each_window(info, b, run)
        else:
            run(pl.ds(0, tokens), tokens)
        return 0

    lax.fori_loop(0, len(parts) * each, step, 0)
    for n, ref in enumerate(parts):
        ref[...] = ctx[n * quarter : (n + 1) * quarter, :]


def attend_forward(info, quarters, qkv_weight, query_bias, value_bias, seg):
    quarter, width = quarters[0].shape
    tokens, half = 4 * quarter, width // 2
    pairs, each = half // PAIR, quarter // BLOCK

    def weight_spec(t):
        return pl.BlockSpec((width, PAIR), lambda p, i: (0, (2 * t + i[1]) * pairs + p))

    def bias_spec():
        return pl.BlockSpec((1, PAIR), lambda p, i: (0, i[1] * pairs + p))

    col = pl.BlockSpec((tokens, PAIR), lambda p, i: (0, p))
    part = pl.BlockSpec((quarter, PAIR), lambda p, i: (0, p))

    def results(count):
        return (
            [part] * count
            + [
                pl.BlockSpec((PAIR, count * quarter), lambda p, i: (p, 0)),
                pl.BlockSpec((1, count * each, 2 * BLOCK), lambda p, i: (p, 0, 0)),
            ],
            [shaped((quarter, half), LOW)] * count
            + [
                shaped((half, count * quarter), F32),
                shaped((pairs, count * each, 2 * BLOCK), F32),
            ],
        )

    def scratch(count):
        return [
            pltpu.VMEM((tokens, UNIT), F32),
            pltpu.VMEM((tokens, PAIR), LOW),
            pltpu.VMEM((PAIR, tokens), LOW),
            pltpu.VMEM((count * quarter, PAIR), LOW),
        ]

    specs, shapes = results(3)
    query, key, value, *parts, context, lse = pl.pallas_call(
        functools.partial(forward_kernel, True),
        grid_spec=pltpu.PrefetchScalarGridSpec(
            num_scalar_prefetch=1,
            grid=(pairs,),
            in_specs=[full((quarter, width))] * 4
            + [weight_spec(0), weight_spec(1), weight_spec(2), bias_spec(), bias_spec()]
            + [full((1, tokens))],
            out_specs=[col] * 3 + specs,
            scratch_shapes=[pltpu.VMEM((tokens, width), LOW)] + scratch(3),
        ),
        out_shape=[shaped((tokens, half), LOW)] * 3 + shapes,
        compiler_params=params(VMEM),
        cost_estimate=cost(16),
        name="attend_forward",
    )(info, *quarters, qkv_weight, qkv_weight, qkv_weight, query_bias[None], value_bias[None], seg)
    specs, shapes = results(1)
    own, own_context, own_lse = pl.pallas_call(
        functools.partial(forward_kernel, False),
        grid_spec=pltpu.PrefetchScalarGridSpec(
            num_scalar_prefetch=1,
            grid=(pairs,),
            in_specs=[col] * 3 + [full((1, tokens))],
            out_specs=specs,
            scratch_shapes=scratch(1),
        ),
        out_shape=shapes,
        compiler_params=params(VMEM),
        cost_estimate=cost(5),
        name="attend_own",
    )(info, query, key, value, seg)
    return query, key, value, [own] + parts, (own_context, context), (own_lse, lse)


QKV_ORDERS = ("zyw", "zyw", "yzw")


def backward_kernel(
    n, info, q_in, k_in, v_in, o0, o1, o1b, o2, o3, o_own, o_far, lse_own, lse_far, seg_row, x_t, vec,
    dq_out, dk_out, dv_out, vec_out, w_send, w_keep,
    seg_col, qs, do, kt, dk, dv, w_rows, o_all, lse,
):
    place, core, me = info[0], info[1], info[3]
    tokens = q_in.shape[0]
    quarter = tokens // 4
    fill_segments(seg_row, seg_col)
    each = quarter // BLOCK
    o_all[:, :quarter] = o_own[...]
    o_all[:, quarter:] = o_far[...]
    lse[:each] = lse_own[0]
    lse[each:] = lse_far[0]
    for j, ref in enumerate((o0, None, o2, o3)):
        if ref is None:
            at = pl.multiple_of((place ^ 1) * quarter, quarter)
            do[pl.ds(at, quarter // 2), :] = o1[...]
            do[pl.ds(at + quarter // 2, quarter // 2), :] = o1b[...]
            continue
        do[pl.ds(pl.multiple_of((place ^ j) * quarter, quarter), quarter), :] = ref[...]
    qs[...] = q_in[...] * jnp.asarray(SCALE, LOW)
    kt[...] = k_in[...].T
    dk[...] = jnp.zeros_like(dk)
    dv[...] = jnp.zeros_like(dv)

    def step(b, _):
        start = pl.multiple_of(b * BLOCK, BLOCK)
        rows = pl.ds(start, BLOCK)

        def run(window, size):
            row = seg_row[:, rows].astype(F32)
            o_block = do[rows, :]
            query, grad = both_heads(qs[rows, :]), both_heads(o_block)
            i = (place ^ (b // each)) * each + b % each
            here = pl.ds(pl.multiple_of(i * BLOCK, BLOCK), BLOCK)
            along = o_block.T.astype(F32) * o_all[:, here]
            delta = jnp.concatenate([column_sum(along[:DH]), column_sum(along[DH:])], axis=1)
            scores = masked_scores(k_in[window, :], query, seg_col[window, :], row)
            probs = jnp.exp(scores - lse[pl.ds(i, 1), :])
            d_scores = (probs * (dot_nt(v_in[window, :], grad) - delta)).astype(LOW)
            dv[window, :] += dot_nn(probs.astype(LOW), grad)
            dk[window, :] += dot_nn(d_scores, query)
            d_query = own_heads(dot_nn(kt[:, window], d_scores)) * SCALE
            dq_out[rows, :] = d_query.T.astype(LOW)

        if n in WINDOWED:
            each_window(info, b, run)
        else:
            run(pl.ds(0, tokens), tokens)
        return 0

    lax.fori_loop(0, tokens // BLOCK, step, 0)
    dk_out[...] = dk[...].astype(LOW)
    dv_out[...] = dv[...].astype(LOW)
    vec_out[...] = vec[...]
    half = vec.shape[1] // 2
    for side in range(2):

        @pl.when(core == side)
        def _():
            cut = slice(side * half + n * PAIR, side * half + (n + 1) * PAIR)
            vec_out[10:11, cut] = column_sum(dq_out[...].astype(F32))
            vec_out[11:12, cut] = column_sum(dv_out[...].astype(F32))

    grad = jnp.concatenate([dq_out[...], dk_out[...], dv_out[...]], axis=1)
    grad = dot_nn(x_t[...], grad)
    put_rows(grad, w_rows, me, 0, QKV_ORDERS[n], w_send, w_keep)


def attend_backward(info, n, query, key, value, parts, context, lse, seg, x_t, vectors, after):
    tokens, half = query.shape
    quarter, blocks, width = tokens // 4, tokens // BLOCK, x_t.shape[0]
    col = pl.BlockSpec((tokens, PAIR), lambda p, i: (0, n))
    pairs = half // PAIR
    part = pl.BlockSpec((quarter, PAIR), lambda p, i: (0, n))
    first = pl.BlockSpec((None, quarter, PAIR), lambda p, i: (0, 0, n))
    packed = quarter // 2
    low, high = [
        pl.BlockSpec((packed, PAIR), lambda p, i, at=at: (half // packed, at * pairs + n))
        for at in range(2)
    ]
    weight = (4, width // 8, 3 * PAIR)
    dtypes = (LOW, F32)
    return pl.pallas_call(
        ordered(functools.partial(backward_kernel, n), after),
        grid_spec=pltpu.PrefetchScalarGridSpec(
            num_scalar_prefetch=1,
            grid=(1,),
            in_specs=waiting(after)
            + [col] * 3
            + [part, low, high, first, part]
            + [pl.BlockSpec((PAIR, array.shape[1]), lambda p, i: (n, 0)) for array in context]
            + [pl.BlockSpec((1,) + array.shape[1:], lambda p, i: (n, 0, 0)) for array in lse]
            + [full((1, tokens)), full((width, tokens)), full(vectors.shape)],
            out_specs=[full((tokens, PAIR))] * 3
            + [full(vectors.shape)]
            + [full(weight)] * len(dtypes),
            scratch_shapes=[
                pltpu.VMEM((tokens, UNIT), F32),
                pltpu.VMEM((tokens, PAIR), LOW),
                pltpu.VMEM((tokens, PAIR), LOW),
                pltpu.VMEM((PAIR, tokens), LOW),
                pltpu.VMEM((tokens, PAIR), F32),
                pltpu.VMEM((tokens, PAIR), F32),
                pltpu.VMEM((8, width // 8, 3 * PAIR), F32),
                pltpu.VMEM((PAIR, tokens), F32),
                pltpu.VMEM((blocks, 2 * BLOCK), F32),
            ],
        ),
        out_shape=[shaped((tokens, PAIR), LOW)] * 3
        + [shaped(vectors.shape, F32)]
        + [shaped(weight, dtype) for dtype in dtypes],
        compiler_params=params(VMEM),
        cost_estimate=cost(8),
        name="attend_backward",
    )(info, *after, query, key, value, *parts, *context, *lse, seg, x_t, vectors)


def normalise(values):
    centred = values - jnp.mean(values, axis=1, keepdims=True)
    root = lax.rsqrt(jnp.mean(centred * centred, axis=1, keepdims=True) + EPS)
    return centred * root, root


def norm_back(grad, gain, normal, root):
    e = grad * gain
    along = jnp.mean(e * normal, axis=1, keepdims=True)
    return root * (e - jnp.mean(e, axis=1, keepdims=True) - normal * along)


def store_columns(place, flipped, mine, send):
    size, count = flipped.shape[0] // 4, flipped.shape[1]
    for b in range(4):
        rel = place ^ b

        @pl.when(rel % 2 == 0)
        def _():
            mine[pl.ds(rel // 2, 1)] = flipped[b * size : (b + 1) * size][None]

        @pl.when(rel % 2 == 1)
        def _():
            rows = pl.ds(pl.multiple_of(rel // 2 * size, size), size)
            send[rows, :count] = flipped[b * size : (b + 1) * size]


def middle_forward_kernel(
    info, p0, p1, p2, p3, x_in, cot, wo, bo, g1, s1, up, bup, down, bdown, g2, s2,
    out, d_res, n1, r1, turned, act, slope, mine, send, vec,
    hid, hid_low, branch,
):
    place, core, chip = info[0], info[1], info[2]
    step = pl.program_id(0)
    quarter = p0.shape[0]

    @pl.when(step == 0)
    def _():
        first = core == 0

        def sides(a, b):
            a, b = a[...], b[...]
            return jnp.concatenate([jnp.where(first, a, b), jnp.where(first, b, a)], axis=1)

        ctx = jnp.concatenate([sides(p0, p1), sides(p2, p3)], axis=0)
        turned[1] = ctx.T
        x = jnp.concatenate([x_in[chip], x_in[1 - chip]], axis=0).astype(F32)
        summed = x + dot_nn(ctx, wo[...]) + bo[...].astype(F32)
        normal, root = normalise(summed)
        n1[...] = normal
        r1[...] = root
        hidden = normal * g1[...].astype(F32) + s1[...].astype(F32)
        hid[...] = hidden
        low = hidden.astype(LOW)
        hid_low[...] = low
        turned[0] = low.T
        branch[...] = jnp.zeros_like(branch)

    size = hid.shape[0] // CHUNKS
    chunks = [slice(n * size, (n + 1) * size) for n in range(CHUNKS)]
    pres = [dot_nn(hid_low[rows, :], up[...]) + bup[...].astype(F32) for rows in chunks]
    for rows, pre in zip(chunks, pres):
        phi = 0.5 + 0.5 * lax.erf(pre * ROOT_HALF)
        low = (pre * phi).astype(LOW)
        act[rows, :] = low
        slope[rows, :] = phi + pre * (jnp.exp(-0.5 * pre * pre) * ROOT_TWO_PI)
        branch[rows, :] += dot_nn(low, down[...])

    @pl.when(step == pl.num_programs(0) - 1)
    def _():
        normal, root = normalise(hid[...] + branch[...] + bdown[...].astype(F32))
        final = (normal * g2[...].astype(F32) + s2[...].astype(F32)).astype(LOW)
        out[pl.ds(chip, 1)] = final[:quarter][None]
        out[pl.ds(1 - chip, 1)] = final[quarter:][None]
        grad = jnp.concatenate([cot[chip], cot[1 - chip]], axis=0).astype(F32)
        back = norm_back(grad, g2[...].astype(F32), normal, root)
        d_res[...] = back
        vec[0:1, :] = column_sum(back)
        vec[1:2, :] = column_sum(grad * normal)
        vec[2:3, :] = column_sum(grad)
        store_columns(place, back.astype(LOW).T, mine, send)


def mark_kernel(*refs):
    refs[-1][...] = jnp.zeros_like(refs[-1])


def mark(*after):
    return pl.pallas_call(
        mark_kernel,
        grid=(1,),
        in_specs=waiting(after),
        out_specs=full((8, 128)),
        out_shape=shaped((8, 128), F32),
        compiler_params=params(VMEM),
        cost_estimate=cost(1),
        name="mark",
    )(*after)


def middle_forward(after, info, parts, inputs, cotangent, wo, bo, g1, s1, up, bup, down, bdown, g2, s2):
    quarter, half = parts[0].shape
    width, inner = 2 * half, up.shape[1]
    count, steps = 2 * quarter, 4
    chunk = inner // steps
    vector = full((1, width))
    tokens = full((count, width))
    turned = full((2, width // 4, count))
    return pl.pallas_call(
        ordered(middle_forward_kernel, after),
        grid_spec=pltpu.PrefetchScalarGridSpec(
            num_scalar_prefetch=1,
            grid=(steps,),
            in_specs=waiting(after)
            + [full((quarter, half))] * 4
            + [full((2, quarter, width))] * 2
            + [full((width, width)), vector, vector, vector]
            + [
                pl.BlockSpec((width, chunk), lambda c, i: (0, c)),
                pl.BlockSpec((1, chunk), lambda c, i: (0, c)),
                pl.BlockSpec((chunk, width), lambda c, i: (c, 0)),
            ]
            + [vector] * 3,
            out_specs=[full((2, quarter, width)), tokens, tokens, full((count, 1))]
            + [full((2, width, count))]
            + [pl.BlockSpec((count, chunk), lambda c, i: (0, c))] * 2
            + [turned, full((width // 2, count)), full((8, width))],
            scratch_shapes=[
                pltpu.VMEM((count, width), F32),
                pltpu.VMEM((count, width), LOW),
                pltpu.VMEM((count, width), F32),
            ],
        ),
        out_shape=[
            shaped((2, quarter, width), LOW),
            shaped((count, width), F32),
            shaped((count, width), F32),
            shaped((count, 1), F32),
            shaped((2, width, count), LOW),
            shaped((count, inner), LOW),
            shaped((count, inner), F32),
            shaped((2, width // 4, count), LOW),
            shaped((width // 2, count), LOW),
            shaped((8, width), F32),
        ],
        compiler_params=params(VMEM),
        cost_estimate=cost(18),
        name="middle_forward",
    )(
        info, *after, *parts, inputs, cotangent, wo, bo[None], g1[None], s1[None],
        up, bup[None], down, bdown[None], g2[None], s2[None],
    )


def middle_backward_kernel(
    info, d_res, slope, down, up, wo, n1, r1, g1, vec_two,
    to_core, mine_pre, d_summed, q0, to_chip, mine, vec,
    d_branch, d_hidden,
):
    place, core = info[0], info[1]
    step = pl.program_id(0)
    quarter = q0.shape[0]
    half = q0.shape[1]
    count = d_res.shape[0]

    @pl.when(step == 0)
    def _():
        d_branch[...] = d_res[...].astype(LOW)
        d_hidden[...] = d_res[...]

    d_pre = (dot_nt(d_branch[...], down[...]) * slope[...]).astype(LOW)
    block = place ^ (1 - step // 2 + 2 * (step % 2))
    vec[pl.ds(6 + block, 1), :] = column_sum(d_pre.astype(F32))
    d_hidden[...] += dot_nt(d_pre, up[...])

    @pl.when(step < 2)
    def _():
        at = pl.multiple_of((1 + step) * count, count)
        to_core[pl.ds(at, count), :] = d_pre

    @pl.when(step >= 2)
    def _():
        mine_pre[0] = d_pre

    @pl.when(step == pl.num_programs(0) - 1)
    def _():
        grad = d_hidden[...]
        normal = n1[...]
        back = norm_back(grad, g1[...].astype(F32), normal, r1[...])
        d_summed[...] = back
        vec[3:6, :] = vec_two[0:3, :]
        vec[10:16, :] = jnp.zeros_like(vec[10:16, :])
        vec[0:1, :] = column_sum(back)
        vec[1:2, :] = column_sum(grad * normal)
        vec[2:3, :] = column_sum(grad)
        low = back.astype(LOW)
        store_columns(place, low.T, mine, to_core)
        d_ctx = dot_nt(low, wo[...]).astype(LOW)
        first = core == 0
        left, right = d_ctx[:, :half], d_ctx[:, half:]
        same = jnp.where(first, left, right)
        other = jnp.where(first, right, left)
        q0[...] = same[:quarter]
        packed = quarter // 2
        to_core[half : half + packed, :] = jnp.concatenate(
            [other[:packed], other[packed:quarter]], axis=1
        )
        to_chip[0] = same[quarter:]
        to_chip[1] = other[quarter:]


def middle_backward(info, d_res, slope, down, up, wo, n1, r1, g1, vec_two):
    count, width = d_res.shape
    inner, quarter, half = up.shape[1], count // 2, width // 2
    steps = 4
    chunk = inner // steps

    def block(c, i):
        return i[0] ^ (1 - c // 2 + 2 * (c % 2))

    tokens = full((count, width))
    turned = full((2, width // 4, count))
    return pl.pallas_call(
        middle_backward_kernel,
        grid_spec=pltpu.PrefetchScalarGridSpec(
            num_scalar_prefetch=1,
            grid=(steps,),
            in_specs=[
                tokens,
                pl.BlockSpec((count, chunk), lambda c, i: (0, block(c, i))),
                pl.BlockSpec((chunk, width), lambda c, i: (block(c, i), 0)),
                pl.BlockSpec((width, chunk), lambda c, i: (0, block(c, i))),
                full((width, width)),
                tokens,
                full((count, 1)),
                full((1, width)),
                full(vec_two.shape),
            ],
            out_specs=[
                full((3 * count, width)),
                pl.BlockSpec((1, count, chunk), lambda c, i: (jnp.maximum(c - 2, 0), 0, 0)),
                tokens,
            ]
            + [full((quarter, half)), full((2, quarter, half)), turned, full((16, width))],
            scratch_shapes=[pltpu.VMEM((count, width), LOW), pltpu.VMEM((count, width), F32)],
        ),
        out_shape=[
            shaped((3 * count, width), LOW),
            shaped((2, count, chunk), LOW),
            shaped((count, width), F32),
        ]
        + [
            shaped((quarter, half), LOW),
            shaped((2, quarter, half), LOW),
            shaped((2, width // 4, count), LOW),
            shaped((16, width), F32),
        ],
        compiler_params=params(VMEM),
        cost_estimate=cost(16),
        name="middle_backward",
    )(info, d_res, slope, down, up, wo, n1, r1, g1[None], vec_two)


DOWN_ORDERS = ("zxwy", "xzwy")


def down_kernel(info, mine, theirs, act, act_pair, *outs):
    left = jnp.concatenate([mine[0], mine[1]], axis=0)
    both = dot_nn(left, act[...]) + dot_nn(theirs[...], act_pair[...])
    size, block = both.shape[0] // 4, both.shape[1] // 2
    for side in range(2):
        rel = 2 * pl.program_id(0) + (side ^ (info[3] % 2))
        grad = both[:, side * block : (side + 1) * block]
        for n, order in enumerate(DOWN_ORDERS):
            for flip in range(2):
                start = (2 * flip + n) * size
                put(grad[start : start + size], rel, flip, order, outs[2 * n], outs[2 * n + 1])


def down_grad(info, mine, theirs, act, act_pair, after):
    _, size, count = mine.shape
    block = act.shape[1] // 8
    part = (8, size // 2, block)
    spec = pl.BlockSpec((count, 2 * block), lambda r, i: (0, r ^ (i[3] // 2)))
    return pl.pallas_call(
        ordered(down_kernel, after),
        grid_spec=pltpu.PrefetchScalarGridSpec(
            num_scalar_prefetch=1,
            grid=(4,),
            in_specs=waiting(after) + [full(mine.shape), full(theirs.shape), spec, spec],
            out_specs=[full(part)] * 4,
        ),
        out_shape=[shaped(part, LOW), shaped(part, F32)] * 2,
        compiler_params=params(VMEM),
        cost_estimate=cost(8),
        name="down_grad",
    )(info, *after, mine, theirs, act, act_pair)


UP_ORDERS = ("xyzw", "yxwz")


def up_kernel(
    info, left, left_pair, mine, theirs, mine_d, theirs_d, send_a, keep_a, send_b, keep_b, rows
):
    me = info[3]
    step = pl.program_id(0)

    for flip in range(2):

        @pl.when(step == flip)
        def _():
            both = dot_nn(left[0], mine[0]) + dot_nn(left_pair[0], theirs[...])
            wide = both.shape[1] // 2
            put_rows(both[:, :wide], rows, me, flip, UP_ORDERS[0], send_a, keep_a)
            put_rows(both[:, wide:], rows, me, flip, UP_ORDERS[1], send_b, keep_b)

    @pl.when(step == 2)
    def _():
        right = jnp.concatenate([mine_d[0], mine_d[1]], axis=0)
        grad = dot_nt(left[1], right) + dot_nt(left_pair[1], theirs_d[...])
        deep, wide = grad.shape[0] // 8, grad.shape[1] // 2
        for b in range(8):
            rows[b] = grad[b * deep : (b + 1) * deep]
        for rel in range(4):
            near, far = rows[me ^ rel], rows[me ^ (rel + 4)]
            for flip in range(2):
                cut = slice(flip * wide, (flip + 1) * wide)
                value = jnp.concatenate([near[:, cut], far[:, cut]], axis=1)
                index = 8 + 2 * flip + rel // 2
                if rel % 2:
                    send_b[index] = value.astype(LOW)
                else:
                    keep_b[index] = value


def up_grad(info, left, left_pair, mine, from_core, mine_d, after):
    _, width, count = left.shape
    half = width // 2

    def at(s):
        return jnp.minimum(s, 1)

    shapes = [
        shaped((lead, width // 8, half), dtype) for lead in (8, 12) for dtype in (LOW, F32)
    ]
    return pl.pallas_call(
        ordered(up_kernel, after),
        grid_spec=pltpu.PrefetchScalarGridSpec(
            num_scalar_prefetch=1,
            grid=(3,),
            in_specs=waiting(after)
            + [full(left.shape)] * 2
            + [
                pl.BlockSpec((1, count, width), lambda s, i: (at(s), 0, 0)),
                pl.BlockSpec((count, width), lambda s, i: (1 + at(s), 0)),
                full(mine_d.shape),
                pl.BlockSpec((half, count), lambda s, i: (0, 0)),
            ],
            out_specs=[full(shape.shape) for shape in shapes],
            scratch_shapes=[pltpu.VMEM((8, width // 8, half), F32)],
        ),
        out_shape=shapes,
        compiler_params=params(VMEM),
        cost_estimate=cost(10),
        name="up_grad",
    )(info, *after, left, left_pair, mine, from_core, mine_d, from_core)


def input_kernel(info, *refs):
    grads, weights, (near, far, send) = refs[:9], refs[9:12], refs[12:]
    rel = pl.program_id(0)
    total = sum(
        dot_nt(jnp.concatenate([ref[...] for ref in grads[t::3]], axis=1), weights[t][...])
        for t in range(3)
    )

    @pl.when(rel < 2)
    def _():
        send[0] = total

    @pl.when(rel == 2)
    def _():
        near[...] = total

    @pl.when(rel == 3)
    def _():
        far[...] = total


def input_part(info, grads, qkv_weight, after):
    tokens = grads[0].shape[0]
    width = qkv_weight.shape[0]
    quarter, half = tokens // 4, width // 2

    rows = pl.BlockSpec((quarter, PAIR), lambda c, i: (i[0] ^ (1 - c // 2 + 2 * (c % 2)), 0))

    def weight(t):
        return pl.BlockSpec((width, half), lambda c, i: (0, 2 * t + i[1]))

    return pl.pallas_call(
        ordered(input_kernel, after),
        grid_spec=pltpu.PrefetchScalarGridSpec(
            num_scalar_prefetch=1,
            grid=(4,),
            in_specs=waiting(after) + [rows] * 9 + [weight(0), weight(1), weight(2)],
            out_specs=[
                full((quarter, width)),
                full((quarter, width)),
                pl.BlockSpec((1, quarter, width), lambda c, i: (jnp.minimum(c, 1), 0, 0)),
            ],
        ),
        out_shape=[shaped((quarter, width), F32)] * 2 + [shaped((2, quarter, width), F32)],
        compiler_params=params(VMEM),
        cost_estimate=cost(6),
        name="input_part",
    )(info, *after, *grads, qkv_weight, qkv_weight, qkv_weight)


UNITS = (((0, 1), (2, 3), (4,), (5,)), ((0,), (1,), (2, 3), (4, 5)))


def share_kernel(info, zero, first, kept, got, own, one, two, three):
    place, core = info[0], info[1]
    total = [zero[zero.shape[0] - 1], first[first.shape[0] - 1], kept[0] + got[0].astype(F32)]
    units = []
    for t in range(3):
        part = jnp.concatenate([pair[:, t * PAIR : (t + 1) * PAIR] for pair in total], axis=1)
        units += jnp.split(part, 2, axis=1)
    for side in range(2):
        for target in range(4):
            for flip, ref in enumerate((own, one, two, three)):

                @pl.when(jnp.logical_and(core == side, place ^ target == flip))
                def _():
                    for n in range(2):
                        unit = units[UNITS[side][target][n % len(UNITS[side][target])]]
                        ref[n] = unit.astype(ref.dtype)


def share(info, zero, one, kept, got, after):
    unit = (2, got.shape[1], got.shape[2] // 2)
    return pl.pallas_call(
        ordered(share_kernel, after),
        grid_spec=pltpu.PrefetchScalarGridSpec(
            num_scalar_prefetch=1,
            grid=(1,),
            in_specs=waiting(after)
            + [full(array.shape) for array in (zero, one, kept, got)],
            out_specs=[full(unit)] * 4,
        ),
        out_shape=[shaped(unit, F32)] + [shaped(unit, LOW)] * 3,
        compiler_params=params(VMEM),
        cost_estimate=cost(1),
        name="share",
    )(info, *after, zero, one, kept, got)


def gather_kernel(info, own, one, two, three, out):
    place = info[0]
    same = own[...] + two[...].astype(F32)
    other = one[...].astype(F32) + three[...].astype(F32)
    for target in range(4):

        @pl.when(place == target)
        def _():
            sides = (same, other) if target % 2 == 0 else (other, same)
            pieces = [
                (side_unit, sides[side][n])
                for side in range(2)
                for n, side_unit in enumerate(
                    unit % 2 + 4 * (unit // 2) + 2 * side for unit in UNITS[side][target]
                )
            ]
            pieces.sort(key=lambda piece: piece[0])
            out[...] = jnp.concatenate([piece[1] for piece in pieces], axis=1)


def gather(info, own, *others):
    shape = (own.shape[1], 3 * own.shape[2])
    return pl.pallas_call(
        gather_kernel,
        grid_spec=pltpu.PrefetchScalarGridSpec(
            num_scalar_prefetch=1,
            grid=(1,),
            in_specs=[full(own.shape)] * 4,
            out_specs=full(shape),
        ),
        out_shape=shaped(shape, F32),
        compiler_params=params(VMEM),
        cost_estimate=cost(1),
        name="gather",
    )(info, own, *others)


def turn_kernel(info, x0, x1, x2, x3, x_t):
    quarter = x0.shape[0]
    for j, ref in enumerate((x0, x1, x2, x3)):
        at = pl.multiple_of((info[0] ^ j) * quarter, quarter)
        x_t[:, pl.ds(at, quarter)] = ref[...].T


def turn(info, quarters):
    quarter, width = quarters[0].shape
    return pl.pallas_call(
        turn_kernel,
        grid_spec=pltpu.PrefetchScalarGridSpec(
            num_scalar_prefetch=1,
            grid=(1,),
            in_specs=[full((quarter, width))] * 4,
            out_specs=full((width, 4 * quarter)),
        ),
        out_shape=shaped((width, 4 * quarter), LOW),
        compiler_params=params(VMEM),
        cost_estimate=cost(1),
        name="turn",
    )(info, *quarters)


def body(
    inputs,
    segments,
    qkv_weight,
    query_bias,
    value_bias,
    out_weight,
    out_bias,
    norm1_gain,
    norm1_shift,
    up_weight,
    up_bias,
    down_weight,
    down_bias,
    norm2_gain,
    norm2_shift,
    cotangent,
):
    rows, quarter, width = inputs.shape
    half = width // 2
    seq_size = lax.axis_size("seq")
    batch_size = lax.axis_size("batch")
    fine = batch_size // 8
    place = lax.axis_index("seq")
    chip, core = place // 2, place % 2
    segment = lax.dynamic_index_in_dim(segments, chip, 0)
    info = jnp.stack([place, core, chip, lax.axis_index("batch") // fine]).astype(jnp.int32)
    info = jnp.concatenate([info] + windows(segment[0]))

    def over_seq(array, flip):
        return lax.ppermute(array, "seq", [(i, i ^ flip) for i in range(seq_size)])

    def over_batch(array, flip):
        return lax.ppermute(array, "batch", [(i, i ^ flip) for i in range(batch_size)])

    def swap(array, axis):
        if axis == "x":
            return over_seq(array, 2)
        return over_batch(array, fine << "yzw".index(axis))

    def pick(array, index, axis=0):
        return lax.dynamic_index_in_dim(array, index, axis, keepdims=False)

    def tie(*arrays):
        return lax.optimization_barrier(arrays)

    def launch(*messages):
        return [
            (order, segments, kept, swap(sent, order[0]))
            for order, segments, sent, kept in messages
        ]

    def land(after, flights, *routes, fresh=()):
        made, token = join(
            [flight[1:] for flight in flights], [route[1:] for route in routes], after, fresh
        )
        return [(route[0],) + new for route, new in zip(routes, made)], token

    def finish(grad):
        if fine > 1:
            groups = [[i * fine + j for j in range(fine)] for i in range(8)]
            grad = lax.psum_scatter(
                grad, "batch", scatter_dimension=0, axis_index_groups=groups, tiled=True
            )
        return grad

    own = pick(inputs, chip)
    far = over_seq(pick(inputs, 1 - chip), 2)
    near = over_seq(own, 1)
    across = over_seq(far, 1)
    quarters = (own, near, far, across)

    query, key, value, parts, context, lse = attend_forward(
        info, quarters, qkv_weight, query_bias, value_bias, segment
    )
    parts = [parts[0]] + [over_seq(parts[j], j) for j in (1, 2, 3)]
    x_t = turn(info, quarters)

    outputs, d_res, n1, r1, turned, act, slope, mine, send, vec_two = middle_forward(
        [x_t], info, parts, inputs, cotangent, out_weight, out_bias, norm1_gain, norm1_shift,
        up_weight, up_bias, down_weight, down_bias, norm2_gain, norm2_shift,
    )
    pair = over_seq(turned, 1), over_seq(act, 1), over_seq(send, 1)
    back = middle_backward(
        info, d_res, slope, down_weight, up_weight, out_weight, n1, r1, norm1_gain, vec_two
    )
    turned_pair, act_pair, theirs = pair
    to_core, mine_pre, d_summed, q0, to_chip, mine_d, vectors = back

    token = mark(turned_pair, act_pair, theirs, vectors)
    to_core, to_chip, token = tie(to_core, to_chip, token)
    from_core, from_chip = over_seq(to_core, 1), over_seq(to_chip, 2)
    made = down_grad(info, mine, theirs, act, act_pair, [token])
    downs = launch(
        (DOWN_ORDERS[0], [8], made[0], made[1]), (DOWN_ORDERS[1], [8], made[2], made[3])
    )
    across = over_seq(from_chip[1], 1)
    made = up_grad(info, turned, turned_pair, mine_pre, from_core, mine_d, [made[1]])
    ups = launch((UP_ORDERS[0], [8], made[0], made[1]), (UP_ORDERS[1], [8, 4], made[2], made[3]))
    d_parts = (q0, from_core, from_core, from_chip, across)

    def piece(n, vectors, after):
        made = attend_backward(
            info, n, query, key, value, d_parts, context, lse, segment, x_t, vectors, after
        )
        return list(made)

    def opening(n, made, token):
        sent, token = tie(made[4], token)
        return (QKV_ORDERS[n], [4], sent, made[5]), token

    zero = piece(0, vectors, [made[1]])
    downs, token = land(
        zero[3:4],
        downs,
        (DOWN_ORDERS[0][1:], (0, 0)),
        (DOWN_ORDERS[1][1:], (1, 0)),
    )
    opened, token = opening(0, zero, token)
    *downs, first = launch(*downs, opened)

    one = piece(1, zero[3], [token])
    (up_a, up_b, down), token = land(
        one[3:4],
        ups + downs + [first],
        (UP_ORDERS[0][1:], (0, 0), (4, 0)),
        (UP_ORDERS[1][1:], (1, 0), (1, 1)),
        ("wy", (2, 0), (3, 0)),
    )
    opened, token = opening(1, one, token)
    flights = launch(up_a, up_b, down, opened)

    two = piece(2, one[3], [token])
    (up_a, up_b, others), token = land(
        two[3:4],
        flights,
        ("zw", (0, 0), (1, 1)),
        ("wz", (1, 0), (0, 1)),
        ("y", (2, 0), (2, 1), (3, 0), (4, 0)),
        fresh=[two[4:6]],
    )
    grads = [*zero[:3], *one[:3], *two[:3]]
    vectors, token = tie(two[3], token)
    flights = launch(others, up_a, up_b)
    vectors_got = over_seq(vectors, 1)

    near, far, send = input_part(info, grads, qkv_weight, [token])
    (up_a, up_b, down), token = land(
        [near],
        flights,
        ("w", (1, 0), (0, 2), (1, 1)),
        ("z", (2, 0), (0, 3)),
        ("", (0, 0), (0, 1), (2, 1)),
    )
    down_total = down[3]
    up_a, up_b = launch(up_a, up_b)
    send, vectors_got, token = tie(send, vectors_got, token)
    d_row_got = over_seq(send, 1)
    far = (far + d_row_got[1]).astype(LOW)
    d_far = over_seq(far, 2)
    vectors = vectors + vectors_got
    vectors = vectors + over_seq(vectors, 2)
    vectors = vectors + swap(vectors, "y")
    (up, third), token = land(
        [token, vectors, far],
        [up_a, up_b],
        ("", (0, 0), (1, 0), (0, 2), (0, 1)),
        ("w", (1, 1)),
    )
    up_total = up[3]
    wide = half // 2
    vectors, token = tie(vectors, token)
    (third,) = launch(third)
    vectors_got = swap(vectors, "z")
    own, *others = share(info, down[3], up[3], third[2], third[3], [token, vectors_got, d_far])
    vectors_got, own = tie(vectors_got, own)
    vectors = vectors + vectors_got
    qkv_total = gather(info, own, *[over_seq(other, 1 + j) for j, other in enumerate(others)])
    qkv_total = finish(qkv_total)
    out_total = finish(up_total[2, :, :wide])
    down_total = finish(down_total[:2].reshape(wide, half).T)
    up_total = finish(jnp.concatenate([up_total[0], up_total[1]], axis=1))

    vectors = vectors + swap(vectors, "w")
    flip = 1
    while flip < fine:
        vectors = vectors + over_batch(vectors, flip)
        flip *= 2
    d_near = d_summed[:quarter] + (near + d_row_got[0])
    d_far = d_summed[quarter:] + d_far.astype(F32)
    d_inputs = jnp.stack([jnp.where(chip == 0, d_near, d_far), jnp.where(chip == 0, d_far, d_near)])
    return (
        outputs,
        d_inputs,
        qkv_total,
        vectors[10],
        vectors[11],
        out_total,
        vectors[0],
        vectors[1],
        vectors[2],
        up_total,
        vectors[6:10].reshape(-1),
        down_total,
        vectors[3],
        vectors[4],
        vectors[5],
    )


def solution(mesh):
    whole, split = P(), P("batch", "seq")
    tokens = P("batch", "seq", None)
    return jax.shard_map(
        body,
        mesh=mesh,
        in_specs=(tokens, P("batch", None)) + (whole,) * 13 + (tokens,),
        out_specs=(tokens, tokens, split, whole, whole, split)
        + (whole,) * 3
        + (split, whole, split)
        + (whole,) * 3,
        check_vma=False,
    )
```

```python
import functools

import jax
import jax.numpy as jnp
from jax import lax
from jax.experimental import pallas as pl
from jax.experimental.pallas import tpu as pltpu
from jax.sharding import PartitionSpec as P

DH = 64
EPS = 1e-05
NEG = -1000000000.0
F32 = jnp.float32
LOW = jnp.bfloat16
PAIR = 2 * DH
SCALE = DH**-0.5
BLOCK = 256
UNIT = 128
WINDOWED = (0, 2)
SIZES = (5, 8)
VMEM = 18
CHUNKS = 2
ROOT_HALF = 0.5**0.5
ROOT_TWO_PI = 0.3989422804014327


def shaped(shape, dtype):
    return jax.ShapeDtypeStruct(shape, dtype)


def dot_nn(left, right):
    return jnp.dot(left, right, preferred_element_type=F32)


def dot_nt(left, right):
    return lax.dot_general(left, right, (((1,), (1,)), ((), ())), preferred_element_type=F32)


def params(mib):
    return pltpu.CompilerParams(vmem_limit_bytes=mib << 20, dimension_semantics=("arbitrary",))


def waiting(after):
    return [pl.BlockSpec(memory_space=pl.ANY)] * len(after)


def ordered(kernel, after):
    return lambda info, *refs: kernel(info, *refs[len(after) :])


def full(shape):
    return pl.BlockSpec(shape, lambda *_: (0,) * len(shape))


def cost(micros):
    return pl.CostEstimate(flops=int(micros * 0.6e9), transcendentals=0, bytes_accessed=0)


def column_sum(values):
    return jnp.sum(values, axis=0, keepdims=True)


def spot(rel, flip_x, order):
    bits = {"y": rel % 2, "z": (rel // 2) % 2, "w": rel // 4, "x": flip_x}
    index = 0
    for axis in order[1:]:
        index = index * 2 + bits[axis]
    return bits[order[0]], index


def put(value, rel, flip_x, order, send, keep):
    sent, index = spot(rel, flip_x, order)

    @pl.when(sent == 1)
    def _():
        send[pl.ds(index, 1)] = value.astype(LOW)[None]

    @pl.when(sent == 0)
    def _():
        keep[pl.ds(index, 1)] = value[None]


def put_rows(grad, rows, me, flip_x, order, send, keep):
    deep = grad.shape[0] // 8
    for b in range(8):
        rows[b] = grad[b * deep : (b + 1) * deep]
    for rel in range(8):
        sent, index = spot(rel, flip_x, order)
        value = rows[me ^ rel]
        if sent:
            send[index] = value.astype(LOW)
        else:
            keep[index] = value


def leaves(segments, route):
    return any(m >= len(segments) or segments[m][n] > 1 for m, n in route)


def join_kernel(skip, segments, fresh, routes, *refs):
    refs = refs[skip:]
    count = 2 * len(segments)
    ins, new = refs[:count], refs[count : count + 2 * fresh]
    outs = list(refs[count + 2 * fresh : -1])
    refs[-1][...] = jnp.zeros_like(refs[-1])
    for route in routes:
        more = leaves(segments, route)
        send = outs.pop(0) if more else None
        keep = outs.pop(0)
        sent = filled = 0
        for m, n in route:
            if m >= len(segments):
                at = 2 * (m - len(segments))
                size = new[at].shape[0]
                send[sent : sent + size] = new[at][...]
                keep[filled : filled + size] = new[at + 1][...]
                sent += size
                filled += size
                continue
            start, size = sum(segments[m][:n]), segments[m][n]
            total = ins[2 * m][start : start + size]
            total = total + ins[2 * m + 1][start : start + size].astype(F32)
            if size > 1:
                size //= 2
                send[sent : sent + size] = total[size:].astype(LOW)
                sent += size
            elif more:
                wide = total.shape[2] // 2
                turned = jnp.concatenate([total[0, :, wide:], total[0, :, :wide]], axis=1)
                send[sent] = turned.astype(LOW)
                sent += 1
            keep[filled : filled + size] = total[:size]
            filled += size


def join(messages, routes, after, fresh):
    segments = [list(message[0]) for message in messages]
    tail = messages[0][1].shape[1:]
    shapes, results = [], []
    for route in routes:
        left = [
            fresh[m - len(segments)][0].shape[0]
            if m >= len(segments)
            else max(segments[m][n] // 2, 1)
            for m, n in route
        ]
        more = leaves(segments, route)
        results.append(left if more else [])
        if more:
            shapes.append(shaped((sum(left),) + tail, LOW))
        shapes.append(shaped((sum(left),) + tail, F32))
    operands = [array for message in messages for array in message[1:]]
    operands += [array for pair in fresh for array in pair]
    shapes.append(shaped((8, 128), F32))
    *arrays, token = pl.pallas_call(
        functools.partial(join_kernel, len(after), segments, len(fresh), routes),
        grid=(1,),
        in_specs=waiting(after) + [full(array.shape) for array in operands],
        out_specs=[full(shape.shape) for shape in shapes],
        out_shape=shapes,
        compiler_params=params(VMEM),
        cost_estimate=cost(1),
        name="join",
    )(*after, *operands)
    return [(left, arrays.pop(0) if left else None, arrays.pop(0)) for left in results], token


def each_window(info, block, run):
    start = pl.multiple_of(info[4 + block], UNIT)
    kind = info[4 + (info.shape[0] - 4) // 2 + block]
    for n, size in enumerate(SIZES):

        @pl.when(kind == n)
        def _():
            run(pl.ds(start, size * UNIT), size * UNIT)


def windows(segment):
    tokens = segment.shape[0]
    rows = segment.reshape(tokens // BLOCK, BLOCK)
    first = jnp.sum((segment[None] < rows[:, :1]).astype(jnp.int32), axis=1) // UNIT
    last = (jnp.sum((segment[None] <= rows[:, -1:]).astype(jnp.int32), axis=1) - 1) // UNIT
    need = last - first + 1
    kind = sum(((need > size).astype(jnp.int32) for size in SIZES[:-1]), jnp.zeros_like(need))
    size = sum(jnp.where(kind == n, size, 0).astype(jnp.int32) for n, size in enumerate(SIZES))
    return [jnp.minimum(first, tokens // UNIT - size) * UNIT, kind]


def both_heads(array):
    lane = lax.broadcasted_iota(jnp.int32, array.shape, 1)
    zero = jnp.zeros_like(array)
    return jnp.concatenate(
        [jnp.where(lane < DH, array, zero), jnp.where(lane < DH, zero, array)], axis=0
    )


def own_heads(turned):
    return jnp.concatenate([turned[:DH, :BLOCK], turned[DH:, BLOCK:]], axis=0)


def fill_segments(seg_row, seg_col):
    seg_col[...] = jnp.broadcast_to(seg_row[...].astype(F32), (UNIT, seg_row.shape[1])).T


def masked_scores(key, query, seg_col, seg_row):
    parts = [seg_col == seg_row[:, n : n + UNIT] for n in range(0, BLOCK, UNIT)]
    return jnp.where(jnp.concatenate(parts + parts, axis=1), dot_nt(key, query), NEG)


def forward_kernel(
    project, info, *refs,
):
    if project:
        x0, x1, x2, x3, wq, wk, wv, bq, bv, seg_row, *refs = refs
        q_all, k_all, v_all, *outs = refs[:8]
        o_out, lse_out = outs[3:]
        parts, first = outs[:3], 1
        xs, seg_col, qs, vt, ctx = refs[8:]
    else:
        q_all, k_all, v_all, seg_row, *refs = refs
        parts, first = refs[:1], 0
        o_out, lse_out, seg_col, qs, vt, ctx = refs[1:]
    place = info[0]
    tokens = q_all.shape[0]
    quarter = tokens // 4
    each = quarter // BLOCK

    @pl.when(pl.program_id(0) == 0)
    def _():
        if project:
            for j, ref in enumerate((x0, x1, x2, x3)):
                xs[pl.ds(pl.multiple_of((place ^ j) * quarter, quarter), quarter), :] = ref[...]
        fill_segments(seg_row, seg_col)

    if project:
        weights = jnp.concatenate([wq[...], wk[...], wv[...]], axis=1)
        projected = dot_nn(xs[...], weights)
        query = (projected[:, :PAIR] + bq[...].astype(F32)).astype(LOW)
        value = (projected[:, 2 * PAIR :] + bv[...].astype(F32)).astype(LOW)
        q_all[...] = query
        k_all[...] = projected[:, PAIR : 2 * PAIR].astype(LOW)
        v_all[...] = value
    else:
        query, value = q_all[...], v_all[...]
    qs[...] = query * jnp.asarray(SCALE, LOW)
    vt[...] = value.T

    def step(i, _):
        b = (place ^ (first + i // each)) * each + i % each
        rows = pl.ds(pl.multiple_of(b * BLOCK, BLOCK), BLOCK)
        here = pl.ds(pl.multiple_of(i * BLOCK, BLOCK), BLOCK)

        def run(window, size):
            row = seg_row[:, rows].astype(F32)
            scores = masked_scores(k_all[window, :], both_heads(qs[rows, :]), seg_col[window, :], row)
            top = jnp.max(scores, axis=0, keepdims=True)
            expo = jnp.exp(scores - top)
            total = jnp.sum(expo, axis=0, keepdims=True)
            mixed = dot_nn(vt[:, window], expo.astype(LOW)) * (1.0 / total)
            lse_out[0, pl.ds(i, 1), :] = top + jnp.log(total)
            mixed = own_heads(mixed)
            o_out[:, here] = mixed
            ctx[here, :] = mixed.T.astype(LOW)

        if project:
            each_window(info, b, run)
        else:
            run(pl.ds(0, tokens), tokens)
        return 0

    lax.fori_loop(0, len(parts) * each, step, 0)
    for n, ref in enumerate(parts):
        ref[...] = ctx[n * quarter : (n + 1) * quarter, :]


def attend_forward(info, quarters, qkv_weight, query_bias, value_bias, seg):
    quarter, width = quarters[0].shape
    tokens, half = 4 * quarter, width // 2
    pairs, each = half // PAIR, quarter // BLOCK

    def weight_spec(t):
        return pl.BlockSpec((width, PAIR), lambda p, i: (0, (2 * t + i[1]) * pairs + p))

    def bias_spec():
        return pl.BlockSpec((1, PAIR), lambda p, i: (0, i[1] * pairs + p))

    col = pl.BlockSpec((tokens, PAIR), lambda p, i: (0, p))
    part = pl.BlockSpec((quarter, PAIR), lambda p, i: (0, p))

    def results(count):
        return (
            [part] * count
            + [
                pl.BlockSpec((PAIR, count * quarter), lambda p, i: (p, 0)),
                pl.BlockSpec((1, count * each, 2 * BLOCK), lambda p, i: (p, 0, 0)),
            ],
            [shaped((quarter, half), LOW)] * count
            + [
                shaped((half, count * quarter), F32),
                shaped((pairs, count * each, 2 * BLOCK), F32),
            ],
        )

    def scratch(count):
        return [
            pltpu.VMEM((tokens, UNIT), F32),
            pltpu.VMEM((tokens, PAIR), LOW),
            pltpu.VMEM((PAIR, tokens), LOW),
            pltpu.VMEM((count * quarter, PAIR), LOW),
        ]

    specs, shapes = results(3)
    query, key, value, *parts, context, lse = pl.pallas_call(
        functools.partial(forward_kernel, True),
        grid_spec=pltpu.PrefetchScalarGridSpec(
            num_scalar_prefetch=1,
            grid=(pairs,),
            in_specs=[full((quarter, width))] * 4
            + [weight_spec(0), weight_spec(1), weight_spec(2), bias_spec(), bias_spec()]
            + [full((1, tokens))],
            out_specs=[col] * 3 + specs,
            scratch_shapes=[pltpu.VMEM((tokens, width), LOW)] + scratch(3),
        ),
        out_shape=[shaped((tokens, half), LOW)] * 3 + shapes,
        compiler_params=params(VMEM),
        cost_estimate=cost(16),
        name="attend_forward",
    )(info, *quarters, qkv_weight, qkv_weight, qkv_weight, query_bias[None], value_bias[None], seg)
    specs, shapes = results(1)
    own, own_context, own_lse = pl.pallas_call(
        functools.partial(forward_kernel, False),
        grid_spec=pltpu.PrefetchScalarGridSpec(
            num_scalar_prefetch=1,
            grid=(pairs,),
            in_specs=[col] * 3 + [full((1, tokens))],
            out_specs=specs,
            scratch_shapes=scratch(1),
        ),
        out_shape=shapes,
        compiler_params=params(VMEM),
        cost_estimate=cost(5),
        name="attend_own",
    )(info, query, key, value, seg)
    return query, key, value, [own] + parts, (own_context, context), (own_lse, lse)


QKV_ORDERS = ("zyw", "zyw", "yzw")


def backward_kernel(
    n, info, q_in, k_in, v_in, o0, o1, o1b, o2, o3, o_own, o_far, lse_own, lse_far, seg_row, x_t, vec,
    dq_out, dk_out, dv_out, vec_out, w_send, w_keep,
    seg_col, qs, do, kt, dk, dv, w_rows, o_all, lse,
):
    place, core, me = info[0], info[1], info[3]
    tokens = q_in.shape[0]
    quarter = tokens // 4
    fill_segments(seg_row, seg_col)
    each = quarter // BLOCK
    o_all[:, :quarter] = o_own[...]
    o_all[:, quarter:] = o_far[...]
    lse[:each] = lse_own[0]
    lse[each:] = lse_far[0]
    for j, ref in enumerate((o0, None, o2, o3)):
        if ref is None:
            at = pl.multiple_of((place ^ 1) * quarter, quarter)
            do[pl.ds(at, quarter // 2), :] = o1[...]
            do[pl.ds(at + quarter // 2, quarter // 2), :] = o1b[...]
            continue
        do[pl.ds(pl.multiple_of((place ^ j) * quarter, quarter), quarter), :] = ref[...]
    qs[...] = q_in[...] * jnp.asarray(SCALE, LOW)
    kt[...] = k_in[...].T
    dk[...] = jnp.zeros_like(dk)
    dv[...] = jnp.zeros_like(dv)

    def step(b, _):
        start = pl.multiple_of(b * BLOCK, BLOCK)
        rows = pl.ds(start, BLOCK)

        def run(window, size):
            row = seg_row[:, rows].astype(F32)
            o_block = do[rows, :]
            query, grad = both_heads(qs[rows, :]), both_heads(o_block)
            i = (place ^ (b // each)) * each + b % each
            here = pl.ds(pl.multiple_of(i * BLOCK, BLOCK), BLOCK)
            along = o_block.T.astype(F32) * o_all[:, here]
            delta = jnp.concatenate([column_sum(along[:DH]), column_sum(along[DH:])], axis=1)
            scores = masked_scores(k_in[window, :], query, seg_col[window, :], row)
            probs = jnp.exp(scores - lse[pl.ds(i, 1), :])
            d_scores = (probs * (dot_nt(v_in[window, :], grad) - delta)).astype(LOW)
            dv[window, :] += dot_nn(probs.astype(LOW), grad)
            dk[window, :] += dot_nn(d_scores, query)
            d_query = own_heads(dot_nn(kt[:, window], d_scores)) * SCALE
            dq_out[rows, :] = d_query.T.astype(LOW)

        if n in WINDOWED:
            each_window(info, b, run)
        else:
            run(pl.ds(0, tokens), tokens)
        return 0

    lax.fori_loop(0, tokens // BLOCK, step, 0)
    dk_out[...] = dk[...].astype(LOW)
    dv_out[...] = dv[...].astype(LOW)
    vec_out[...] = vec[...]
    half = vec.shape[1] // 2
    for side in range(2):

        @pl.when(core == side)
        def _():
            cut = slice(side * half + n * PAIR, side * half + (n + 1) * PAIR)
            vec_out[10:11, cut] = column_sum(dq_out[...].astype(F32))
            vec_out[11:12, cut] = column_sum(dv_out[...].astype(F32))

    grad = jnp.concatenate([dq_out[...], dk_out[...], dv_out[...]], axis=1)
    grad = dot_nn(x_t[...], grad)
    put_rows(grad, w_rows, me, 0, QKV_ORDERS[n], w_send, w_keep)


def attend_backward(info, n, query, key, value, parts, context, lse, seg, x_t, vectors, after):
    tokens, half = query.shape
    quarter, blocks, width = tokens // 4, tokens // BLOCK, x_t.shape[0]
    col = pl.BlockSpec((tokens, PAIR), lambda p, i: (0, n))
    pairs = half // PAIR
    part = pl.BlockSpec((quarter, PAIR), lambda p, i: (0, n))
    first = pl.BlockSpec((None, quarter, PAIR), lambda p, i: (0, 0, n))
    packed = quarter // 2
    low, high = [
        pl.BlockSpec((packed, PAIR), lambda p, i, at=at: (half // packed, at * pairs + n))
        for at in range(2)
    ]
    weight = (4, width // 8, 3 * PAIR)
    dtypes = (LOW, F32)
    return pl.pallas_call(
        ordered(functools.partial(backward_kernel, n), after),
        grid_spec=pltpu.PrefetchScalarGridSpec(
            num_scalar_prefetch=1,
            grid=(1,),
            in_specs=waiting(after)
            + [col] * 3
            + [part, low, high, first, part]
            + [pl.BlockSpec((PAIR, array.shape[1]), lambda p, i: (n, 0)) for array in context]
            + [pl.BlockSpec((1,) + array.shape[1:], lambda p, i: (n, 0, 0)) for array in lse]
            + [full((1, tokens)), full((width, tokens)), full(vectors.shape)],
            out_specs=[full((tokens, PAIR))] * 3
            + [full(vectors.shape)]
            + [full(weight)] * len(dtypes),
            scratch_shapes=[
                pltpu.VMEM((tokens, UNIT), F32),
                pltpu.VMEM((tokens, PAIR), LOW),
                pltpu.VMEM((tokens, PAIR), LOW),
                pltpu.VMEM((PAIR, tokens), LOW),
                pltpu.VMEM((tokens, PAIR), F32),
                pltpu.VMEM((tokens, PAIR), F32),
                pltpu.VMEM((8, width // 8, 3 * PAIR), F32),
                pltpu.VMEM((PAIR, tokens), F32),
                pltpu.VMEM((blocks, 2 * BLOCK), F32),
            ],
        ),
        out_shape=[shaped((tokens, PAIR), LOW)] * 3
        + [shaped(vectors.shape, F32)]
        + [shaped(weight, dtype) for dtype in dtypes],
        compiler_params=params(VMEM),
        cost_estimate=cost(8),
        name="attend_backward",
    )(info, *after, query, key, value, *parts, *context, *lse, seg, x_t, vectors)


def normalise(values):
    centred = values - jnp.mean(values, axis=1, keepdims=True)
    root = lax.rsqrt(jnp.mean(centred * centred, axis=1, keepdims=True) + EPS)
    return centred * root, root


def norm_back(grad, gain, normal, root):
    e = grad * gain
    along = jnp.mean(e * normal, axis=1, keepdims=True)
    return root * (e - jnp.mean(e, axis=1, keepdims=True) - normal * along)


def store_columns(place, flipped, mine, send):
    size, count = flipped.shape[0] // 4, flipped.shape[1]
    for b in range(4):
        rel = place ^ b

        @pl.when(rel % 2 == 0)
        def _():
            mine[pl.ds(rel // 2, 1)] = flipped[b * size : (b + 1) * size][None]

        @pl.when(rel % 2 == 1)
        def _():
            rows = pl.ds(pl.multiple_of(rel // 2 * size, size), size)
            send[rows, :count] = flipped[b * size : (b + 1) * size]


def middle_forward_kernel(
    info, p0, p1, p2, p3, x_in, cot, wo, bo, g1, s1, up, bup, down, bdown, g2, s2,
    out, d_res, n1, r1, turned, act, slope, mine, send, vec,
    hid, hid_low, branch,
):
    place, core, chip = info[0], info[1], info[2]
    step = pl.program_id(0)
    quarter = p0.shape[0]

    @pl.when(step == 0)
    def _():
        first = core == 0

        def sides(a, b):
            a, b = a[...], b[...]
            return jnp.concatenate([jnp.where(first, a, b), jnp.where(first, b, a)], axis=1)

        ctx = jnp.concatenate([sides(p0, p1), sides(p2, p3)], axis=0)
        turned[1] = ctx.T
        x = jnp.concatenate([x_in[chip], x_in[1 - chip]], axis=0).astype(F32)
        summed = x + dot_nn(ctx, wo[...]) + bo[...].astype(F32)
        normal, root = normalise(summed)
        n1[...] = normal
        r1[...] = root
        hidden = normal * g1[...].astype(F32) + s1[...].astype(F32)
        hid[...] = hidden
        low = hidden.astype(LOW)
        hid_low[...] = low
        turned[0] = low.T
        branch[...] = jnp.zeros_like(branch)

    size = hid.shape[0] // CHUNKS
    chunks = [slice(n * size, (n + 1) * size) for n in range(CHUNKS)]
    pres = [dot_nn(hid_low[rows, :], up[...]) + bup[...].astype(F32) for rows in chunks]
    for rows, pre in zip(chunks, pres):
        phi = 0.5 + 0.5 * lax.erf(pre * ROOT_HALF)
        low = (pre * phi).astype(LOW)
        act[rows, :] = low
        slope[rows, :] = phi + pre * (jnp.exp(-0.5 * pre * pre) * ROOT_TWO_PI)
        branch[rows, :] += dot_nn(low, down[...])

    @pl.when(step == pl.num_programs(0) - 1)
    def _():
        normal, root = normalise(hid[...] + branch[...] + bdown[...].astype(F32))
        final = (normal * g2[...].astype(F32) + s2[...].astype(F32)).astype(LOW)
        out[pl.ds(chip, 1)] = final[:quarter][None]
        out[pl.ds(1 - chip, 1)] = final[quarter:][None]
        grad = jnp.concatenate([cot[chip], cot[1 - chip]], axis=0).astype(F32)
        back = norm_back(grad, g2[...].astype(F32), normal, root)
        d_res[...] = back
        vec[0:1, :] = column_sum(back)
        vec[1:2, :] = column_sum(grad * normal)
        vec[2:3, :] = column_sum(grad)
        store_columns(place, back.astype(LOW).T, mine, send)


def mark_kernel(*refs):
    refs[-1][...] = jnp.zeros_like(refs[-1])


def mark(*after):
    return pl.pallas_call(
        mark_kernel,
        grid=(1,),
        in_specs=waiting(after),
        out_specs=full((8, 128)),
        out_shape=shaped((8, 128), F32),
        compiler_params=params(VMEM),
        cost_estimate=cost(1),
        name="mark",
    )(*after)


def middle_forward(after, info, parts, inputs, cotangent, wo, bo, g1, s1, up, bup, down, bdown, g2, s2):
    quarter, half = parts[0].shape
    width, inner = 2 * half, up.shape[1]
    count, steps = 2 * quarter, 4
    chunk = inner // steps
    vector = full((1, width))
    tokens = full((count, width))
    turned = full((2, width // 4, count))
    return pl.pallas_call(
        ordered(middle_forward_kernel, after),
        grid_spec=pltpu.PrefetchScalarGridSpec(
            num_scalar_prefetch=1,
            grid=(steps,),
            in_specs=waiting(after)
            + [full((quarter, half))] * 4
            + [full((2, quarter, width))] * 2
            + [full((width, width)), vector, vector, vector]
            + [
                pl.BlockSpec((width, chunk), lambda c, i: (0, c)),
                pl.BlockSpec((1, chunk), lambda c, i: (0, c)),
                pl.BlockSpec((chunk, width), lambda c, i: (c, 0)),
            ]
            + [vector] * 3,
            out_specs=[full((2, quarter, width)), tokens, tokens, full((count, 1))]
            + [full((2, width, count))]
            + [pl.BlockSpec((count, chunk), lambda c, i: (0, c))] * 2
            + [turned, full((width // 2, count)), full((8, width))],
            scratch_shapes=[
                pltpu.VMEM((count, width), F32),
                pltpu.VMEM((count, width), LOW),
                pltpu.VMEM((count, width), F32),
            ],
        ),
        out_shape=[
            shaped((2, quarter, width), LOW),
            shaped((count, width), F32),
            shaped((count, width), F32),
            shaped((count, 1), F32),
            shaped((2, width, count), LOW),
            shaped((count, inner), LOW),
            shaped((count, inner), F32),
            shaped((2, width // 4, count), LOW),
            shaped((width // 2, count), LOW),
            shaped((8, width), F32),
        ],
        compiler_params=params(VMEM),
        cost_estimate=cost(18),
        name="middle_forward",
    )(
        info, *after, *parts, inputs, cotangent, wo, bo[None], g1[None], s1[None],
        up, bup[None], down, bdown[None], g2[None], s2[None],
    )


def middle_backward_kernel(
    info, d_res, slope, down, up, wo, n1, r1, g1, vec_two,
    to_core, mine_pre, d_summed, q0, to_chip, mine, vec,
    d_branch, d_hidden,
):
    place, core = info[0], info[1]
    step = pl.program_id(0)
    quarter = q0.shape[0]
    half = q0.shape[1]
    count = d_res.shape[0]

    @pl.when(step == 0)
    def _():
        d_branch[...] = d_res[...].astype(LOW)
        d_hidden[...] = d_res[...]

    d_pre = (dot_nt(d_branch[...], down[...]) * slope[...]).astype(LOW)
    block = place ^ (1 - step // 2 + 2 * (step % 2))
    vec[pl.ds(6 + block, 1), :] = column_sum(d_pre.astype(F32))
    d_hidden[...] += dot_nt(d_pre, up[...])

    @pl.when(step < 2)
    def _():
        at = pl.multiple_of((1 + step) * count, count)
        to_core[pl.ds(at, count), :] = d_pre

    @pl.when(step >= 2)
    def _():
        mine_pre[0] = d_pre

    @pl.when(step == pl.num_programs(0) - 1)
    def _():
        grad = d_hidden[...]
        normal = n1[...]
        back = norm_back(grad, g1[...].astype(F32), normal, r1[...])
        d_summed[...] = back
        vec[3:6, :] = vec_two[0:3, :]
        vec[10:16, :] = jnp.zeros_like(vec[10:16, :])
        vec[0:1, :] = column_sum(back)
        vec[1:2, :] = column_sum(grad * normal)
        vec[2:3, :] = column_sum(grad)
        low = back.astype(LOW)
        store_columns(place, low.T, mine, to_core)
        d_ctx = dot_nt(low, wo[...]).astype(LOW)
        first = core == 0
        left, right = d_ctx[:, :half], d_ctx[:, half:]
        same = jnp.where(first, left, right)
        other = jnp.where(first, right, left)
        q0[...] = same[:quarter]
        packed = quarter // 2
        to_core[half : half + packed, :] = jnp.concatenate(
            [other[:packed], other[packed:quarter]], axis=1
        )
        to_chip[0] = same[quarter:]
        to_chip[1] = other[quarter:]


def middle_backward(info, d_res, slope, down, up, wo, n1, r1, g1, vec_two):
    count, width = d_res.shape
    inner, quarter, half = up.shape[1], count // 2, width // 2
    steps = 4
    chunk = inner // steps

    def block(c, i):
        return i[0] ^ (1 - c // 2 + 2 * (c % 2))

    tokens = full((count, width))
    turned = full((2, width // 4, count))
    return pl.pallas_call(
        middle_backward_kernel,
        grid_spec=pltpu.PrefetchScalarGridSpec(
            num_scalar_prefetch=1,
            grid=(steps,),
            in_specs=[
                tokens,
                pl.BlockSpec((count, chunk), lambda c, i: (0, block(c, i))),
                pl.BlockSpec((chunk, width), lambda c, i: (block(c, i), 0)),
                pl.BlockSpec((width, chunk), lambda c, i: (0, block(c, i))),
                full((width, width)),
                tokens,
                full((count, 1)),
                full((1, width)),
                full(vec_two.shape),
            ],
            out_specs=[
                full((3 * count, width)),
                pl.BlockSpec((1, count, chunk), lambda c, i: (jnp.maximum(c - 2, 0), 0, 0)),
                tokens,
            ]
            + [full((quarter, half)), full((2, quarter, half)), turned, full((16, width))],
            scratch_shapes=[pltpu.VMEM((count, width), LOW), pltpu.VMEM((count, width), F32)],
        ),
        out_shape=[
            shaped((3 * count, width), LOW),
            shaped((2, count, chunk), LOW),
            shaped((count, width), F32),
        ]
        + [
            shaped((quarter, half), LOW),
            shaped((2, quarter, half), LOW),
            shaped((2, width // 4, count), LOW),
            shaped((16, width), F32),
        ],
        compiler_params=params(VMEM),
        cost_estimate=cost(16),
        name="middle_backward",
    )(info, d_res, slope, down, up, wo, n1, r1, g1[None], vec_two)


DOWN_ORDERS = ("zxwy", "xzwy")


def down_kernel(info, mine, theirs, act, act_pair, *outs):
    left = jnp.concatenate([mine[0], mine[1]], axis=0)
    both = dot_nn(left, act[...]) + dot_nn(theirs[...], act_pair[...])
    size, block = both.shape[0] // 4, both.shape[1] // 2
    for side in range(2):
        rel = 2 * pl.program_id(0) + (side ^ (info[3] % 2))
        grad = both[:, side * block : (side + 1) * block]
        for n, order in enumerate(DOWN_ORDERS):
            for flip in range(2):
                start = (2 * flip + n) * size
                put(grad[start : start + size], rel, flip, order, outs[2 * n], outs[2 * n + 1])


def down_grad(info, mine, theirs, act, act_pair, after):
    _, size, count = mine.shape
    block = act.shape[1] // 8
    part = (8, size // 2, block)
    spec = pl.BlockSpec((count, 2 * block), lambda r, i: (0, r ^ (i[3] // 2)))
    return pl.pallas_call(
        ordered(down_kernel, after),
        grid_spec=pltpu.PrefetchScalarGridSpec(
            num_scalar_prefetch=1,
            grid=(4,),
            in_specs=waiting(after) + [full(mine.shape), full(theirs.shape), spec, spec],
            out_specs=[full(part)] * 4,
        ),
        out_shape=[shaped(part, LOW), shaped(part, F32)] * 2,
        compiler_params=params(VMEM),
        cost_estimate=cost(8),
        name="down_grad",
    )(info, *after, mine, theirs, act, act_pair)


UP_ORDERS = ("xyzw", "yxwz")


def up_kernel(
    info, left, left_pair, mine, theirs, mine_d, theirs_d, send_a, keep_a, send_b, keep_b, rows
):
    me = info[3]
    step = pl.program_id(0)

    for flip in range(2):

        @pl.when(step == flip)
        def _():
            both = dot_nn(left[0], mine[0]) + dot_nn(left_pair[0], theirs[...])
            wide = both.shape[1] // 2
            put_rows(both[:, :wide], rows, me, flip, UP_ORDERS[0], send_a, keep_a)
            put_rows(both[:, wide:], rows, me, flip, UP_ORDERS[1], send_b, keep_b)

    @pl.when(step == 2)
    def _():
        right = jnp.concatenate([mine_d[0], mine_d[1]], axis=0)
        grad = dot_nt(left[1], right) + dot_nt(left_pair[1], theirs_d[...])
        deep, wide = grad.shape[0] // 8, grad.shape[1] // 2
        for b in range(8):
            rows[b] = grad[b * deep : (b + 1) * deep]
        for rel in range(4):
            near, far = rows[me ^ rel], rows[me ^ (rel + 4)]
            for flip in range(2):
                cut = slice(flip * wide, (flip + 1) * wide)
                value = jnp.concatenate([near[:, cut], far[:, cut]], axis=1)
                index = 8 + 2 * flip + rel // 2
                if rel % 2:
                    send_b[index] = value.astype(LOW)
                else:
                    keep_b[index] = value


def up_grad(info, left, left_pair, mine, from_core, mine_d, after):
    _, width, count = left.shape
    half = width // 2

    def at(s):
        return jnp.minimum(s, 1)

    shapes = [
        shaped((lead, width // 8, half), dtype) for lead in (8, 12) for dtype in (LOW, F32)
    ]
    return pl.pallas_call(
        ordered(up_kernel, after),
        grid_spec=pltpu.PrefetchScalarGridSpec(
            num_scalar_prefetch=1,
            grid=(3,),
            in_specs=waiting(after)
            + [full(left.shape)] * 2
            + [
                pl.BlockSpec((1, count, width), lambda s, i: (at(s), 0, 0)),
                pl.BlockSpec((count, width), lambda s, i: (1 + at(s), 0)),
                full(mine_d.shape),
                pl.BlockSpec((half, count), lambda s, i: (0, 0)),
            ],
            out_specs=[full(shape.shape) for shape in shapes],
            scratch_shapes=[pltpu.VMEM((8, width // 8, half), F32)],
        ),
        out_shape=shapes,
        compiler_params=params(VMEM),
        cost_estimate=cost(10),
        name="up_grad",
    )(info, *after, left, left_pair, mine, from_core, mine_d, from_core)


def input_kernel(info, *refs):
    grads, weights, (near, far, send) = refs[:9], refs[9:12], refs[12:]
    rel = pl.program_id(0)
    total = sum(
        dot_nt(jnp.concatenate([ref[...] for ref in grads[t::3]], axis=1), weights[t][...])
        for t in range(3)
    )

    @pl.when(rel < 2)
    def _():
        send[0] = total

    @pl.when(rel == 2)
    def _():
        near[...] = total

    @pl.when(rel == 3)
    def _():
        far[...] = total


def input_part(info, grads, qkv_weight, after):
    tokens = grads[0].shape[0]
    width = qkv_weight.shape[0]
    quarter, half = tokens // 4, width // 2

    rows = pl.BlockSpec((quarter, PAIR), lambda c, i: (i[0] ^ (1 - c // 2 + 2 * (c % 2)), 0))

    def weight(t):
        return pl.BlockSpec((width, half), lambda c, i: (0, 2 * t + i[1]))

    return pl.pallas_call(
        ordered(input_kernel, after),
        grid_spec=pltpu.PrefetchScalarGridSpec(
            num_scalar_prefetch=1,
            grid=(4,),
            in_specs=waiting(after) + [rows] * 9 + [weight(0), weight(1), weight(2)],
            out_specs=[
                full((quarter, width)),
                full((quarter, width)),
                pl.BlockSpec((1, quarter, width), lambda c, i: (jnp.minimum(c, 1), 0, 0)),
            ],
        ),
        out_shape=[shaped((quarter, width), F32)] * 2 + [shaped((2, quarter, width), F32)],
        compiler_params=params(VMEM),
        cost_estimate=cost(6),
        name="input_part",
    )(info, *after, *grads, qkv_weight, qkv_weight, qkv_weight)


UNITS = (((0, 1), (2, 3), (4,), (5,)), ((0,), (1,), (2, 3), (4, 5)))


def share_kernel(info, zero, first, kept, got, own, one, two, three):
    place, core = info[0], info[1]
    total = [zero[zero.shape[0] - 1], first[first.shape[0] - 1], kept[0] + got[0].astype(F32)]
    units = []
    for t in range(3):
        part = jnp.concatenate([pair[:, t * PAIR : (t + 1) * PAIR] for pair in total], axis=1)
        units += jnp.split(part, 2, axis=1)
    for side in range(2):
        for target in range(4):
            for flip, ref in enumerate((own, one, two, three)):

                @pl.when(jnp.logical_and(core == side, place ^ target == flip))
                def _():
                    for n in range(2):
                        unit = units[UNITS[side][target][n % len(UNITS[side][target])]]
                        ref[n] = unit.astype(ref.dtype)


def share(info, zero, one, kept, got, after):
    unit = (2, got.shape[1], got.shape[2] // 2)
    return pl.pallas_call(
        ordered(share_kernel, after),
        grid_spec=pltpu.PrefetchScalarGridSpec(
            num_scalar_prefetch=1,
            grid=(1,),
            in_specs=waiting(after)
            + [full(array.shape) for array in (zero, one, kept, got)],
            out_specs=[full(unit)] * 4,
        ),
        out_shape=[shaped(unit, F32)] + [shaped(unit, LOW)] * 3,
        compiler_params=params(VMEM),
        cost_estimate=cost(1),
        name="share",
    )(info, *after, zero, one, kept, got)


def gather_kernel(info, own, one, two, three, out):
    place = info[0]
    same = own[...] + two[...].astype(F32)
    other = one[...].astype(F32) + three[...].astype(F32)
    for target in range(4):

        @pl.when(place == target)
        def _():
            sides = (same, other) if target % 2 == 0 else (other, same)
            pieces = [
                (side_unit, sides[side][n])
                for side in range(2)
                for n, side_unit in enumerate(
                    unit % 2 + 4 * (unit // 2) + 2 * side for unit in UNITS[side][target]
                )
            ]
            pieces.sort(key=lambda piece: piece[0])
            out[...] = jnp.concatenate([piece[1] for piece in pieces], axis=1)


def gather(info, own, *others):
    shape = (own.shape[1], 3 * own.shape[2])
    return pl.pallas_call(
        gather_kernel,
        grid_spec=pltpu.PrefetchScalarGridSpec(
            num_scalar_prefetch=1,
            grid=(1,),
            in_specs=[full(own.shape)] * 4,
            out_specs=full(shape),
        ),
        out_shape=shaped(shape, F32),
        compiler_params=params(VMEM),
        cost_estimate=cost(1),
        name="gather",
    )(info, own, *others)


def turn_kernel(info, x0, x1, x2, x3, x_t):
    quarter = x0.shape[0]
    for j, ref in enumerate((x0, x1, x2, x3)):
        at = pl.multiple_of((info[0] ^ j) * quarter, quarter)
        x_t[:, pl.ds(at, quarter)] = ref[...].T


def turn(info, quarters):
    quarter, width = quarters[0].shape
    return pl.pallas_call(
        turn_kernel,
        grid_spec=pltpu.PrefetchScalarGridSpec(
            num_scalar_prefetch=1,
            grid=(1,),
            in_specs=[full((quarter, width))] * 4,
            out_specs=full((width, 4 * quarter)),
        ),
        out_shape=shaped((width, 4 * quarter), LOW),
        compiler_params=params(VMEM),
        cost_estimate=cost(1),
        name="turn",
    )(info, *quarters)


def body(
    inputs,
    segments,
    qkv_weight,
    query_bias,
    value_bias,
    out_weight,
    out_bias,
    norm1_gain,
    norm1_shift,
    up_weight,
    up_bias,
    down_weight,
    down_bias,
    norm2_gain,
    norm2_shift,
    cotangent,
):
    rows, quarter, width = inputs.shape
    half = width // 2
    seq_size = lax.axis_size("seq")
    batch_size = lax.axis_size("batch")
    fine = batch_size // 8
    place = lax.axis_index("seq")
    chip, core = place // 2, place % 2
    segment = lax.dynamic_index_in_dim(segments, chip, 0)
    info = jnp.stack([place, core, chip, lax.axis_index("batch") // fine]).astype(jnp.int32)
    info = jnp.concatenate([info] + windows(segment[0]))

    def over_seq(array, flip):
        return lax.ppermute(array, "seq", [(i, i ^ flip) for i in range(seq_size)])

    def over_batch(array, flip):
        return lax.ppermute(array, "batch", [(i, i ^ flip) for i in range(batch_size)])

    def swap(array, axis):
        if axis == "x":
            return over_seq(array, 2)
        return over_batch(array, fine << "yzw".index(axis))

    def pick(array, index, axis=0):
        return lax.dynamic_index_in_dim(array, index, axis, keepdims=False)

    def tie(*arrays):
        return lax.optimization_barrier(arrays)

    def launch(*messages):
        return [
            (order, segments, kept, swap(sent, order[0]))
            for order, segments, sent, kept in messages
        ]

    def land(after, flights, *routes, fresh=()):
        made, token = join(
            [flight[1:] for flight in flights], [route[1:] for route in routes], after, fresh
        )
        return [(route[0],) + new for route, new in zip(routes, made)], token

    def finish(grad):
        if fine > 1:
            groups = [[i * fine + j for j in range(fine)] for i in range(8)]
            grad = lax.psum_scatter(
                grad, "batch", scatter_dimension=0, axis_index_groups=groups, tiled=True
            )
        return grad

    own = pick(inputs, chip)
    far = over_seq(pick(inputs, 1 - chip), 2)
    near = over_seq(own, 1)
    across = over_seq(far, 1)
    quarters = (own, near, far, across)

    query, key, value, parts, context, lse = attend_forward(
        info, quarters, qkv_weight, query_bias, value_bias, segment
    )
    parts = [parts[0]] + [over_seq(parts[j], j) for j in (1, 2, 3)]
    x_t = turn(info, quarters)

    outputs, d_res, n1, r1, turned, act, slope, mine, send, vec_two = middle_forward(
        [x_t], info, parts, inputs, cotangent, out_weight, out_bias, norm1_gain, norm1_shift,
        up_weight, up_bias, down_weight, down_bias, norm2_gain, norm2_shift,
    )
    pair = over_seq(turned, 1), over_seq(act, 1), over_seq(send, 1)
    back = middle_backward(
        info, d_res, slope, down_weight, up_weight, out_weight, n1, r1, norm1_gain, vec_two
    )
    turned_pair, act_pair, theirs = pair
    to_core, mine_pre, d_summed, q0, to_chip, mine_d, vectors = back

    token = mark(turned_pair, act_pair, theirs, vectors)
    to_core, to_chip, token = tie(to_core, to_chip, token)
    from_core, from_chip = over_seq(to_core, 1), over_seq(to_chip, 2)
    made = down_grad(info, mine, theirs, act, act_pair, [token])
    downs = launch(
        (DOWN_ORDERS[0], [8], made[0], made[1]), (DOWN_ORDERS[1], [8], made[2], made[3])
    )
    across = over_seq(from_chip[1], 1)
    made = up_grad(info, turned, turned_pair, mine_pre, from_core, mine_d, [made[1]])
    ups = launch((UP_ORDERS[0], [8], made[0], made[1]), (UP_ORDERS[1], [8, 4], made[2], made[3]))
    d_parts = (q0, from_core, from_core, from_chip, across)

    def piece(n, vectors, after):
        made = attend_backward(
            info, n, query, key, value, d_parts, context, lse, segment, x_t, vectors, after
        )
        return list(made)

    def opening(n, made, token):
        sent, token = tie(made[4], token)
        return (QKV_ORDERS[n], [4], sent, made[5]), token

    zero = piece(0, vectors, [made[1]])
    downs, token = land(
        zero[3:4],
        downs,
        (DOWN_ORDERS[0][1:], (0, 0)),
        (DOWN_ORDERS[1][1:], (1, 0)),
    )
    opened, token = opening(0, zero, token)
    *downs, first = launch(*downs, opened)

    one = piece(1, zero[3], [token])
    (up_a, up_b, down), token = land(
        one[3:4],
        ups + downs + [first],
        (UP_ORDERS[0][1:], (0, 0), (4, 0)),
        (UP_ORDERS[1][1:], (1, 0), (1, 1)),
        ("wy", (2, 0), (3, 0)),
    )
    opened, token = opening(1, one, token)
    flights = launch(up_a, up_b, down, opened)

    two = piece(2, one[3], [token])
    (up_a, up_b, others), token = land(
        two[3:4],
        flights,
        ("zw", (0, 0), (1, 1)),
        ("wz", (1, 0), (0, 1)),
        ("y", (2, 0), (2, 1), (3, 0), (4, 0)),
        fresh=[two[4:6]],
    )
    grads = [*zero[:3], *one[:3], *two[:3]]
    vectors, token = tie(two[3], token)
    flights = launch(others, up_a, up_b)
    vectors = vectors + over_seq(vectors, 1)

    near, far, send = input_part(info, grads, qkv_weight, [token])
    vectors, token = tie(vectors, mark(near))
    vectors = vectors + over_seq(vectors, 2)
    (up_a, up_b, down, first), token = land(
        [token, vectors],
        flights,
        ("w", (1, 0), (0, 2), (1, 1)),
        ("z", (2, 0), (0, 3)),
        ("", (0, 0), (0, 1)),
        ("", (2, 1)),
    )
    down_total = down[3]
    up_a, up_b = launch(up_a, up_b)
    send, vectors, token = tie(send, vectors, token)
    d_row_got = over_seq(send, 1)
    far = (far + d_row_got[1]).astype(LOW)
    d_far = over_seq(far, 2)
    vectors = vectors + swap(vectors, "y")
    (up, out_total, second, third), token = land(
        [token, vectors, far],
        [up_a, up_b],
        ("", (0, 0), (1, 0)),
        ("", (0, 2)),
        ("", (0, 1)),
        ("w", (1, 1)),
    )
    up_total = up[3]
    wide = half // 2
    vectors, token = tie(vectors, token)
    (third,) = launch(third)
    vectors_got = swap(vectors, "z")
    own, *others = share(info, first[3], second[3], third[2], third[3], [token, vectors_got, d_far])
    vectors_got, own = tie(vectors_got, own)
    vectors = vectors + vectors_got
    qkv_total = gather(info, own, *[over_seq(other, 1 + j) for j, other in enumerate(others)])
    qkv_total = finish(qkv_total)
    out_total = finish(out_total[3][0, :, :wide])
    down_total = finish(down_total.reshape(wide, half).T)
    up_total = finish(jnp.concatenate([up_total[0], up_total[1]], axis=1))

    vectors = vectors + swap(vectors, "w")
    flip = 1
    while flip < fine:
        vectors = vectors + over_batch(vectors, flip)
        flip *= 2
    d_near = d_summed[:quarter] + (near + d_row_got[0])
    d_far = d_summed[quarter:] + d_far.astype(F32)
    d_inputs = jnp.stack([jnp.where(chip == 0, d_near, d_far), jnp.where(chip == 0, d_far, d_near)])
    return (
        outputs,
        d_inputs,
        qkv_total,
        vectors[10],
        vectors[11],
        out_total,
        vectors[0],
        vectors[1],
        vectors[2],
        up_total,
        vectors[6:10].reshape(-1),
        down_total,
        vectors[3],
        vectors[4],
        vectors[5],
    )


def solution(mesh):
    whole, split = P(), P("batch", "seq")
    tokens = P("batch", "seq", None)
    return jax.shard_map(
        body,
        mesh=mesh,
        in_specs=(tokens, P("batch", None)) + (whole,) * 13 + (tokens,),
        out_specs=(tokens, tokens, split, whole, whole, split)
        + (whole,) * 3
        + (split, whole, split)
        + (whole,) * 3,
        check_vma=False,
    )
```
